32 devices in a mesh: pairs: 4 (over y, core), stripe: 8 (over z, x).
Axes of the slice: x: 2, y: 2, z: 4, core: 2. Of those that a mesh axis runs over, the one named last changes fastest.
Arguments:
- slc_stack: bfloat16 [256, 2, 128, 1024], P(('pairs', 'stripe')), may hold values from -16 to 16
- az_offset: int32 [256], replicated, may hold values from -8 to 8
- rg_offset: int32 [256], replicated, may hold values from -16 to 16
- pair_list: int32 [1000, 2], replicated, may hold values from 0 to 255, as said below
Outputs:
- screen: float32 [256, 2, 32, 64], P(None, None, 'pairs', 'stripe')
- motion: float32 [256, 2, 32, 64], P(None, None, 'pairs', 'stripe')
The draws below stay inside these ranges and needn't reach their ends.
Inputs may be any that keep to these rules, and one draw needn't show every extreme that they name: `pair_list`: rows g * 250 to (g + 1) * 250 - 1 form pair group g: their reference dates lie in g * 64 to (g + 1) * 64 - 1, each secondary date is 1 to 5 dates after its reference, and no pair repeats.
All inputs are finite; a program needn't handle non-finite values.
Results may differ from the reference program's by a relative error of at most 0.0029.
Values may be sent and summed in bfloat16 or wider, within the bound.
No kernel may reach another device: no remote copies, remote signals or barrier semaphores. Data moves between devices by JAX's collectives and lax.ppermute only.
A program may use at most 64 MiB of HBM per device.

```python
import jax
import jax.numpy as jnp
from jax import lax

DATES = 256
DATE_BLK = 64
PAIR_GRP = 250
PAIRS = 1000
MAXB = 5
LA = 4
LR = 16
MAXA = 8
MAXR = 16
FILTER_R = 3
AZ = 128
RANGE = 1024
MLR = 32
MLC = 64


def draw_pair_list(key, part):
    group_total = PAIRS // PAIR_GRP
    combos = DATE_BLK * MAXB
    combo_ids = jnp.arange(combos, dtype=jnp.int32)
    ref_offsets = combo_ids // MAXB
    date_gaps = combo_ids % MAXB + 1

    def draw_group(group_key, group_index):
        ref_dates = group_index * DATE_BLK + ref_offsets
        sec_dates = ref_dates + date_gaps
        scores = jax.random.permutation(group_key, combos).astype(jnp.int32)
        forced = (ref_offsets == DATE_BLK - 1) & (date_gaps == MAXB)
        scores = jnp.where(forced, -1, scores)
        scores = jnp.where(sec_dates <= DATES - 1, scores, combos + combo_ids)
        chosen = jnp.argsort(scores, stable=True)[:PAIR_GRP]
        return jnp.stack([ref_dates[chosen], sec_dates[chosen]], axis=1)
    group_keys = jax.random.split(jax.random.fold_in(key, 17), group_total)
    drawn = jax.vmap(draw_group)(group_keys, jnp.arange(group_total, dtype=jnp.int32))
    return drawn.reshape(PAIRS, 2).astype(jnp.int32)


def with_ends(result, rng, least, high):
    longest = result.shape.index(max(result.shape))
    spots = []
    for shift in (0, 1):
        where = [jax.random.randint(jax.random.fold_in(rng, axis), (), 0, length) for axis, length in enumerate(result.shape)]
        where[longest] = (where[longest] + shift) % result.shape[longest]
        spots.append(tuple(where))
    return result.at[spots[0]].set(least).at[spots[1]].set(high)


def steps_of(key, shape, shards, smallest, high):
    def one(dim, parts):
        heights = jax.random.uniform(jax.random.fold_in(jax.random.fold_in(key, 6), dim), (parts,), jnp.float32, smallest / len(shards), high / len(shards))
        return jnp.repeat(jnp.exp(heights), shape[dim] // parts).reshape((-1,) + (1,) * (len(shape) - dim - 1))

    level = one(*shards[0])
    for cut in shards[1:]:
        level = level * one(*cut)
    return level


def bell_draw(own_key, shape, spread, most, pieces=(), kind=jnp.bfloat16):
    array = spread * jax.random.normal(own_key, shape, jnp.float32)
    if pieces:
        array = array * steps_of(own_key, shape, pieces, -0.22, 0.18)
    return jnp.clip(array, -most, most).astype(kind)


def setup_inputs(seed: int = 0) -> dict:
    key_of = jax.random.split(jax.random.key(seed), 5)
    slc_stack = bell_draw(key_of[0], (DATES, 2, AZ, RANGE), 3.0, 16.0, ((0, 32),))
    az_offset = with_ends(jax.random.randint(key_of[1], (DATES,), 0 - MAXA, MAXA + 1), jax.random.fold_in(key_of[1], 1), 0 - MAXA, MAXA).astype(jnp.int32)
    rg_offset = with_ends(jax.random.randint(key_of[2], (DATES,), 0 - MAXR, MAXR + 1), jax.random.fold_in(key_of[2], 1), 0 - MAXR, MAXR).astype(jnp.int32)
    pair_list = draw_pair_list(jax.random.fold_in(key_of[4], 71), 0)
    return {"slc_stack": slc_stack, "az_offset": az_offset, "rg_offset": rg_offset, "pair_list": pair_list}


damping = 0.5

def resample(picture, az_shift, rg_shift):
    padded = jnp.pad(picture, ((0, 0), (MAXA, MAXA), (MAXR, MAXR)))
    starts = (jnp.int32(0), (az_shift + MAXA).astype(jnp.int32), (rg_shift + MAXR).astype(jnp.int32))
    return lax.dynamic_slice(padded, starts, (2, AZ, RANGE))

def form_pair(slc_stack, az_offset, rg_offset, pair_row):
    ref_date = pair_row[0]
    sec_date = pair_row[1]
    ref_image = resample(slc_stack[ref_date], az_offset[ref_date], rg_offset[ref_date]).astype(jnp.float32)
    sec_image = resample(slc_stack[sec_date], az_offset[sec_date], rg_offset[sec_date]).astype(jnp.float32)
    real_part = ref_image[0] * sec_image[0] + ref_image[1] * sec_image[1]
    imag_part = ref_image[1] * sec_image[0] - ref_image[0] * sec_image[1]
    product = jnp.stack([real_part, imag_part])
    summed = product.reshape(2, AZ // LA, LA, RANGE // LR, LR).sum(axis=(2, 4))
    return (summed / (LA * LR)).astype(jnp.bfloat16)

def filter_weights(extent):
    positions = jnp.arange(extent, dtype=jnp.int32)
    offsets = (positions[None, :] - positions[:, None]).astype(jnp.float32)
    sigma = FILTER_R / 2.0
    tap_weights = jnp.where(jnp.abs(offsets) <= FILTER_R, jnp.exp(-(offsets * offsets) / (2.0 * sigma * sigma)), 0.0)
    return tap_weights / jnp.sum(tap_weights, axis=1, keepdims=True)

def reference(slc_stack, az_offset, rg_offset, pair_list):
    multilooked = lax.map(lambda pair_row: form_pair(slc_stack, az_offset, rg_offset, pair_row), pair_list)
    date_ids = jnp.arange(DATES, dtype=jnp.int32)
    design = (pair_list[:, 0:1] == date_ids[None, :]).astype(jnp.float32) - (pair_list[:, 1:2] == date_ids[None, :]).astype(jnp.float32)
    highest = lax.Precision.HIGHEST
    normal = jnp.dot(design.T, design, precision=highest) + damping * jnp.eye(DATES, dtype=jnp.float32)
    right = jnp.dot(design.T, multilooked.reshape(PAIRS, -1).astype(jnp.float32), precision=highest)
    series = jnp.linalg.solve(normal, right).reshape(DATES, 2, MLR, MLC)
    row_filter = filter_weights(MLR)
    col_filter = filter_weights(MLC)
    screen = jnp.einsum('uw,dcwv->dcuv', row_filter, series, precision=highest)
    screen = jnp.einsum('dcuw,vw->dcuv', screen, col_filter, precision=highest)
    return (screen, series - screen)
```

```python
from functools import partial

import jax
import jax.numpy as jnp
from jax import lax
from jax.experimental import pallas as pl
from jax.experimental.pallas import tpu as pltpu
from jax.sharding import Mesh, PartitionSpec as P

MAXB = 5
LA = 4
LR = 16
MAXA = 8
FILTER_R = 3
LANES = 128
damping = 0.5


def vmem():
    return pl.BlockSpec(memory_space=pltpu.VMEM)


def tap(k):
    sigma = FILTER_R / 2.0
    return jnp.exp(-jnp.float32(k * k) / jnp.float32(2.0 * sigma * sigma))


def resample_kernel(first, per_stripe, chunks, info, az, rg, img, *rest):
    keep, sends, shifted = rest[0], rest[1 : 1 + chunks], rest[1 + chunks]
    lines, full = img.shape[2], img.shape[3]
    tiles = full // LANES
    half = tiles // 2
    high = lines + 2 * MAXA
    groups = lines // 8
    date = info[1] + first + pl.program_id(0)
    x = info[0]
    shift = rg[date]
    step = az[date]
    behind = shift < 0
    origin = jnp.where(behind, -1, 0)
    amount = shift - origin * LANES
    turn = lax.rem(LANES - amount, LANES)
    lane = lax.broadcasted_iota(jnp.int32, (lines, LANES), 1)
    own = lane + amount < LANES

    @pl.when(pl.program_id(0) == 0)
    def _():
        blank = jnp.zeros((MAXA, LANES), jnp.float32)
        for t in range(tiles):
            shifted[pl.ds(t * high, MAXA), :] = blank
            shifted[pl.ds(t * high + MAXA + lines, MAXA), :] = blank

    for c in range(2):

        def turned(t):
            place = jnp.clip(t + origin, 0, tiles - 1)
            tile = img[0, c, :, pl.ds(pl.multiple_of(place * LANES, LANES), LANES)]
            out = pltpu.roll(tile.astype(jnp.float32), turn, 1)
            if t == 0:
                out = jnp.where(behind, 0.0, out)
            if t == tiles:
                out = jnp.where(behind, out, 0.0)
            return out

        here = turned(0)
        for t in range(tiles):
            after = turned(t + 1)
            shifted[pl.ds(t * high + MAXA, lines), :] = jnp.where(own, here, after)
            here = after

        def put(out, place, source):
            base = source * high + MAXA + step
            for pair in range(groups // 2):
                both = [
                    shifted[pl.ds(base + 2 * pair + k, 8, stride=groups), :] for k in range(2)
                ]
                out[0, c, place, pl.ds(16 * pair, 16), :] = jnp.concatenate(both, 0).astype(
                    jnp.bfloat16
                )

        per_chunk = half // chunks
        for h in range(half):
            stripe, inner = h // per_stripe, h % per_stripe
            put(keep, h, (2 * stripe + x) * per_stripe + inner)
            put(sends[h // per_chunk], h % per_chunk, (2 * stripe + 1 - x) * per_stripe + inner)


def resample(images, az, rg, info, first, count, per_stripe, chunks):
    lines, full = images.shape[2], images.shape[3]
    tiles = full // LANES
    half = tiles // 2

    def block(width):
        return pl.BlockSpec((1, 2, width, lines, LANES), lambda i, *_: (i, 0, 0, 0, 0))

    def shape(width):
        return jax.ShapeDtypeStruct((count, 2, width, lines, LANES), jnp.bfloat16)

    return pl.pallas_call(
        partial(resample_kernel, first, per_stripe, chunks),
        grid_spec=pltpu.PrefetchScalarGridSpec(
            num_scalar_prefetch=3,
            grid=(count,),
            in_specs=[pl.BlockSpec((1, 2, lines, full), lambda i, *_: (i + first, 0, 0, 0))],
            out_specs=[block(half)] + [block(half // chunks)] * chunks,
            scratch_shapes=[pltpu.VMEM((tiles * (lines + 2 * MAXA), LANES), jnp.float32)],
        ),
        out_shape=[shape(half)] + [shape(half // chunks)] * chunks,
        name=f"resample{first}",
        cost_estimate=pl.CostEstimate(
            flops=count * lines * full * 4,
            transcendentals=0,
            bytes_accessed=count * lines * full * 8,
        ),
    )(info, az, rg, images)


def merge(x, y, bit, distance):
    return jnp.where(
        bit, x + pltpu.roll(x, LANES - distance, 1), y + pltpu.roll(y, distance, 1)
    )


def pair_kernel(own, split, info, mask, *rest):
    parts, right, images, sums = rest[:-3], rest[-3], rest[-2], rest[-1]
    block = 2 * own
    x = info[0]
    mine, other = x * own, (1 - x) * own
    starts = [0, split][: (len(parts) - 1) // 2]
    for s, start in enumerate(starts):
        for where, ref in ((mine, parts[2 * s]), (other, parts[2 * s + 1])):
            for i in range(ref.shape[0]):
                images[where + start + i] = ref[i, :, 0].astype(jnp.float32)
    for i in range(MAXB):
        images[block + i] = parts[-1][i, :, 0].astype(jnp.float32)
    sums[...] = jnp.zeros_like(sums)
    lane = lax.broadcasted_iota(jnp.int32, (8, LANES), 1)
    bits = [lane & (1 << k) == 0 for k in range(4)]

    def slot(d, g, used):
        looked = []
        for comp in range(2):
            row = []
            for low in range(4):
                total = None
                for k in range(LA):
                    at = pl.ds(8 * (LA * low + k), 8)
                    a, b = images[d, 0, at, :], images[d, 1, at, :]
                    c, e = images[d + g, 0, at, :], images[d + g, 1, at, :]
                    term = a * c + b * e if comp == 0 else b * c - a * e
                    total = term if total is None else total + term
                row.append(total)
            looked.append(row)
        joined = []
        for row in looked:
            first = merge(row[0], row[1], bits[0], 1)
            second = merge(row[2], row[3], bits[0], 1)
            joined.append(merge(first, second, bits[1], 2))
        both = merge(joined[0], joined[1], bits[3], 8)
        result = merge(both, pltpu.roll(both, 7, 0), bits[2], 4)
        result = (result * (1.0 / (LA * LR))).astype(jnp.bfloat16).astype(jnp.float32)
        return result * used

    def date(d, carry):
        for g in range(1, MAXB + 1):
            used = mask[(info[2] + d) * MAXB + g - 1].astype(jnp.float32)
            value = slot(d, g, used)
            here, there = pl.ds(8 * d, 8), pl.ds(8 * (d + g), 8)
            sums[here, :] = sums[here, :] + value
            sums[there, :] = sums[there, :] - value
        return carry

    lax.fori_loop(0, block, date, 0)
    for row in range(right.shape[1]):
        for group in range(right.shape[2] // 8):
            right[0, row, pl.ds(8 * group, 8), :] = sums[
                pl.ds(64 * group + 2 * row, 8, stride=8), :
            ]


def pair_sums(info, mask, keeps, received, following, chunk, width, own, rows, deep):
    lines = following.shape[3]
    parts, specs = [], []
    for keep, got in zip(keeps, received):
        parts += [keep, got]
        count = keep.shape[0]
        specs += [
            pl.BlockSpec((count, 2, 1, lines, LANES), lambda i, *_: (0, 0, chunk * width + i, 0, 0)),
            pl.BlockSpec((count, 2, 1, lines, LANES), lambda i, *_: (0, 0, i, 0, 0)),
        ]
    specs.append(pl.BlockSpec((MAXB, 2, 1, lines, LANES), lambda i, *_: (0, 0, i, 0, 0)))
    work = 2 * own * MAXB * lines * LANES * width
    return pl.pallas_call(
        partial(pair_kernel, own, keeps[0].shape[0]),
        grid_spec=pltpu.PrefetchScalarGridSpec(
            num_scalar_prefetch=2,
            grid=(width,),
            in_specs=specs,
            out_specs=pl.BlockSpec((1, rows, deep, LANES), lambda i, *_: (i, 0, 0, 0)),
            scratch_shapes=[
                pltpu.VMEM((2 * own + MAXB, 2, lines, LANES), jnp.float32),
                pltpu.VMEM((8 * deep, LANES), jnp.float32),
            ],
        ),
        out_shape=jax.ShapeDtypeStruct((width, rows, deep, LANES), jnp.float32),
        name=f"pairs{chunk}",
        cost_estimate=pl.CostEstimate(flops=work * 8, transcendentals=0, bytes_accessed=work),
    )(info, mask, *parts, following)


def filter_kernel(per_stripe, chunks, info, *rest):
    own, partner = rest[:chunks], rest[chunks : 2 * chunks]
    weight, out, whole, along = rest[2 * chunks :]
    width, rows, deep = own[0].shape[:3]
    total = 2 * width * chunks
    x = info[0]
    blank = jnp.zeros((rows, deep, LANES), jnp.float32)
    along[0] = blank
    along[total + 1] = blank
    for c in range(chunks):
        for i in range(width):
            stripe, inner = divmod(c * width + i, per_stripe)
            whole[(2 * stripe + x) * per_stripe + inner] = own[c][i]
            whole[(2 * stripe + 1 - x) * per_stripe + inner] = partner[c][i]
    lane = lax.broadcasted_iota(jnp.int32, (deep, LANES), 1)
    place = lane & 7
    taps = [tap(k) for k in range(FILTER_R + 1)]

    def turn(v, k):
        return pltpu.roll(v, k % LANES, 1)

    def filter_rows(i, carry):
        for r in range(rows):
            v = whole[i, r]
            acc = v
            for k in range(1, FILTER_R + 1):
                up = turn(whole[i, r + 1], 8 - k) if r + 1 < rows else jnp.zeros_like(v)
                down = turn(whole[i, r - 1], k - 8) if r > 0 else jnp.zeros_like(v)
                near = jnp.where(place < 8 - k, turn(v, -k), up) + jnp.where(
                    place >= k, turn(v, k), down
                )
                acc = acc + taps[k] * near
            along[i + 1, r] = acc
        return carry

    lax.fori_loop(0, total, filter_rows, 0)

    for c in range(chunks):
        for i in range(width):
            h = c * width + i
            stripe, inner = divmod(h, per_stripe)
            at = (2 * stripe + x) * per_stripe + inner + 1
            for r in range(rows):
                v, left, right = along[at, r], along[at - 1, r], along[at + 1, r]
                acc = v
                for k in range(1, FILTER_R + 1):
                    reach = 16 * k
                    near = jnp.where(
                        lane < LANES - reach, turn(v, -reach), turn(right, -reach)
                    ) + jnp.where(lane >= reach, turn(v, reach), turn(left, reach))
                    acc = acc + taps[k] * near
                out[r, stripe, inner, 0] = own[c][i, r]
                out[r, stripe, inner, 1] = acc * weight[h, r : r + 1, :]


def filtered(info, own, partner, weight, per_stripe):
    chunks = len(own)
    width, rows, deep = own[0].shape[:3]
    tiles = width * chunks
    stripes = tiles // per_stripe
    smem = pl.BlockSpec(memory_space=pltpu.SMEM)
    return pl.pallas_call(
        partial(filter_kernel, per_stripe, chunks),
        in_specs=[smem] + [vmem()] * (2 * chunks + 1),
        out_specs=vmem(),
        out_shape=jax.ShapeDtypeStruct((rows, stripes, per_stripe, 2, deep, LANES), jnp.float32),
        scratch_shapes=[
            pltpu.VMEM((2 * tiles, rows, deep, LANES), jnp.float32),
            pltpu.VMEM((2 * tiles + 2, rows, deep, LANES), jnp.float32),
        ],
        name="smooth",
    )(info, *own, *partner, weight)


def edge_weights(positions, whole):
    total = jnp.zeros(positions.shape, jnp.float32)
    for k in range(-FILTER_R, FILTER_R + 1):
        at = positions + k
        total = total + jnp.where((at >= 0) & (at < whole), tap(k), 0.0)
    return total


def invert_kernel(normal, out):
    size = normal.shape[0]
    low, high = damping, damping + 4.0 * MAXB
    middle, spread = high + low, high - low
    peak = 2.0 * (middle / spread) ** 2 - 1.0
    row = lax.broadcasted_iota(jnp.int32, (size, size), 0)
    col = lax.broadcasted_iota(jnp.int32, (size, size), 1)
    unit = jnp.where(row == col, 1.0, 0.0).astype(jnp.float32)
    n = normal[...]
    guess = (8.0 * middle / spread**2 / peak) * unit - (8.0 / spread**2 / peak) * n
    dot = partial(jnp.dot, precision=lax.Precision.HIGHEST, preferred_element_type=jnp.float32)
    error = 1.0 / peak
    while error > 1e-8:
        scale = 2.0 / (2.0 - error * error)
        guess = scale * (guess + dot(guess, unit - dot(n, guess)))
        error = error * error / (2.0 - error * error)
    out[...] = guess


def invert(normal):
    size = normal.shape[0]
    return pl.pallas_call(
        invert_kernel,
        in_specs=[vmem()],
        out_specs=vmem(),
        out_shape=jax.ShapeDtypeStruct((size, size), jnp.float32),
        name="invert",
        cost_estimate=pl.CostEstimate(
            flops=120 * size**3, transcendentals=0, bytes_accessed=8 * size * size
        ),
    )(normal)


def series_kernel(block, got, inverse, screen, motion, right, solved):
    sources, per_stripe, _, deep = got.shape[:4]
    for q in range(per_stripe):
        for part in range(2):
            lanes = pl.ds(part * LANES, LANES)
            right[:, lanes] = jnp.zeros((right.shape[0], LANES), jnp.float32)
            for s in range(sources):
                at = pl.ds(s * block, deep)
                right[at, lanes] = right[at, lanes] + got[s, q, part]
        result = jnp.dot(
            right[: inverse.shape[0], :].T,
            inverse[...],
            precision=lax.Precision.HIGHEST,
            preferred_element_type=jnp.float32,
        )
        for part in range(inverse.shape[1] // LANES):
            lanes = pl.ds(part * LANES, LANES)
            solved[...] = result[:, part * LANES : (part + 1) * LANES]
            for comp in range(2):
                for u in range(8):
                    first = solved[pl.ds(comp * 8 + u, 8, stride=16), :]
                    second = solved[pl.ds(LANES + comp * 8 + u, 8, stride=16), :]
                    screen[comp, u, pl.ds(8 * q, 8), lanes] = second
                    motion[comp, u, pl.ds(8 * q, 8), lanes] = first - second


def invert_pixels(got, inverse, block):
    per_stripe = got.shape[1]
    dates = inverse.shape[0]
    shape = jax.ShapeDtypeStruct((2, 8, 8 * per_stripe, dates), jnp.float32)
    return pl.pallas_call(
        partial(series_kernel, block),
        in_specs=[vmem(), vmem()],
        out_specs=[vmem(), vmem()],
        out_shape=[shape, shape],
        scratch_shapes=[
            pltpu.VMEM((dates + got.shape[3] - block, 2 * LANES), jnp.float32),
            pltpu.VMEM((2 * LANES, LANES), jnp.float32),
        ],
        name="series",
    )(got, inverse)


def local(images, az, rg, pair_list):
    own, _, lines, full = images.shape
    dates = az.shape[0]
    groups, along, _ = (lax.axis_size(name) for name in ("pairs", "z", "x"))
    blocks = groups * along
    block = 2 * own
    deep = -(-(block + MAXB) // 8) * 8
    rows = groups
    tiles = full // LANES
    half = tiles // 2
    per_stripe = tiles // (2 * along)
    chunks = 2
    width = half // chunks
    x = lax.axis_index("x")
    place = lax.axis_index(("pairs", "z"))
    info = jnp.stack([x, (2 * place + x) * own, place * block]).astype(jnp.int32)

    split = min(own, MAXB)
    first = resample(images, az, rg, info, 0, split, per_stripe, chunks)
    pieces = [first]
    if own > split:
        pieces.append(resample(images, az, rg, info, split, own - split, per_stripe, chunks))

    swap = [(0, 1), (1, 0)]
    received = [[lax.ppermute(p[1 + c], "x", swap) for c in range(chunks)] for p in pieces]
    keeps = [p[0] for p in pieces]

    following = []
    for c in range(chunks):
        mine = lax.slice_in_dim(keeps[0], c * width, (c + 1) * width, axis=2)
        other = received[0][c]
        lower, upper = mine, other
        if split < MAXB:
            lower = jnp.concatenate([mine, other], 0)[:MAXB]
            upper = jnp.concatenate([other, mine], 0)[:MAXB]
        leading = jnp.where(x == 0, lower, upper)
        hops = []
        for hop in range(1, -(-MAXB // block) + 1):
            back = [(i + hop, i) for i in range(blocks - hop)]
            count = min(block, MAXB - (hop - 1) * block)
            hops.append(lax.ppermute(leading[:count], ("pairs", "z"), back))
        following.append(hops[0] if len(hops) == 1 else jnp.concatenate(hops, 0))

    date_ids = jnp.arange(dates, dtype=jnp.int32)
    is_reference = date_ids[:, None] == pair_list[None, :, 0]
    is_secondary = date_ids[:, None] == pair_list[None, :, 1]
    design = (is_reference.astype(jnp.float32) - is_secondary.astype(jnp.float32)).astype(
        jnp.bfloat16
    )
    normal = jnp.dot(design, design.T, preferred_element_type=jnp.float32)
    normal = normal + damping * jnp.eye(dates, dtype=jnp.float32)
    gaps = pair_list[:, 1] - pair_list[:, 0]
    is_gap = gaps[:, None] == jnp.arange(1, MAXB + 1, dtype=jnp.int32)[None, :]
    mask = jnp.dot(
        is_reference.astype(jnp.bfloat16),
        is_gap.astype(jnp.bfloat16),
        preferred_element_type=jnp.float32,
    )
    mask = mask.astype(jnp.int32).reshape(-1)
    inverse = invert(normal)

    sums = [
        pair_sums(
            info,
            mask,
            keeps,
            [r[c] for r in received],
            following[c],
            c,
            width,
            own,
            rows,
            deep,
        )
        for c in range(chunks)
    ]
    partner = [lax.ppermute(s, "x", swap) for s in sums]

    lane = jnp.arange(LANES, dtype=jnp.int32)
    row_at = jnp.arange(rows, dtype=jnp.int32)[:, None] * 8 + (lane & 7)[None, :]
    tile = jnp.arange(half, dtype=jnp.int32)
    tile = (2 * (tile // per_stripe) + x) * per_stripe + tile % per_stripe
    col_at = tile[:, None] * 8 + (lane // 16)[None, :]
    row_weight = edge_weights(row_at, lines // LA)
    col_weight = edge_weights(col_at, full // LR)
    weight = 1.0 / (row_weight[None, :, :] * col_weight[:, None, :])

    outgoing = filtered(info, sums, partner, weight, per_stripe)
    outgoing = outgoing.reshape((rows * along,) + outgoing.shape[2:])
    got = lax.all_to_all(outgoing, ("pairs", "z"), split_axis=0, concat_axis=0, tiled=True)
    screen, motion = invert_pixels(got, inverse, block)
    return tuple(jnp.transpose(v, (3, 0, 1, 2)) for v in (screen, motion))


def solution(mesh):
    shape = (mesh.shape["pairs"], mesh.shape["stripe"] // 2, 2)
    if isinstance(mesh, Mesh):
        finer = Mesh(mesh.devices.reshape(shape), ("pairs", "z", "x"))
    else:
        finer = jax.sharding.AbstractMesh(shape, ("pairs", "z", "x"))
    placed = P(None, None, "pairs", ("z", "x"))
    return jax.shard_map(
        local,
        mesh=finer,
        in_specs=(P(("pairs", "z", "x"), None, None, None), P(), P(), P()),
        out_specs=(placed, placed),
        check_vma=False,
    )
```

```python
from functools import partial

import jax
import jax.numpy as jnp
from jax import lax
from jax.experimental import pallas as pl
from jax.experimental.pallas import tpu as pltpu
from jax.sharding import Mesh, PartitionSpec as P


MAXB = 5
LA = 4
LR = 16
MAXA = 8
FILTER_R = 3
LANES = 128
GRANT = 16 << 20
damping = 0.5


def vmem():
    return pl.BlockSpec(memory_space=pltpu.VMEM)


def tap(k):
    sigma = FILTER_R / 2.0
    return jnp.exp(-jnp.float32(k * k) / jnp.float32(2.0 * sigma * sigma))


def resample_kernel(first, per_stripe, chunks, info, az, rg, img, *rest):
    rest = rest[-2 - chunks :]
    keep, sends, shifted = rest[0], rest[1 : 1 + chunks], rest[1 + chunks]
    lines, full = img.shape[2], img.shape[3]
    tiles = full // LANES
    half = tiles // 2
    high = lines + 2 * MAXA
    groups = lines // 8
    date = info[1] + first + pl.program_id(0)
    x = info[0]
    shift = rg[date]
    step = az[date]
    behind = shift < 0
    origin = jnp.where(behind, -1, 0)
    amount = shift - origin * LANES
    turn = lax.rem(LANES - amount, LANES)
    lane = lax.broadcasted_iota(jnp.int32, (lines, LANES), 1)
    own = lane + amount < LANES

    @pl.when((pl.program_id(0) == 0) & (pl.program_id(1) == 0))
    def _():
        blank = jnp.zeros((MAXA, LANES), jnp.float32)
        for t in range(tiles):
            shifted[pl.ds(t * high, MAXA), :] = blank
            shifted[pl.ds(t * high + MAXA + lines, MAXA), :] = blank

    def turned(t):
        place = jnp.clip(t + origin, 0, tiles - 1)
        tile = img[0, 0, :, pl.ds(pl.multiple_of(place * LANES, LANES), LANES)]
        out = pltpu.roll(tile.astype(jnp.float32), turn, 1)
        if t == 0:
            out = jnp.where(behind, 0.0, out)
        if t == tiles:
            out = jnp.where(behind, out, 0.0)
        return out

    here = turned(0)
    for t in range(tiles):
        after = turned(t + 1)
        shifted[pl.ds(t * high + MAXA, lines), :] = jnp.where(own, here, after)
        here = after

    def put(out, place, source):
        base = source * high + MAXA + step
        for pair in range(groups // 2):
            both = [shifted[pl.ds(base + 2 * pair + k, 8, stride=groups), :] for k in range(2)]
            out[0, 0, place, pl.ds(16 * pair, 16), :] = jnp.concatenate(both, 0).astype(
                jnp.bfloat16
            )

    per_chunk = half // chunks
    for h in range(half):
        stripe, inner = h // per_stripe, h % per_stripe
        put(sends[h // per_chunk], h % per_chunk, (2 * stripe + 1 - x) * per_stripe + inner)
        put(keep, h, (2 * stripe + x) * per_stripe + inner)


def resample(images, az, rg, info, first, count, per_stripe, chunks, earlier):
    lines, full = images.shape[2], images.shape[3]
    tiles = full // LANES
    half = tiles // 2

    def block(width):
        return pl.BlockSpec((1, 1, width, lines, LANES), lambda i, c, *_: (i, c, 0, 0, 0))

    def shape(width):
        return jax.ShapeDtypeStruct((count, 2, width, lines, LANES), jnp.bfloat16)

    return pl.pallas_call(
        partial(resample_kernel, first, per_stripe, chunks),
        grid_spec=pltpu.PrefetchScalarGridSpec(
            num_scalar_prefetch=3,
            grid=(count, 2),
            in_specs=[pl.BlockSpec((1, 1, lines, full), lambda i, c, *_: (i + first, c, 0, 0))]
            + [pl.BlockSpec(memory_space=pl.ANY)] * len(earlier),
            out_specs=[block(half)] + [block(half // chunks)] * chunks,
            scratch_shapes=[pltpu.VMEM((tiles * (lines + 2 * MAXA), LANES), jnp.float32)],
        ),
        out_shape=[shape(half)] + [shape(half // chunks)] * chunks,
        compiler_params=pltpu.CompilerParams(vmem_limit_bytes=GRANT),
        cost_estimate=pl.CostEstimate(
            flops=count * lines * full * 4,
            transcendentals=0,
            bytes_accessed=count * lines * full * 8,
        ),
    )(info, az, rg, images, *earlier)


def merge(x, y, bit, distance):
    return jnp.where(
        bit, x + pltpu.roll(x, LANES - distance, 1), y + pltpu.roll(y, distance, 1)
    )


def pair_kernel(own, starts, reached, info, mask, *refs):
    count = len(starts)
    parts, following = refs[: 2 * count], refs[2 * count : 2 * count + len(reached)]
    right, images, products, sums = refs[-4:]
    block = 2 * own
    x = info[0]
    mine, other = x * own, (1 - x) * own
    for s, start in enumerate(starts):
        for where, ref in ((mine, parts[2 * s]), (other, parts[2 * s + 1])):
            for i in range(ref.shape[0]):
                images[where + start + i] = ref[i, :, 0].astype(jnp.float32)
    for start, ref in zip(reached, following):
        for i in range(ref.shape[0]):
            images[block + start + i] = ref[i, :, 0].astype(jnp.float32)
    sums[...] = jnp.zeros_like(sums)

    def multiply(d, carry):
        for low in range(4):
            totals = [[None] * 2 for _ in range(MAXB)]
            for k in range(LA):
                at = pl.ds(8 * (LA * low + k), 8)
                a, b = images[d, 0, at, :], images[d, 1, at, :]
                for g in range(MAXB):
                    c, e = images[d + g + 1, 0, at, :], images[d + g + 1, 1, at, :]
                    terms = (a * c + b * e, b * c - a * e)
                    for comp, term in enumerate(terms):
                        old = totals[g][comp]
                        totals[g][comp] = term if old is None else old + term
            for g in range(MAXB):
                for comp in range(2):
                    at = (d * MAXB + g) * 64 + comp * 32 + low * 8
                    products[pl.ds(pl.multiple_of(at, 8), 8), :] = totals[g][comp]
        return carry

    lax.fori_loop(0, block, multiply, 0)
    lane = lax.broadcasted_iota(jnp.int32, (8, LANES), 1)
    bits = [lane & (1 << k) == 0 for k in range(4)]

    def slot(d, g):
        def load(comp, low):
            at = (d * MAXB + g) * 64 + comp * 32 + low * 8
            return products[pl.ds(pl.multiple_of(at, 8), 8), :]

        joined = []
        for comp in range(2):
            first = merge(load(comp, 0), load(comp, 1), bits[0], 1)
            second = merge(load(comp, 2), load(comp, 3), bits[0], 1)
            joined.append(merge(first, second, bits[1], 2))
        both = merge(joined[0], joined[1], bits[3], 8)
        result = merge(both, pltpu.roll(both, 7, 0), bits[2], 4)
        result = (result * (1.0 / (LA * LR))).astype(jnp.bfloat16).astype(jnp.float32)
        return result * mask[(info[2] + d) * MAXB + g].astype(jnp.float32)

    step = 4 if block % 4 == 0 else 1

    def gather(i, carry):
        totals = [None] * (step + MAXB)

        def add(at, value):
            totals[at] = value if totals[at] is None else totals[at] + value

        for j in range(step):
            for g in range(MAXB):
                value = slot(i * step + j, g)
                add(j, value)
                add(j + g + 1, -value)
        for j, value in enumerate(totals):
            at = pl.ds(pl.multiple_of(8 * (i * step + j), 8), 8)
            sums[at, :] = sums[at, :] + value
        return carry

    lax.fori_loop(0, block // step, gather, 0)
    for row in range(right.shape[1]):
        for group in range(right.shape[2] // 8):
            right[0, row, pl.ds(8 * group, 8), :] = sums[
                pl.ds(64 * group + 2 * row, 8, stride=8), :
            ]


def pair_sums(info, mask, pieces, following, earlier, chunk, chunks, width, own, rows, deep):
    lines = pieces[0][1].shape[3]

    def window(array, tiles):
        offset = chunk * width % tiles
        return pl.BlockSpec(
            (array.shape[0], 2, 1, lines, LANES), lambda i, *_: (0, 0, offset + i, 0, 0)
        )

    operands, specs = [], []
    for _, keep, received in pieces:
        got = received[chunk * len(received) // chunks]
        operands += [keep, got]
        specs += [window(keep, keep.shape[2]), window(got, got.shape[2])]
    for _, received in following:
        got = received[chunk * len(received) // chunks]
        operands.append(got)
        specs.append(window(got, got.shape[2]))
    if earlier is not None:
        operands.append(earlier)
        specs.append(pl.BlockSpec(memory_space=pl.ANY))
    work = 2 * own * MAXB * lines * LANES * width
    return pl.pallas_call(
        partial(pair_kernel, own, [p[0] for p in pieces], [f[0] for f in following]),
        grid_spec=pltpu.PrefetchScalarGridSpec(
            num_scalar_prefetch=2,
            grid=(width,),
            in_specs=specs,
            out_specs=pl.BlockSpec((1, rows, deep, LANES), lambda i, *_: (i, 0, 0, 0)),
            scratch_shapes=[
                pltpu.VMEM((2 * own + MAXB, 2, lines, LANES), jnp.float32),
                pltpu.VMEM((2 * own * MAXB * 64, LANES), jnp.float32),
                pltpu.VMEM((8 * deep, LANES), jnp.float32),
            ],
        ),
        out_shape=jax.ShapeDtypeStruct((width, rows, deep, LANES), jnp.float32),
        compiler_params=pltpu.CompilerParams(vmem_limit_bytes=GRANT),
        cost_estimate=pl.CostEstimate(flops=work * 8, transcendentals=0, bytes_accessed=work),
    )(info, mask, *operands)


def filter_kernel(per_stripe, chunks, info, *rest):
    own, partner = rest[:chunks], rest[chunks : 2 * chunks]
    weight, out, whole, along = rest[2 * chunks :]
    width, rows, deep = own[0].shape[:3]
    total = 2 * width * chunks
    x = info[0]
    blank = jnp.zeros((rows, deep, LANES), jnp.float32)
    along[0] = blank
    along[total + 1] = blank
    for c in range(chunks):
        for i in range(width):
            stripe, inner = divmod(c * width + i, per_stripe)
            whole[(2 * stripe + x) * per_stripe + inner] = own[c][i]
            whole[(2 * stripe + 1 - x) * per_stripe + inner] = partner[c][i]
    lane = lax.broadcasted_iota(jnp.int32, (deep, LANES), 1)
    place = lane & 7
    taps = [tap(k) for k in range(FILTER_R + 1)]

    def turn(v, k):
        return pltpu.roll(v, k % LANES, 1)

    def filter_rows(i, carry):
        for r in range(rows):
            v = whole[i, r]
            acc = v
            for k in range(1, FILTER_R + 1):
                up = turn(whole[i, r + 1], 8 - k) if r + 1 < rows else jnp.zeros_like(v)
                down = turn(whole[i, r - 1], k - 8) if r > 0 else jnp.zeros_like(v)
                near = jnp.where(place < 8 - k, turn(v, -k), up) + jnp.where(
                    place >= k, turn(v, k), down
                )
                acc = acc + taps[k] * near
            along[i + 1, r] = acc
        return carry

    lax.fori_loop(0, total, filter_rows, 0)

    for c in range(chunks):
        for i in range(width):
            h = c * width + i
            stripe, inner = divmod(h, per_stripe)
            at = (2 * stripe + x) * per_stripe + inner + 1
            for r in range(rows):
                v, left, right = along[at, r], along[at - 1, r], along[at + 1, r]
                acc = v
                for k in range(1, FILTER_R + 1):
                    reach = 16 * k
                    near = jnp.where(
                        lane < LANES - reach, turn(v, -reach), turn(right, -reach)
                    ) + jnp.where(lane >= reach, turn(v, reach), turn(left, reach))
                    acc = acc + taps[k] * near
                out[r, stripe, inner, 0] = own[c][i, r]
                out[r, stripe, inner, 1] = acc * weight[h, r : r + 1, :]


def filtered(info, own, partner, weight, per_stripe):
    chunks = len(own)
    width, rows, deep = own[0].shape[:3]
    tiles = width * chunks
    stripes = tiles // per_stripe
    smem = pl.BlockSpec(memory_space=pltpu.SMEM)
    return pl.pallas_call(
        partial(filter_kernel, per_stripe, chunks),
        in_specs=[smem] + [vmem()] * (2 * chunks + 1),
        out_specs=vmem(),
        out_shape=jax.ShapeDtypeStruct((rows, stripes, per_stripe, 2, deep, LANES), jnp.float32),
        scratch_shapes=[
            pltpu.VMEM((2 * tiles, rows, deep, LANES), jnp.float32),
            pltpu.VMEM((2 * tiles + 2, rows, deep, LANES), jnp.float32),
        ],
        name="smooth",
        compiler_params=pltpu.CompilerParams(vmem_limit_bytes=GRANT),
    )(info, *own, *partner, weight)


def edge_weights(positions, whole):
    total = jnp.zeros(positions.shape, jnp.float32)
    for k in range(-FILTER_R, FILTER_R + 1):
        at = positions + k
        total = total + jnp.where((at >= 0) & (at < whole), tap(k), 0.0)
    return total


def invert_kernel(normal, out):
    size = normal.shape[0]
    low, high = damping, damping + 4.0 * MAXB
    middle, spread = high + low, high - low
    peak = 2.0 * (middle / spread) ** 2 - 1.0
    row = lax.broadcasted_iota(jnp.int32, (size, size), 0)
    col = lax.broadcasted_iota(jnp.int32, (size, size), 1)
    unit = jnp.where(row == col, 1.0, 0.0).astype(jnp.float32)
    n = normal[...]
    guess = (8.0 * middle / spread**2 / peak) * unit - (8.0 / spread**2 / peak) * n
    whole = n.astype(jnp.bfloat16)

    def times_normal(value):
        total = None
        for _ in range(3):
            part = value.astype(jnp.bfloat16)
            value = value - part.astype(jnp.float32)
            term = jnp.dot(whole, part, preferred_element_type=jnp.float32)
            total = term if total is None else total + term
        return total

    error = 1.0 / peak
    while error > 1e-8:
        scale = 2.0 / (2.0 - error * error)
        residual = unit - times_normal(guess)
        precision = lax.Precision.HIGHEST if error < 0.1 else lax.Precision.DEFAULT
        change = jnp.dot(guess, residual, precision=precision, preferred_element_type=jnp.float32)
        guess = scale * (guess + change)
        error = error * error / (2.0 - error * error)
    out[...] = guess


def invert(normal):
    size = normal.shape[0]
    return pl.pallas_call(
        invert_kernel,
        in_specs=[vmem()],
        out_specs=vmem(),
        out_shape=jax.ShapeDtypeStruct((size, size), jnp.float32),
        name="invert",
        compiler_params=pltpu.CompilerParams(vmem_limit_bytes=GRANT),
        cost_estimate=pl.CostEstimate(
            flops=120 * size**3, transcendentals=0, bytes_accessed=8 * size * size
        ),
    )(normal)


def series_kernel(block, got, inverse, screen, motion, right, solved):
    sources, per_stripe, _, deep = got.shape[:4]
    for q in range(per_stripe):
        for part in range(2):
            lanes = pl.ds(part * LANES, LANES)
            right[:, lanes] = jnp.zeros((right.shape[0], LANES), jnp.float32)
            for s in range(sources):
                at = pl.ds(s * block, deep)
                right[at, lanes] = right[at, lanes] + got[s, q, part]
        result = jnp.dot(
            right[: inverse.shape[0], :].T,
            inverse[...],
            precision=lax.Precision.HIGHEST,
            preferred_element_type=jnp.float32,
        )
        for part in range(inverse.shape[1] // LANES):
            lanes = pl.ds(part * LANES, LANES)
            solved[...] = result[:, part * LANES : (part + 1) * LANES]
            for comp in range(2):
                for u in range(8):
                    first = solved[pl.ds(comp * 8 + u, 8, stride=16), :]
                    second = solved[pl.ds(LANES + comp * 8 + u, 8, stride=16), :]
                    screen[comp, u, pl.ds(8 * q, 8), lanes] = second
                    motion[comp, u, pl.ds(8 * q, 8), lanes] = first - second


def invert_pixels(got, inverse, block):
    per_stripe = got.shape[1]
    dates = inverse.shape[0]
    shape = jax.ShapeDtypeStruct((2, 8, 8 * per_stripe, dates), jnp.float32)
    return pl.pallas_call(
        partial(series_kernel, block),
        in_specs=[vmem(), vmem()],
        out_specs=[vmem(), vmem()],
        out_shape=[shape, shape],
        scratch_shapes=[
            pltpu.VMEM((dates + got.shape[3] - block, 2 * LANES), jnp.float32),
            pltpu.VMEM((2 * LANES, LANES), jnp.float32),
        ],
        name="series",
        compiler_params=pltpu.CompilerParams(vmem_limit_bytes=GRANT),
    )(got, inverse)


def local(images, az, rg, pair_list):
    own, _, lines, full = images.shape
    dates = az.shape[0]
    groups, along, _ = (lax.axis_size(name) for name in ("pairs", "z", "x"))
    blocks = groups * along
    block = 2 * own
    deep = -(-(block + MAXB) // 8) * 8
    rows = groups
    tiles = full // LANES
    half = tiles // 2
    per_stripe = tiles // (2 * along)
    chunks = 4 if half % 4 == 0 else 1
    width = half // chunks
    x = lax.axis_index("x")
    place = lax.axis_index(("pairs", "z"))
    info = jnp.stack([x, (2 * place + x) * own, place * block]).astype(jnp.int32)

    date_ids = jnp.arange(dates, dtype=jnp.int32)
    is_reference = date_ids[:, None] == pair_list[None, :, 0]
    is_secondary = date_ids[:, None] == pair_list[None, :, 1]
    design = (is_reference.astype(jnp.float32) - is_secondary.astype(jnp.float32)).astype(
        jnp.bfloat16
    )
    normal = jnp.dot(design, design.T, preferred_element_type=jnp.float32)
    normal = normal + damping * jnp.eye(dates, dtype=jnp.float32)
    gaps = pair_list[:, 1] - pair_list[:, 0]
    is_gap = gaps[:, None] == jnp.arange(1, MAXB + 1, dtype=jnp.int32)[None, :]
    mask = jnp.dot(
        is_reference.astype(jnp.bfloat16),
        is_gap.astype(jnp.bfloat16),
        preferred_element_type=jnp.float32,
    )
    mask = mask.astype(jnp.int32).reshape(-1)
    inverse = invert(normal)

    swap = [(0, 1), (1, 0)]
    cuts = [0, own] if own <= MAXB else [0, 2, MAXB, own]
    pieces, following = [], []
    left, turn = x == 0, 0
    for k, (start, end) in enumerate(zip(cuts, cuts[1:])):
        keep, *sends = resample(
            images,
            az,
            rg,
            info,
            start,
            end - start,
            per_stripe,
            min(chunks, 2**k),
            [p[1] for p in pieces[-1:]],
        )
        received = []
        for v in sends:
            received.append(lax.ppermute(v, "x", swap))
            turn += 1
        pieces.append((start, keep, received))
        if start >= MAXB:
            continue
        hops = []
        for c, other in enumerate(pieces[-1][2]):
            tiles = other.shape[2]
            mine = lax.slice_in_dim(keep, c * tiles, (c + 1) * tiles, axis=2)
            lower, upper = mine, other
            if own < MAXB:
                lower = jnp.concatenate([mine, other], 0)[:MAXB]
                upper = jnp.concatenate([other, mine], 0)[:MAXB]
            hops.append(jnp.where(left, lower, upper))
            if end == own:
                continue
            waited = (left, hops[-1]) if following else (left, hops[-1], inverse)
            left, hops[-1], *waited = lax.optimization_barrier(waited)
            inverse = waited[0] if waited else inverse
        if own < MAXB:
            for hop in range(1, -(-MAXB // block) + 1):
                route = [(i + hop, i) for i in range(blocks - hop)]
                count = min(block, MAXB - (hop - 1) * block)
                going = [lax.ppermute(v[:count], ("pairs", "z"), route) for v in hops]
                following.append(((hop - 1) * block, going))
        else:
            route = [(i + 1, i) for i in range(blocks - 1)]
            following.append((start, [lax.ppermute(v, ("pairs", "z"), route) for v in hops]))

    sums = []
    for c in range(chunks):
        earlier = sums[-1] if sums else None
        sums.append(
            pair_sums(
                info, mask, pieces, following, earlier, c, chunks, width, own, rows, deep
            )
        )
    partner = [lax.ppermute(s, "x", swap) for s in sums]

    lane = jnp.arange(LANES, dtype=jnp.int32)
    row_at = jnp.arange(rows, dtype=jnp.int32)[:, None] * 8 + (lane & 7)[None, :]
    tile = jnp.arange(half, dtype=jnp.int32)
    tile = (2 * (tile // per_stripe) + x) * per_stripe + tile % per_stripe
    col_at = tile[:, None] * 8 + (lane // 16)[None, :]
    row_weight = edge_weights(row_at, lines // LA)
    col_weight = edge_weights(col_at, full // LR)
    weight = 1.0 / (row_weight[None, :, :] * col_weight[:, None, :])

    outgoing = filtered(info, sums, partner, weight, per_stripe)
    outgoing = outgoing.reshape((rows * along,) + outgoing.shape[2:])
    got = lax.all_to_all(outgoing, ("pairs", "z"), split_axis=0, concat_axis=0, tiled=True)
    screen, motion = invert_pixels(got, inverse, block)
    return tuple(jnp.transpose(v, (3, 0, 1, 2)) for v in (screen, motion))


def solution(mesh):
    shape = (mesh.shape["pairs"], mesh.shape["stripe"] // 2, 2)
    if isinstance(mesh, Mesh):
        finer = Mesh(mesh.devices.reshape(shape), ("pairs", "z", "x"))
    else:
        finer = jax.sharding.AbstractMesh(shape, ("pairs", "z", "x"))
    placed = P(None, None, "pairs", ("z", "x"))

    return jax.shard_map(
        local,
        mesh=finer,
        in_specs=(P(("pairs", "z", "x"), None, None, None), P(), P(), P()),
        out_specs=(placed, placed),
        check_vma=False,
    )
```

```python
from functools import partial

import jax
import jax.numpy as jnp
from jax import lax
from jax.experimental import pallas as pl
from jax.experimental.pallas import tpu as pltpu
from jax.sharding import Mesh, PartitionSpec as P


MAXB = 5
LA = 4
LR = 16
MAXA = 8
FILTER_R = 3
LANES = 128
STRIPES = 4
GRANT = 16 << 20
WHOLE_GRANT = 60 << 20
damping = 0.5


def vmem():
    return pl.BlockSpec(memory_space=pltpu.VMEM)


def tap(k):
    sigma = FILTER_R / 2.0
    return jnp.exp(-jnp.float32(k * k) / jnp.float32(2.0 * sigma * sigma))


def resample_kernel(first, parts, info, az, rg, img, *rest):
    rest = rest[-4 - parts :]
    keep, sends = rest[0], rest[1 : 1 + parts]
    tiles_of, spread, shifted = rest[1 + parts :]
    lines, full = img.shape[2], img.shape[3]
    tiles = full // LANES
    groups = tiles // (2 * STRIPES)
    blocks = lines // (8 * LA)
    high = lines + 2 * MAXA
    span = STRIPES * LANES
    date = info[1] + first + pl.program_id(0)
    x = info[0]
    shift = rg[date]
    step = az[date]
    behind = shift < 0
    origin = jnp.where(behind, -1, 0)
    amount = shift - origin * LANES
    turn = lax.rem(LANES - amount, LANES)
    lane = lax.broadcasted_iota(jnp.int32, (lines, LANES), 1)
    own = lane + amount < LANES

    @pl.when(pl.program_id(0) == 0)
    def _():
        blank = jnp.zeros((MAXA, LANES), jnp.float32)
        for t in range(shifted.shape[0] // high):
            shifted[pl.ds(t * high, MAXA), :] = blank
            shifted[pl.ds(t * high + MAXA + lines, MAXA), :] = blank
        source = lax.broadcasted_iota(jnp.int32, (span, span), 0)
        target = lax.broadcasted_iota(jnp.int32, (1, span), 1)
        column, few = target & 7, (target >> 3) & 3
        stripe, many = (target >> 5) & 3, target >> 7
        wanted = stripe * LANES + column * LR + many * 4 + few
        spread[...] = jnp.where(source == wanted, 1.0, 0.0).astype(jnp.bfloat16)

    for c in range(2):

        def turned(t):
            place = jnp.clip(t + origin, 0, tiles - 1)
            tile = img[0, c, :, pl.ds(pl.multiple_of(place * LANES, LANES), LANES)]
            out = pltpu.roll(tile.astype(jnp.float32), turn, 1)
            if t == 0:
                out = jnp.where(behind, 0.0, out)
            if t == tiles:
                out = jnp.where(behind, out, 0.0)
            return out

        here = turned(0)
        for t in range(tiles):
            after = turned(t + 1)
            group, stripe, parity = t // 2 // STRIPES, t // 2 % STRIPES, t % 2
            tiles_of[
                group, pl.ds((c * 2 + parity) * lines, lines), pl.ds(stripe * LANES, LANES)
            ] = jnp.where(own, here, after).astype(jnp.bfloat16)
            here = after

    def slab(c, parity, group, many):
        return (((c * 2 + parity) * groups + group) * 4 + many) * high + MAXA

    for group in range(groups):
        for half in range(2):
            result = jnp.dot(
                tiles_of[group],
                spread[:, half * span // 2 : (half + 1) * span // 2],
                preferred_element_type=jnp.float32,
            )
            for c in range(2):
                for parity in range(2):
                    for k in range(2):
                        at = (c * 2 + parity) * lines
                        shifted[pl.ds(slab(c, parity, group, 2 * half + k), lines), :] = result[
                            at : at + lines, k * LANES : (k + 1) * LANES
                        ]

    def put(out, place, block, c, group, parity):
        for look in range(LA):
            for pair in range(2):
                both = [
                    shifted[
                        pl.ds(
                            slab(c, parity, group, 2 * pair + k) + step + 8 * LA * block + look,
                            8,
                            stride=LA,
                        ),
                        :,
                    ]
                    for k in range(2)
                ]
                out[0, c, place, group, pl.ds(32 * look + 16 * pair, 16), :] = jnp.concatenate(
                    both, 0
                ).astype(jnp.bfloat16)

    width = blocks // parts
    for c in range(2):
        for block in range(blocks):
            for group in range(groups):
                put(sends[block // width], block % width, block, c, group, 1 - x)
                put(keep, block, block, c, group, x)


def resample(images, az, rg, info, first, count, parts, earlier):
    lines, full = images.shape[2], images.shape[3]
    tiles = full // LANES
    groups = tiles // (2 * STRIPES)
    blocks = lines // (8 * LA)
    rows = 8 * LA * 4

    def block(width):
        return pl.BlockSpec(
            (1, 2, width, groups, rows, LANES), lambda i, *_: (i, 0, 0, 0, 0, 0)
        )

    def shape(width):
        return jax.ShapeDtypeStruct((count, 2, width, groups, rows, LANES), jnp.bfloat16)

    widths = [blocks] + [blocks // parts] * parts
    return pl.pallas_call(
        partial(resample_kernel, first, parts),
        grid_spec=pltpu.PrefetchScalarGridSpec(
            num_scalar_prefetch=3,
            grid=(count,),
            in_specs=[pl.BlockSpec((1, 2, lines, full), lambda i, *_: (i + first, 0, 0, 0))]
            + [pl.BlockSpec(memory_space=pl.ANY)] * len(earlier),
            out_specs=[block(w) for w in widths],
            scratch_shapes=[
                pltpu.VMEM((groups, 4 * lines, STRIPES * LANES), jnp.bfloat16),
                pltpu.VMEM((STRIPES * LANES, STRIPES * LANES), jnp.bfloat16),
                pltpu.VMEM((16 * groups * (lines + 2 * MAXA), LANES), jnp.float32),
            ],
        ),
        out_shape=[shape(w) for w in widths],
        compiler_params=pltpu.CompilerParams(vmem_limit_bytes=WHOLE_GRANT),
        cost_estimate=pl.CostEstimate(
            flops=count * lines * full * 4,
            transcendentals=0,
            bytes_accessed=count * lines * full * 8,
        ),
    )(info, az, rg, images, *earlier)


def merge(x, y, bit, distance):
    return jnp.where(
        bit, x + pltpu.roll(x, LANES - distance, 1), y + pltpu.roll(y, distance, 1)
    )


def pair_kernel(own, starts, reached, info, mask, *refs):
    count = len(starts)
    parts, following = refs[: 2 * count], refs[2 * count : 2 * count + len(reached)]
    right, images, products, sums = refs[-4:]
    block = 2 * own
    x = info[0]
    mine, other = x * own, (1 - x) * own
    for s, start in enumerate(starts):
        for where, ref in ((mine, parts[2 * s]), (other, parts[2 * s + 1])):
            for i in range(ref.shape[0]):
                images[where + start + i] = ref[i, :, 0, 0].astype(jnp.float32)
    for start, ref in zip(reached, following):
        for i in range(ref.shape[0]):
            images[block + start + i] = ref[i, :, 0, 0].astype(jnp.float32)
    sums[...] = jnp.zeros_like(sums)

    def multiply(d, carry):
        totals = [[None] * 2 for _ in range(MAXB)]
        for k in range(images.shape[2] // 8):
            at = pl.ds(8 * k, 8)
            a, b = images[d, 0, at, :], images[d, 1, at, :]
            for g in range(MAXB):
                c, e = images[d + g + 1, 0, at, :], images[d + g + 1, 1, at, :]
                terms = (a * c + b * e, b * c - a * e)
                for comp, term in enumerate(terms):
                    old = totals[g][comp]
                    totals[g][comp] = term if old is None else old + term
        for g in range(MAXB):
            for comp in range(2):
                at = ((d * MAXB + g) * 2 + comp) * 8
                products[pl.ds(pl.multiple_of(at, 8), 8), :] = totals[g][comp]
        return carry

    lax.fori_loop(0, block, multiply, 0)
    lane = lax.broadcasted_iota(jnp.int32, (8, LANES), 1)
    real = lane & 8 == 0
    place = lane >> 4

    def slot(d, g):
        at = (d * MAXB + g) * 16
        value = merge(
            products[pl.ds(pl.multiple_of(at, 8), 8), :],
            products[pl.ds(pl.multiple_of(at + 8, 8), 8), :],
            real,
            8,
        )
        value = value + pltpu.roll(value, LANES - 16, 1)
        value = (value * (1.0 / (LA * LR))).astype(jnp.bfloat16).astype(jnp.float32)
        return value * mask[(info[2] + d) * MAXB + g].astype(jnp.float32)

    step = 4 if block % 4 == 0 else 1

    def gather(i, carry):
        totals = [None] * (step + MAXB)

        def add(at, value):
            totals[at] = value if totals[at] is None else totals[at] + value

        for j in range(step):
            for g in range(MAXB):
                value = slot(i * step + j, g)
                add(j, value)
                add(j + g + 1, -value)
        for j, value in enumerate(totals):
            at = pl.ds(pl.multiple_of(8 * (i * step + j), 8), 8)
            sums[at, :] = sums[at, :] + value
        return carry

    lax.fori_loop(0, block // step, gather, 0)
    for group in range(right.shape[1] // 8):
        rows = [sums[pl.ds(64 * group + u, 8, stride=8), :] for u in range(8)]
        turned = []
        for s in range(8):
            joined = rows[s]
            for z in range(1, STRIPES):
                joined = jnp.where(place == 2 * z, rows[(s + 2 * z) % 8], joined)
            turned.append(pltpu.roll(joined, 16 * s, 1) if s else joined)
        for z in range(STRIPES):
            out = turned[0]
            for s in range(1, 8):
                out = jnp.where(place == (2 * z + s) % 8, turned[s], out)
            right[z, pl.ds(8 * group, 8), :] = out


def pair_sums(info, mask, pieces, following, earlier, chunk, chunks, own, deep):
    groups, lines = pieces[0][1].shape[3:5]

    def window(array, parts):
        offset = chunk % (chunks // parts)
        return pl.BlockSpec(
            (array.shape[0], 2, 1, 1, lines, LANES), lambda i, *_: (0, 0, offset, i, 0, 0)
        )

    operands, specs = [], []
    for _, keep, received in pieces:
        got = received[chunk * len(received) // chunks]
        operands += [keep, got]
        specs += [window(keep, 1), window(got, len(received))]
    for _, received in following:
        got = received[chunk * len(received) // chunks]
        operands.append(got)
        specs.append(window(got, len(received)))
    if earlier is not None:
        operands.append(earlier)
        specs.append(pl.BlockSpec(memory_space=pl.ANY))
    work = 2 * own * MAXB * lines * LANES * groups
    return pl.pallas_call(
        partial(pair_kernel, own, [p[0] for p in pieces], [f[0] for f in following]),
        grid_spec=pltpu.PrefetchScalarGridSpec(
            num_scalar_prefetch=2,
            grid=(groups,),
            in_specs=specs,
            out_specs=pl.BlockSpec((STRIPES, deep, LANES), lambda i, *_: (i, 0, 0)),
            scratch_shapes=[
                pltpu.VMEM((2 * own + MAXB, 2, lines, LANES), jnp.float32),
                pltpu.VMEM((2 * own * MAXB * 16, LANES), jnp.float32),
                pltpu.VMEM((8 * deep, LANES), jnp.float32),
            ],
        ),
        out_shape=jax.ShapeDtypeStruct((groups * STRIPES, deep, LANES), jnp.float32),
        compiler_params=pltpu.CompilerParams(vmem_limit_bytes=GRANT),
        cost_estimate=pl.CostEstimate(flops=work * 8, transcendentals=0, bytes_accessed=work),
    )(info, mask, *operands)


def filter_kernel(rows, info, *rest):
    own, partner = rest[:rows], rest[rows : 2 * rows]
    weight, out, along = rest[2 * rows :]
    tiles, deep = own[0].shape[:2]
    x = info[0]
    blank = jnp.zeros((rows, deep, LANES), jnp.float32)
    along[0] = blank
    along[2 * tiles + 1] = blank
    lane = lax.broadcasted_iota(jnp.int32, (deep, LANES), 1)
    place = lane & 7
    taps = [tap(k) for k in range(FILTER_R + 1)]

    def turn(v, k):
        return pltpu.roll(v, k % LANES, 1)

    for refs, side in ((partner, 1 - x), (own, x)):
        for i in range(tiles):
            values = [ref[i] for ref in refs]
            for r in range(rows):
                acc = values[r]
                for k in range(1, FILTER_R + 1):
                    reach = 16 * k
                    last = values[r - 1] if r > 0 else jnp.zeros_like(acc)
                    later = values[r + 1] if r + 1 < rows else jnp.zeros_like(acc)
                    up = turn(jnp.where(lane >= reach, values[r], later), -reach)
                    down = turn(jnp.where(lane < LANES - reach, values[r], last), reach)
                    acc = acc + taps[k] * (up + down)
                along[2 * i + side + 1, r] = acc

    for i in range(tiles):
        at = 2 * i + x + 1
        for r in range(rows):
            v, left, right = along[at, r], along[at - 1, r], along[at + 1, r]
            acc = v
            for k in range(1, FILTER_R + 1):
                near = jnp.where(place < 8 - k, turn(v, -k), turn(right, 8 - k)) + jnp.where(
                    place >= k, turn(v, k), turn(left, k - 8)
                )
                acc = acc + taps[k] * near
            out[r, i, 0] = own[r][i]
            out[r, i, 1] = acc * weight[i, r : r + 1, :]


def filtered(info, own, partner, weight):
    rows = len(own)
    tiles, deep = own[0].shape[:2]
    smem = pl.BlockSpec(memory_space=pltpu.SMEM)
    return pl.pallas_call(
        partial(filter_kernel, rows),
        in_specs=[smem] + [vmem()] * (2 * rows + 1),
        out_specs=vmem(),
        out_shape=jax.ShapeDtypeStruct((rows, tiles, 2, deep, LANES), jnp.float32),
        scratch_shapes=[pltpu.VMEM((2 * tiles + 2, rows, deep, LANES), jnp.float32)],
        name="smooth",
        compiler_params=pltpu.CompilerParams(vmem_limit_bytes=GRANT),
    )(info, *own, *partner, weight)


def edge_weights(positions, whole):
    total = jnp.zeros(positions.shape, jnp.float32)
    for k in range(-FILTER_R, FILTER_R + 1):
        at = positions + k
        total = total + jnp.where((at >= 0) & (at < whole), tap(k), 0.0)
    return total


def invert_kernel(normal, out):
    size = normal.shape[0]
    low, high = damping, damping + 4.0 * MAXB
    middle, spread = high + low, high - low
    peak = 2.0 * (middle / spread) ** 2 - 1.0
    row = lax.broadcasted_iota(jnp.int32, (size, size), 0)
    col = lax.broadcasted_iota(jnp.int32, (size, size), 1)
    unit = jnp.where(row == col, 1.0, 0.0).astype(jnp.float32)
    n = normal[...]
    guess = (8.0 * middle / spread**2 / peak) * unit - (8.0 / spread**2 / peak) * n
    whole = n.astype(jnp.bfloat16)

    def times_normal(value):
        total = None
        for _ in range(3):
            part = value.astype(jnp.bfloat16)
            value = value - part.astype(jnp.float32)
            term = jnp.dot(whole, part, preferred_element_type=jnp.float32)
            total = term if total is None else total + term
        return total

    error = 1.0 / peak
    while error > 1e-8:
        scale = 2.0 / (2.0 - error * error)
        residual = unit - times_normal(guess)
        precision = lax.Precision.HIGHEST if error < 0.1 else lax.Precision.DEFAULT
        change = jnp.dot(guess, residual, precision=precision, preferred_element_type=jnp.float32)
        guess = scale * (guess + change)
        error = error * error / (2.0 - error * error)
    out[...] = guess


def invert(normal):
    size = normal.shape[0]
    return pl.pallas_call(
        invert_kernel,
        in_specs=[vmem()],
        out_specs=vmem(),
        out_shape=jax.ShapeDtypeStruct((size, size), jnp.float32),
        name="invert",
        compiler_params=pltpu.CompilerParams(vmem_limit_bytes=GRANT),
        cost_estimate=pl.CostEstimate(
            flops=120 * size**3, transcendentals=0, bytes_accessed=8 * size * size
        ),
    )(normal)


def series_kernel(block, got, inverse, screen, motion, right):
    sources, _, deep = got.shape[:3]
    right[...] = jnp.zeros_like(right)
    for part in range(2):
        lanes = pl.ds(part * LANES, LANES)
        for s in range(sources):
            at = pl.ds(s * block, deep)
            right[at, lanes] = right[at, lanes] + got[s, part]
    result = jnp.dot(
        right[: inverse.shape[0], :].T,
        inverse[...],
        precision=lax.Precision.HIGHEST,
        preferred_element_type=jnp.float32,
    )
    for u in range(8):
        for comp in range(2):
            at = u * 16 + comp * 8
            first, second = result[at : at + 8], result[LANES + at : LANES + at + 8]
            screen[comp, u] = second
            motion[comp, u] = first - second


def invert_pixels(got, inverse, block):
    dates = inverse.shape[0]
    shape = jax.ShapeDtypeStruct((2, 8, 8, dates), jnp.float32)
    return pl.pallas_call(
        partial(series_kernel, block),
        in_specs=[vmem(), vmem()],
        out_specs=[vmem(), vmem()],
        out_shape=[shape, shape],
        scratch_shapes=[pltpu.VMEM((dates + got.shape[2] - block, 2 * LANES), jnp.float32)],
        name="series",
        compiler_params=pltpu.CompilerParams(vmem_limit_bytes=GRANT),
    )(got, inverse)


def local(images, az, rg, pair_list):
    own, _, lines, full = images.shape
    dates = az.shape[0]
    groups, along, _ = (lax.axis_size(name) for name in ("pairs", "z", "x"))
    blocks = groups * along
    block = 2 * own
    deep = -(-(block + MAXB) // 8) * 8
    rows = groups
    if full != 2 * along * LANES or along % STRIPES or lines != rows * 8 * LA:
        raise ValueError("unsupported shape")
    x = lax.axis_index("x")
    place = lax.axis_index(("pairs", "z"))
    info = jnp.stack([x, (2 * place + x) * own, place * block]).astype(jnp.int32)

    date_ids = jnp.arange(dates, dtype=jnp.int32)
    is_reference = date_ids[:, None] == pair_list[None, :, 0]
    is_secondary = date_ids[:, None] == pair_list[None, :, 1]
    design = (is_reference.astype(jnp.float32) - is_secondary.astype(jnp.float32)).astype(
        jnp.bfloat16
    )
    normal = jnp.dot(design, design.T, preferred_element_type=jnp.float32)
    normal = normal + damping * jnp.eye(dates, dtype=jnp.float32)
    gaps = pair_list[:, 1] - pair_list[:, 0]
    is_gap = gaps[:, None] == jnp.arange(1, MAXB + 1, dtype=jnp.int32)[None, :]
    mask = jnp.dot(
        is_reference.astype(jnp.bfloat16),
        is_gap.astype(jnp.bfloat16),
        preferred_element_type=jnp.float32,
    )
    mask = mask.astype(jnp.int32).reshape(-1)
    inverse = invert(normal)

    swap = [(0, 1), (1, 0)]
    cuts = [0, own] if own <= MAXB else [0, 2, MAXB, own]
    pieces, following = [], []
    left, turn = x == 0, 0
    for k, (start, end) in enumerate(zip(cuts, cuts[1:])):
        keep, *sends = resample(
            images, az, rg, info, start, end - start, min(rows, 2**k), [p[1] for p in pieces[-1:]]
        )
        received = []
        for v in sends:
            received.append(lax.ppermute(v, "x", swap))
            turn += 1
        pieces.append((start, keep, received))
        if start >= MAXB:
            continue
        hops = []
        for c, other in enumerate(pieces[-1][2]):
            tiles = other.shape[2]
            mine = lax.slice_in_dim(keep, c * tiles, (c + 1) * tiles, axis=2)
            lower, upper = mine, other
            if own < MAXB:
                lower = jnp.concatenate([mine, other], 0)[:MAXB]
                upper = jnp.concatenate([other, mine], 0)[:MAXB]
            hops.append(jnp.where(left, lower, upper))
            if end == own:
                continue
            waited = (left, hops[-1]) if following else (left, hops[-1], inverse)
            left, hops[-1], *waited = lax.optimization_barrier(waited)
            inverse = waited[0] if waited else inverse
        if own < MAXB:
            for hop in range(1, -(-MAXB // block) + 1):
                route = [(i + hop, i) for i in range(blocks - hop)]
                count = min(block, MAXB - (hop - 1) * block)
                going = [lax.ppermute(v[:count], ("pairs", "z"), route) for v in hops]
                following.append(((hop - 1) * block, going))
        else:
            route = [(i + 1, i) for i in range(blocks - 1)]
            following.append((start, [lax.ppermute(v, ("pairs", "z"), route) for v in hops]))

    sums = []
    for c in range(rows):
        earlier = sums[-1] if sums else None
        sums.append(pair_sums(info, mask, pieces, following, earlier, c, rows, own, deep))
    partner = [lax.ppermute(s, "x", swap) for s in sums]

    lane = jnp.arange(LANES, dtype=jnp.int32)
    row_at = jnp.arange(rows, dtype=jnp.int32)[:, None] * 8 + (lane // 16)[None, :]
    stripe = 2 * jnp.arange(along, dtype=jnp.int32) + x
    col_at = stripe[:, None] * 8 + (lane & 7)[None, :]
    row_weight = edge_weights(row_at, lines // LA)
    col_weight = edge_weights(col_at, full // LR)
    weight = 1.0 / (row_weight[None, :, :] * col_weight[:, None, :])

    outgoing = filtered(info, sums, partner, weight)
    outgoing = outgoing.reshape((rows * along,) + outgoing.shape[2:])
    got = lax.all_to_all(outgoing, ("pairs", "z"), split_axis=0, concat_axis=0, tiled=True)
    screen, motion = invert_pixels(got, inverse, block)
    return tuple(jnp.transpose(v, (3, 0, 1, 2)) for v in (screen, motion))


def solution(mesh):
    shape = (mesh.shape["pairs"], mesh.shape["stripe"] // 2, 2)
    if isinstance(mesh, Mesh):
        finer = Mesh(mesh.devices.reshape(shape), ("pairs", "z", "x"))
    else:
        finer = jax.sharding.AbstractMesh(shape, ("pairs", "z", "x"))
    placed = P(None, None, "pairs", ("z", "x"))

    return jax.shard_map(
        local,
        mesh=finer,
        in_specs=(P(("pairs", "z", "x"), None, None, None), P(), P(), P()),
        out_specs=(placed, placed),
        check_vma=False,
    )
```

```python
from functools import partial

import jax
import jax.numpy as jnp
from jax import lax
from jax.experimental import pallas as pl
from jax.experimental.pallas import tpu as pltpu
from jax.sharding import Mesh, PartitionSpec as P


MAXB = 5
LA = 4
LR = 16
MAXA = 8
FILTER_R = 3
LANES = 128
STRIPES = 4
GRANT = 16 << 20
WHOLE_GRANT = 60 << 20
damping = 0.5


def vmem():
    return pl.BlockSpec(memory_space=pltpu.VMEM)


def tap(k):
    sigma = FILTER_R / 2.0
    return jnp.exp(-jnp.float32(k * k) / jnp.float32(2.0 * sigma * sigma))


def resample_kernel(first, parts, info, az, rg, img, *rest):
    rest = rest[-4 - parts :]
    keep, sends = rest[0], rest[1 : 1 + parts]
    tiles_of, spread, shifted = rest[1 + parts :]
    lines, full = img.shape[2], img.shape[3]
    tiles = full // LANES
    groups = tiles // (2 * STRIPES)
    blocks = lines // (8 * LA)
    high = lines + 2 * MAXA
    span = STRIPES * LANES
    date = info[1] + first + pl.program_id(0)
    x = info[0]
    shift = rg[date]
    step = az[date]
    behind = shift < 0
    origin = jnp.where(behind, -1, 0)
    amount = shift - origin * LANES
    turn = lax.rem(LANES - amount, LANES)
    lane = lax.broadcasted_iota(jnp.int32, (lines, LANES), 1)
    own = lane + amount < LANES

    @pl.when(pl.program_id(0) == 0)
    def _():
        blank = jnp.zeros((MAXA, LANES), jnp.float32)
        for t in range(shifted.shape[0] // high):
            shifted[pl.ds(t * high, MAXA), :] = blank
            shifted[pl.ds(t * high + MAXA + lines, MAXA), :] = blank
        source = lax.broadcasted_iota(jnp.int32, (span, span), 0)
        target = lax.broadcasted_iota(jnp.int32, (1, span), 1)
        column, few = target & 7, (target >> 3) & 3
        stripe, many = (target >> 5) & 3, target >> 7
        wanted = stripe * LANES + column * LR + many * 4 + few
        spread[...] = jnp.where(source == wanted, 1.0, 0.0).astype(jnp.bfloat16)

    for c in range(2):

        def turned(t):
            place = jnp.clip(t + origin, 0, tiles - 1)
            tile = img[0, c, :, pl.ds(pl.multiple_of(place * LANES, LANES), LANES)]
            out = pltpu.roll(tile.astype(jnp.float32), turn, 1)
            if t == 0:
                out = jnp.where(behind, 0.0, out)
            if t == tiles:
                out = jnp.where(behind, out, 0.0)
            return out

        here = turned(0)
        for t in range(tiles):
            after = turned(t + 1)
            group, stripe, parity = t // 2 // STRIPES, t // 2 % STRIPES, t % 2
            tiles_of[
                group, pl.ds((c * 2 + parity) * lines, lines), pl.ds(stripe * LANES, LANES)
            ] = jnp.where(own, here, after).astype(jnp.bfloat16)
            here = after

    def slab(c, parity, group, many):
        return (((c * 2 + parity) * groups + group) * 4 + many) * high + MAXA

    for group in range(groups):
        for half in range(2):
            result = jnp.dot(
                tiles_of[group],
                spread[:, half * span // 2 : (half + 1) * span // 2],
                preferred_element_type=jnp.float32,
            )
            for c in range(2):
                for parity in range(2):
                    for k in range(2):
                        at = (c * 2 + parity) * lines
                        shifted[pl.ds(slab(c, parity, group, 2 * half + k), lines), :] = result[
                            at : at + lines, k * LANES : (k + 1) * LANES
                        ]

    def put(out, place, block, c, group, parity):
        for look in range(LA):
            for pair in range(2):
                both = [
                    shifted[
                        pl.ds(
                            slab(c, parity, group, 2 * pair + k) + step + 8 * LA * block + look,
                            8,
                            stride=LA,
                        ),
                        :,
                    ]
                    for k in range(2)
                ]
                out[0, c, place, group, pl.ds(32 * look + 16 * pair, 16), :] = jnp.concatenate(
                    both, 0
                ).astype(jnp.bfloat16)

    width = blocks // parts
    for c in range(2):
        for block in range(blocks):
            for group in range(groups):
                put(sends[block // width], block % width, block, c, group, 1 - x)
                put(keep, block, block, c, group, x)


def resample(images, az, rg, info, first, count, parts, earlier):
    lines, full = images.shape[2], images.shape[3]
    tiles = full // LANES
    groups = tiles // (2 * STRIPES)
    blocks = lines // (8 * LA)
    rows = 8 * LA * 4

    def block(width):
        return pl.BlockSpec(
            (1, 2, width, groups, rows, LANES), lambda i, *_: (i, 0, 0, 0, 0, 0)
        )

    def shape(width):
        return jax.ShapeDtypeStruct((count, 2, width, groups, rows, LANES), jnp.bfloat16)

    widths = [blocks] + [blocks // parts] * parts
    return pl.pallas_call(
        partial(resample_kernel, first, parts),
        grid_spec=pltpu.PrefetchScalarGridSpec(
            num_scalar_prefetch=3,
            grid=(count,),
            in_specs=[pl.BlockSpec((1, 2, lines, full), lambda i, *_: (i + first, 0, 0, 0))]
            + [pl.BlockSpec(memory_space=pl.ANY)] * len(earlier),
            out_specs=[block(w) for w in widths],
            scratch_shapes=[
                pltpu.VMEM((groups, 4 * lines, STRIPES * LANES), jnp.bfloat16),
                pltpu.VMEM((STRIPES * LANES, STRIPES * LANES), jnp.bfloat16),
                pltpu.VMEM((16 * groups * (lines + 2 * MAXA), LANES), jnp.float32),
            ],
        ),
        out_shape=[shape(w) for w in widths],
        compiler_params=pltpu.CompilerParams(vmem_limit_bytes=WHOLE_GRANT),
        cost_estimate=pl.CostEstimate(
            flops=count * lines * full * 4,
            transcendentals=0,
            bytes_accessed=count * lines * full * 8,
        ),
    )(info, az, rg, images, *earlier)


def merge(x, y, bit, distance):
    return jnp.where(
        bit, x + pltpu.roll(x, LANES - distance, 1), y + pltpu.roll(y, distance, 1)
    )


def pair_kernel(own, starts, reached, info, mask, *refs):
    count = len(starts)
    parts, following = refs[: 2 * count], refs[2 * count : 2 * count + len(reached)]
    right, images, products, sums = refs[-4:]
    block = 2 * own
    x = info[0]
    mine, other = x * own, (1 - x) * own
    for s, start in enumerate(starts):
        for where, ref in ((mine, parts[2 * s]), (other, parts[2 * s + 1])):
            for i in range(ref.shape[0]):
                images[where + start + i] = ref[i, :, 0, 0].astype(jnp.float32)
    for start, ref in zip(reached, following):
        for i in range(ref.shape[0]):
            images[block + start + i] = ref[i, :, 0, 0].astype(jnp.float32)
    sums[...] = jnp.zeros_like(sums)

    def multiply(d, carry):
        totals = [[None] * 2 for _ in range(MAXB)]
        for k in range(images.shape[2] // 8):
            at = pl.ds(8 * k, 8)
            a, b = images[d, 0, at, :], images[d, 1, at, :]
            for g in range(MAXB):
                c, e = images[d + g + 1, 0, at, :], images[d + g + 1, 1, at, :]
                terms = (a * c + b * e, b * c - a * e)
                for comp, term in enumerate(terms):
                    old = totals[g][comp]
                    totals[g][comp] = term if old is None else old + term
        for g in range(MAXB):
            for comp in range(2):
                at = ((d * MAXB + g) * 2 + comp) * 8
                products[pl.ds(pl.multiple_of(at, 8), 8), :] = totals[g][comp]
        return carry

    lax.fori_loop(0, block, multiply, 0)
    lane = lax.broadcasted_iota(jnp.int32, (8, LANES), 1)
    real = lane & 8 == 0
    place = lane >> 4

    def slot(d, g):
        at = (d * MAXB + g) * 16
        value = merge(
            products[pl.ds(pl.multiple_of(at, 8), 8), :],
            products[pl.ds(pl.multiple_of(at + 8, 8), 8), :],
            real,
            8,
        )
        value = value + pltpu.roll(value, LANES - 16, 1)
        value = (value * (1.0 / (LA * LR))).astype(jnp.bfloat16).astype(jnp.float32)
        return value * mask[g, info[2] + d].astype(jnp.float32)

    step = 4 if block % 4 == 0 else 1

    def gather(i, carry):
        totals = [None] * (step + MAXB)

        def add(at, value):
            totals[at] = value if totals[at] is None else totals[at] + value

        for j in range(step):
            for g in range(MAXB):
                value = slot(i * step + j, g)
                add(j, value)
                add(j + g + 1, -value)
        for j, value in enumerate(totals):
            at = pl.ds(pl.multiple_of(8 * (i * step + j), 8), 8)
            sums[at, :] = sums[at, :] + value
        return carry

    lax.fori_loop(0, block // step, gather, 0)
    for group in range(right.shape[2] // 8):
        rows = [sums[pl.ds(64 * group + u, 8, stride=8), :] for u in range(8)]
        turned = []
        for s in range(8):
            joined = rows[s]
            for z in range(1, STRIPES):
                joined = jnp.where(place == 2 * z, rows[(s + 2 * z) % 8], joined)
            turned.append(pltpu.roll(joined, 16 * s, 1) if s else joined)
        for z in range(STRIPES):
            out = turned[0]
            for s in range(1, 8):
                out = jnp.where(place == (2 * z + s) % 8, turned[s], out)
            right[right.shape[0] - 1, z, pl.ds(8 * group, 8), :] = out
    if right.shape[0] > 1:
        right[0] = refs[-5][0]


def pair_sums(info, mask, pieces, following, earlier, chunk, chunks, own, deep):
    groups, lines = pieces[0][1].shape[3:5]

    def window(array, parts):
        offset = chunk % (chunks // parts)
        return pl.BlockSpec(
            (array.shape[0], 2, 1, 1, lines, LANES), lambda i, *_: (0, 0, offset, i, 0, 0)
        )

    operands, specs = [], []
    for _, keep, received in pieces:
        got = received[chunk * len(received) // chunks]
        operands += [keep, got]
        specs += [window(keep, 1), window(got, len(received))]
    for _, received in following:
        got = received[chunk * len(received) // chunks]
        operands.append(got)
        specs.append(window(got, len(received)))
    joined = chunk == 1
    if earlier is not None:
        operands.append(earlier)
        specs.append(
            pl.BlockSpec((1, STRIPES, deep, LANES), lambda i, *_: (0, i, 0, 0))
            if joined
            else pl.BlockSpec(memory_space=pl.ANY)
        )
    work = 2 * own * MAXB * lines * LANES * groups
    return pl.pallas_call(
        partial(pair_kernel, own, [p[0] for p in pieces], [f[0] for f in following]),
        grid_spec=pltpu.PrefetchScalarGridSpec(
            num_scalar_prefetch=2,
            grid=(groups,),
            in_specs=specs,
            out_specs=pl.BlockSpec((1 + joined, STRIPES, deep, LANES), lambda i, *_: (0, i, 0, 0)),
            scratch_shapes=[
                pltpu.VMEM((2 * own + MAXB, 2, lines, LANES), jnp.float32),
                pltpu.VMEM((2 * own * MAXB * 16, LANES), jnp.float32),
                pltpu.VMEM((8 * deep, LANES), jnp.float32),
            ],
        ),
        out_shape=jax.ShapeDtypeStruct((1 + joined, groups * STRIPES, deep, LANES), jnp.float32),
        compiler_params=pltpu.CompilerParams(vmem_limit_bytes=GRANT),
        cost_estimate=pl.CostEstimate(flops=work * 8, transcendentals=0, bytes_accessed=work),
    )(info, mask, *operands)


def filter_kernel(count, info, *rest):
    weight, out, along = rest[2 * count :]
    own, partner = (
        [ref.at[i] for ref in refs for i in range(ref.shape[0])]
        for refs in (rest[:count], rest[count : 2 * count])
    )
    rows = len(own)
    tiles, deep = own[0].shape[:2]
    x = info[0]
    blank = jnp.zeros((rows, deep, LANES), jnp.float32)
    along[0] = blank
    along[2 * tiles + 1] = blank
    lane = lax.broadcasted_iota(jnp.int32, (deep, LANES), 1)
    place = lane & 7
    taps = [tap(k) for k in range(FILTER_R + 1)]

    def turn(v, k):
        return pltpu.roll(v, k % LANES, 1)

    for refs, side in ((partner, 1 - x), (own, x)):
        for i in range(tiles):
            values = [ref[i] for ref in refs]
            for r in range(rows):
                acc = values[r]
                for k in range(1, FILTER_R + 1):
                    reach = 16 * k
                    last = values[r - 1] if r > 0 else jnp.zeros_like(acc)
                    later = values[r + 1] if r + 1 < rows else jnp.zeros_like(acc)
                    up = turn(jnp.where(lane >= reach, values[r], later), -reach)
                    down = turn(jnp.where(lane < LANES - reach, values[r], last), reach)
                    acc = acc + taps[k] * (up + down)
                along[2 * i + side + 1, r] = acc

    for i in range(tiles):
        at = 2 * i + x + 1
        for r in range(rows):
            v, left, right = along[at, r], along[at - 1, r], along[at + 1, r]
            acc = v
            for k in range(1, FILTER_R + 1):
                near = jnp.where(place < 8 - k, turn(v, -k), turn(right, 8 - k)) + jnp.where(
                    place >= k, turn(v, k), turn(left, k - 8)
                )
                acc = acc + taps[k] * near
            out[r, i, 0] = own[r][i]
            out[r, i, 1] = acc * weight[i, r : r + 1, :]


def filtered(info, own, partner, weight):
    count = len(own)
    rows = sum(v.shape[0] for v in own)
    tiles, deep = own[0].shape[1:3]
    smem = pl.BlockSpec(memory_space=pltpu.SMEM)
    return pl.pallas_call(
        partial(filter_kernel, count),
        in_specs=[smem] + [vmem()] * (2 * count + 1),
        out_specs=vmem(),
        out_shape=jax.ShapeDtypeStruct((rows, tiles, 2, deep, LANES), jnp.float32),
        scratch_shapes=[pltpu.VMEM((2 * tiles + 2, rows, deep, LANES), jnp.float32)],
        name="smooth",
        compiler_params=pltpu.CompilerParams(vmem_limit_bytes=GRANT),
    )(info, *own, *partner, weight)


def edge_weights(positions, whole):
    total = jnp.zeros(positions.shape, jnp.float32)
    for k in range(-FILTER_R, FILTER_R + 1):
        at = positions + k
        total = total + jnp.where((at >= 0) & (at < whole), tap(k), 0.0)
    return total


def invert_kernel(normal, out):
    size = normal.shape[0]
    low, high = damping, damping + 4.0 * MAXB
    middle, spread = high + low, high - low
    peak = 2.0 * (middle / spread) ** 2 - 1.0
    row = lax.broadcasted_iota(jnp.int32, (size, size), 0)
    col = lax.broadcasted_iota(jnp.int32, (size, size), 1)
    unit = jnp.where(row == col, 1.0, 0.0).astype(jnp.float32)
    n = normal[...]
    guess = (8.0 * middle / spread**2 / peak) * unit - (8.0 / spread**2 / peak) * n
    whole = n.astype(jnp.bfloat16)

    def times_normal(value):
        total = None
        for _ in range(3):
            part = value.astype(jnp.bfloat16)
            value = value - part.astype(jnp.float32)
            term = jnp.dot(whole, part, preferred_element_type=jnp.float32)
            total = term if total is None else total + term
        return total

    error = 1.0 / peak
    while error > 1e-8:
        scale = 2.0 / (2.0 - error * error)
        residual = unit - times_normal(guess)
        precision = lax.Precision.HIGHEST if error < 0.1 else lax.Precision.DEFAULT
        change = jnp.dot(guess, residual, precision=precision, preferred_element_type=jnp.float32)
        guess = scale * (guess + change)
        error = error * error / (2.0 - error * error)
    out[...] = guess


def invert(normal):
    size = normal.shape[0]
    return pl.pallas_call(
        invert_kernel,
        in_specs=[vmem()],
        out_specs=vmem(),
        out_shape=jax.ShapeDtypeStruct((size, size), jnp.float32),
        name="invert",
        compiler_params=pltpu.CompilerParams(vmem_limit_bytes=GRANT),
        cost_estimate=pl.CostEstimate(
            flops=120 * size**3, transcendentals=0, bytes_accessed=8 * size * size
        ),
    )(normal)


def series_kernel(block, got, inverse, screen, motion, right):
    sources, _, deep = got.shape[:3]
    right[...] = jnp.zeros_like(right)
    for part in range(2):
        lanes = pl.ds(part * LANES, LANES)
        for s in range(sources):
            at = pl.ds(s * block, deep)
            right[at, lanes] = right[at, lanes] + got[s, part]
    result = jnp.dot(
        right[: inverse.shape[0], :].T,
        inverse[...],
        precision=lax.Precision.HIGHEST,
        preferred_element_type=jnp.float32,
    )
    for u in range(8):
        for comp in range(2):
            at = u * 16 + comp * 8
            first, second = result[at : at + 8], result[LANES + at : LANES + at + 8]
            screen[comp, u] = second
            motion[comp, u] = first - second


def invert_pixels(got, inverse, block):
    dates = inverse.shape[0]
    shape = jax.ShapeDtypeStruct((2, 8, 8, dates), jnp.float32)
    return pl.pallas_call(
        partial(series_kernel, block),
        in_specs=[vmem(), vmem()],
        out_specs=[vmem(), vmem()],
        out_shape=[shape, shape],
        scratch_shapes=[pltpu.VMEM((dates + got.shape[2] - block, 2 * LANES), jnp.float32)],
        name="series",
        compiler_params=pltpu.CompilerParams(vmem_limit_bytes=GRANT),
    )(got, inverse)


def local(images, az, rg, pair_list):
    own, _, lines, full = images.shape
    dates = az.shape[0]
    groups, along, _ = (lax.axis_size(name) for name in ("pairs", "z", "x"))
    blocks = groups * along
    block = 2 * own
    deep = -(-(block + MAXB) // 8) * 8
    rows = groups
    if full != 2 * along * LANES or along % STRIPES or lines != rows * 8 * LA:
        raise ValueError("unsupported shape")
    x = lax.axis_index("x")
    place = lax.axis_index(("pairs", "z"))
    info = jnp.stack([x, (2 * place + x) * own, place * block]).astype(jnp.int32)

    date_ids = jnp.arange(dates, dtype=jnp.int32)
    is_reference = date_ids[:, None] == pair_list[None, :, 0]
    is_secondary = date_ids[:, None] == pair_list[None, :, 1]
    design = (is_reference.astype(jnp.float32) - is_secondary.astype(jnp.float32)).astype(
        jnp.bfloat16
    )
    normal = jnp.dot(design, design.T, preferred_element_type=jnp.float32)
    normal = normal + damping * jnp.eye(dates, dtype=jnp.float32)
    gaps = pair_list[:, 1] - pair_list[:, 0]
    is_gap = jnp.arange(1, MAXB + 1, dtype=jnp.int32)[:, None] == gaps[None, :]
    mask = jnp.dot(
        is_gap.astype(jnp.bfloat16),
        is_reference.astype(jnp.bfloat16).T,
        preferred_element_type=jnp.float32,
    )
    mask = mask.astype(jnp.int32)
    inverse = invert(normal)

    swap = [(0, 1), (1, 0)]
    cuts = [0, own] if own <= MAXB else [0, 2, MAXB, own]
    pieces, following = [], []
    left, turn, leaving = x == 0, 0, None

    def send_back(start, keep, received, left, inverse):
        hops = []
        for c, other in enumerate(received):
            part = other.shape[2]
            mine = lax.slice_in_dim(keep, c * part, (c + 1) * part, axis=2)
            lower, upper = mine, other
            if own < MAXB:
                lower = jnp.concatenate([mine, other], 0)[:MAXB]
                upper = jnp.concatenate([other, mine], 0)[:MAXB]
            hops.append(jnp.where(left, lower, upper))
            if own > MAXB:
                left, hops[-1], inverse = lax.optimization_barrier((left, hops[-1], inverse))
        if own < MAXB:
            for hop in range(1, -(-MAXB // block) + 1):
                route = [(i + hop, i) for i in range(blocks - hop)]
                count = min(block, MAXB - (hop - 1) * block)
                going = [lax.ppermute(v[:count], ("pairs", "z"), route) for v in hops]
                following.append(((hop - 1) * block, going))
        else:
            route = [(i + 1, i) for i in range(blocks - 1)]
            going = []
            for v in hops:
                going.append(lax.ppermute(v, ("pairs", "z"), route))
            following.append((start, going))
        return hops[0], left, inverse

    for k, (start, end) in enumerate(zip(cuts, cuts[1:])):
        after = [p[1] for p in pieces[-1:]] + [v for v in (leaving,) if v is not None]
        keep, *sends = resample(
            images, az, rg, info, start, end - start, min(rows, 2**k), after
        )
        received = []
        for v in sends:
            received.append(lax.ppermute(v, "x", swap))
            turn += 1
        pieces.append((start, keep, received))
        if k > 0:
            if k == len(cuts) - 2:
                left, _ = lax.optimization_barrier((left, keep))
            leaving, left, inverse = send_back(*pieces[k - 1], left, inverse)
    if cuts[-2] < MAXB:
        send_back(*pieces[-1], left, inverse)

    sums = []
    for c in range(rows):
        earlier = sums[-1] if sums else None
        sums.append(pair_sums(info, mask, pieces, following, earlier, c, rows, own, deep))
    sums = sums[1:]
    partner = [lax.ppermute(s, "x", swap) for s in sums]

    lane = jnp.arange(LANES, dtype=jnp.int32)
    row_at = jnp.arange(rows, dtype=jnp.int32)[:, None] * 8 + (lane // 16)[None, :]
    stripe = 2 * jnp.arange(along, dtype=jnp.int32) + x
    col_at = stripe[:, None] * 8 + (lane & 7)[None, :]
    row_weight = edge_weights(row_at, lines // LA)
    col_weight = edge_weights(col_at, full // LR)
    weight = 1.0 / (row_weight[None, :, :] * col_weight[:, None, :])

    outgoing = filtered(info, sums, partner, weight)
    outgoing = outgoing.reshape((rows * along,) + outgoing.shape[2:])
    got = lax.all_to_all(outgoing, ("pairs", "z"), split_axis=0, concat_axis=0, tiled=True)
    screen, motion = invert_pixels(got, inverse, block)
    return tuple(jnp.transpose(v, (3, 0, 1, 2)) for v in (screen, motion))


def solution(mesh):
    shape = (mesh.shape["pairs"], mesh.shape["stripe"] // 2, 2)
    if isinstance(mesh, Mesh):
        finer = Mesh(mesh.devices.reshape(shape), ("pairs", "z", "x"))
    else:
        finer = jax.sharding.AbstractMesh(shape, ("pairs", "z", "x"))
    placed = P(None, None, "pairs", ("z", "x"))

    return jax.shard_map(
        local,
        mesh=finer,
        in_specs=(P(("pairs", "z", "x"), None, None, None), P(), P(), P()),
        out_specs=(placed, placed),
        check_vma=False,
    )
```

```python
from functools import partial

import jax
import jax.numpy as jnp
from jax import lax
from jax.experimental import pallas as pl
from jax.experimental.pallas import tpu as pltpu
from jax.sharding import Mesh, PartitionSpec as P


MAXB = 5
LA = 4
LR = 16
MAXA = 8
FILTER_R = 3
LANES = 128
STRIPES = 4
GRANT = 16 << 20
WHOLE_GRANT = 60 << 20
damping = 0.5


def vmem():
    return pl.BlockSpec(memory_space=pltpu.VMEM)


def tap(k):
    sigma = FILTER_R / 2.0
    return jnp.exp(-jnp.float32(k * k) / jnp.float32(2.0 * sigma * sigma))


def resample_kernel(first, parts, info, az, rg, img, *rest):
    rest = rest[-4 - parts :]
    keep, sends = rest[0], rest[1 : 1 + parts]
    tiles_of, spread, shifted = rest[1 + parts :]
    lines, full = img.shape[2], img.shape[3]
    tiles = full // LANES
    groups = tiles // (2 * STRIPES)
    blocks = lines // (8 * LA)
    high = lines + 2 * MAXA
    span = STRIPES * LANES
    date = info[1] + first + pl.program_id(0)
    x = info[0]
    shift = rg[date]
    step = az[date]
    behind = shift < 0
    origin = jnp.where(behind, -1, 0)
    amount = shift - origin * LANES
    turn = lax.rem(LANES - amount, LANES)
    lane = lax.broadcasted_iota(jnp.int32, (lines, LANES), 1)
    own = lane + amount < LANES

    @pl.when(pl.program_id(0) == 0)
    def _():
        blank = jnp.zeros((MAXA, LANES), jnp.float32)
        for t in range(shifted.shape[0] // high):
            shifted[pl.ds(t * high, MAXA), :] = blank
            shifted[pl.ds(t * high + MAXA + lines, MAXA), :] = blank
        source = lax.broadcasted_iota(jnp.int32, (span, span), 0)
        target = lax.broadcasted_iota(jnp.int32, (1, span), 1)
        column, few = target & 7, (target >> 3) & 3
        stripe, many = (target >> 5) & 3, target >> 7
        wanted = stripe * LANES + column * LR + many * 4 + few
        spread[...] = jnp.where(source == wanted, 1.0, 0.0).astype(jnp.bfloat16)

    for c in range(2):

        def turned(t):
            place = jnp.clip(t + origin, 0, tiles - 1)
            tile = img[0, c, :, pl.ds(pl.multiple_of(place * LANES, LANES), LANES)]
            out = pltpu.roll(tile.astype(jnp.float32), turn, 1)
            if t == 0:
                out = jnp.where(behind, 0.0, out)
            if t == tiles:
                out = jnp.where(behind, out, 0.0)
            return out

        here = turned(0)
        for t in range(tiles):
            after = turned(t + 1)
            group, stripe, parity = t // 2 // STRIPES, t // 2 % STRIPES, t % 2
            tiles_of[
                group, pl.ds((c * 2 + parity) * lines, lines), pl.ds(stripe * LANES, LANES)
            ] = jnp.where(own, here, after).astype(jnp.bfloat16)
            here = after

    def slab(c, parity, group, many):
        return (((c * 2 + parity) * groups + group) * 4 + many) * high + MAXA

    for group in range(groups):
        for half in range(2):
            result = jnp.dot(
                tiles_of[group],
                spread[:, half * span // 2 : (half + 1) * span // 2],
                preferred_element_type=jnp.float32,
            )
            for c in range(2):
                for parity in range(2):
                    for k in range(2):
                        at = (c * 2 + parity) * lines
                        shifted[pl.ds(slab(c, parity, group, 2 * half + k), lines), :] = result[
                            at : at + lines, k * LANES : (k + 1) * LANES
                        ]

    def put(out, place, block, c, group, parity):
        for look in range(LA):
            for pair in range(2):
                both = [
                    shifted[
                        pl.ds(
                            slab(c, parity, group, 2 * pair + k) + step + 8 * LA * block + look,
                            8,
                            stride=LA,
                        ),
                        :,
                    ]
                    for k in range(2)
                ]
                out[0, c, place, group, pl.ds(32 * look + 16 * pair, 16), :] = jnp.concatenate(
                    both, 0
                ).astype(jnp.bfloat16)

    width = blocks // parts
    for c in range(2):
        for block in range(blocks):
            for group in range(groups):
                put(sends[block // width], block % width, block, c, group, 1 - x)
                put(keep, block, block, c, group, x)


def resample(images, az, rg, info, first, count, parts, earlier):
    lines, full = images.shape[2], images.shape[3]
    tiles = full // LANES
    groups = tiles // (2 * STRIPES)
    blocks = lines // (8 * LA)
    rows = 8 * LA * 4

    def block(width):
        return pl.BlockSpec(
            (1, 2, width, groups, rows, LANES), lambda i, *_: (i, 0, 0, 0, 0, 0)
        )

    def shape(width):
        return jax.ShapeDtypeStruct((count, 2, width, groups, rows, LANES), jnp.bfloat16)

    widths = [blocks] + [blocks // parts] * parts
    return pl.pallas_call(
        partial(resample_kernel, first, parts),
        grid_spec=pltpu.PrefetchScalarGridSpec(
            num_scalar_prefetch=3,
            grid=(count,),
            in_specs=[pl.BlockSpec((1, 2, lines, full), lambda i, *_: (i + first, 0, 0, 0))]
            + [pl.BlockSpec(memory_space=pl.ANY)] * len(earlier),
            out_specs=[block(w) for w in widths],
            scratch_shapes=[
                pltpu.VMEM((groups, 4 * lines, STRIPES * LANES), jnp.bfloat16),
                pltpu.VMEM((STRIPES * LANES, STRIPES * LANES), jnp.bfloat16),
                pltpu.VMEM((16 * groups * (lines + 2 * MAXA), LANES), jnp.float32),
            ],
        ),
        out_shape=[shape(w) for w in widths],
        compiler_params=pltpu.CompilerParams(vmem_limit_bytes=WHOLE_GRANT),
        cost_estimate=pl.CostEstimate(
            flops=count * lines * full * 4,
            transcendentals=0,
            bytes_accessed=count * lines * full * 8,
        ),
    )(info, az, rg, images, *earlier)


def merge(x, y, bit, distance):
    return jnp.where(
        bit, x + pltpu.roll(x, LANES - distance, 1), y + pltpu.roll(y, distance, 1)
    )


def pair_kernel(own, starts, reached, info, mask, *refs):
    count = len(starts)
    parts, following = refs[: 2 * count], refs[2 * count : 2 * count + len(reached)]
    right, images, products, sums = refs[-4:]
    block = 2 * own
    x = info[0]
    mine, other = x * own, (1 - x) * own
    for s, start in enumerate(starts):
        for where, ref in ((mine, parts[2 * s]), (other, parts[2 * s + 1])):
            for i in range(ref.shape[0]):
                images[where + start + i] = ref[i, :, 0, 0].astype(jnp.float32)
    for start, ref in zip(reached, following):
        for i in range(ref.shape[0]):
            images[block + start + i] = ref[i, :, 0, 0].astype(jnp.float32)
    sums[...] = jnp.zeros_like(sums)

    def multiply(d, carry):
        totals = [[None] * 2 for _ in range(MAXB)]
        for k in range(images.shape[2] // 8):
            at = pl.ds(8 * k, 8)
            a, b = images[d, 0, at, :], images[d, 1, at, :]
            for g in range(MAXB):
                c, e = images[d + g + 1, 0, at, :], images[d + g + 1, 1, at, :]
                terms = (a * c + b * e, b * c - a * e)
                for comp, term in enumerate(terms):
                    old = totals[g][comp]
                    totals[g][comp] = term if old is None else old + term
        for g in range(MAXB):
            for comp in range(2):
                at = ((d * MAXB + g) * 2 + comp) * 8
                products[pl.ds(pl.multiple_of(at, 8), 8), :] = totals[g][comp]
        return carry

    lax.fori_loop(0, block, multiply, 0)
    lane = lax.broadcasted_iota(jnp.int32, (8, LANES), 1)
    real = lane & 8 == 0
    place = lane >> 4

    def slot(d, g):
        at = (d * MAXB + g) * 16
        value = merge(
            products[pl.ds(pl.multiple_of(at, 8), 8), :],
            products[pl.ds(pl.multiple_of(at + 8, 8), 8), :],
            real,
            8,
        )
        value = value + pltpu.roll(value, LANES - 16, 1)
        value = (value * (1.0 / (LA * LR))).astype(jnp.bfloat16).astype(jnp.float32)
        return value * mask[g, info[2] + d].astype(jnp.float32)

    step = 4 if block % 4 == 0 else 1

    def gather(i, carry):
        totals = [None] * (step + MAXB)

        def add(at, value):
            totals[at] = value if totals[at] is None else totals[at] + value

        for j in range(step):
            for g in range(MAXB):
                value = slot(i * step + j, g)
                add(j, value)
                add(j + g + 1, -value)
        for j, value in enumerate(totals):
            at = pl.ds(pl.multiple_of(8 * (i * step + j), 8), 8)
            sums[at, :] = sums[at, :] + value
        return carry

    lax.fori_loop(0, block // step, gather, 0)
    for group in range(right.shape[2] // 8):
        rows = [sums[pl.ds(64 * group + u, 8, stride=8), :] for u in range(8)]
        turned = []
        for s in range(8):
            joined = rows[s]
            for z in range(1, STRIPES):
                joined = jnp.where(place == 2 * z, rows[(s + 2 * z) % 8], joined)
            turned.append(pltpu.roll(joined, 16 * s, 1) if s else joined)
        for z in range(STRIPES):
            out = turned[0]
            for s in range(1, 8):
                out = jnp.where(place == (2 * z + s) % 8, turned[s], out)
            right[right.shape[0] - 1, z, pl.ds(8 * group, 8), :] = out
    if right.shape[0] > 1:
        right[0] = refs[-5][0]


def pair_sums(info, mask, pieces, following, earlier, chunk, chunks, own, deep):
    groups, lines = pieces[0][1].shape[3:5]

    def window(array, parts):
        offset = chunk % (chunks // parts)
        return pl.BlockSpec(
            (array.shape[0], 2, 1, 1, lines, LANES), lambda i, *_: (0, 0, offset, i, 0, 0)
        )

    operands, specs = [], []
    for _, keep, received in pieces:
        got = received[chunk * len(received) // chunks]
        operands += [keep, got]
        specs += [window(keep, 1), window(got, len(received))]
    for _, received in following:
        got = received[chunk * len(received) // chunks]
        operands.append(got)
        specs.append(window(got, len(received)))
    joined = chunk == 1
    if earlier is not None:
        operands.append(earlier)
        specs.append(
            pl.BlockSpec((1, STRIPES, deep, LANES), lambda i, *_: (0, i, 0, 0))
            if joined
            else pl.BlockSpec(memory_space=pl.ANY)
        )
    work = 2 * own * MAXB * lines * LANES * groups
    return pl.pallas_call(
        partial(pair_kernel, own, [p[0] for p in pieces], [f[0] for f in following]),
        grid_spec=pltpu.PrefetchScalarGridSpec(
            num_scalar_prefetch=2,
            grid=(groups,),
            in_specs=specs,
            out_specs=pl.BlockSpec((1 + joined, STRIPES, deep, LANES), lambda i, *_: (0, i, 0, 0)),
            scratch_shapes=[
                pltpu.VMEM((2 * own + MAXB, 2, lines, LANES), jnp.float32),
                pltpu.VMEM((2 * own * MAXB * 16, LANES), jnp.float32),
                pltpu.VMEM((8 * deep, LANES), jnp.float32),
            ],
        ),
        out_shape=jax.ShapeDtypeStruct((1 + joined, groups * STRIPES, deep, LANES), jnp.float32),
        compiler_params=pltpu.CompilerParams(vmem_limit_bytes=GRANT),
        cost_estimate=pl.CostEstimate(flops=work * 8, transcendentals=0, bytes_accessed=work),
    )(info, mask, *operands)


def filter_kernel(count, info, *rest):
    weight, out, along = rest[2 * count :]
    own, partner = (
        [ref.at[i] for ref in refs for i in range(ref.shape[0])]
        for refs in (rest[:count], rest[count : 2 * count])
    )
    rows = len(own)
    tiles, deep = own[0].shape[:2]
    x = info[0]
    blank = jnp.zeros((rows, deep, LANES), jnp.float32)
    along[0] = blank
    along[2 * tiles + 1] = blank
    lane = lax.broadcasted_iota(jnp.int32, (deep, LANES), 1)
    place = lane & 7
    taps = [tap(k) for k in range(FILTER_R + 1)]

    def turn(v, k):
        return pltpu.roll(v, k % LANES, 1)

    for refs, side in ((partner, 1 - x), (own, x)):
        for i in range(tiles):
            values = [ref[i] for ref in refs]
            for r in range(rows):
                acc = values[r]
                for k in range(1, FILTER_R + 1):
                    reach = 16 * k
                    last = values[r - 1] if r > 0 else jnp.zeros_like(acc)
                    later = values[r + 1] if r + 1 < rows else jnp.zeros_like(acc)
                    up = turn(jnp.where(lane >= reach, values[r], later), -reach)
                    down = turn(jnp.where(lane < LANES - reach, values[r], last), reach)
                    acc = acc + taps[k] * (up + down)
                along[2 * i + side + 1, r] = acc

    for i in range(tiles):
        at = 2 * i + x + 1
        for r in range(rows):
            v, left, right = along[at, r], along[at - 1, r], along[at + 1, r]
            acc = v
            for k in range(1, FILTER_R + 1):
                near = jnp.where(place < 8 - k, turn(v, -k), turn(right, 8 - k)) + jnp.where(
                    place >= k, turn(v, k), turn(left, k - 8)
                )
                acc = acc + taps[k] * near
            out[r, i, 0] = own[r][i]
            out[r, i, 1] = acc * weight[i, r : r + 1, :]


def filtered(info, own, partner, weight):
    count = len(own)
    rows = sum(v.shape[0] for v in own)
    tiles, deep = own[0].shape[1:3]
    smem = pl.BlockSpec(memory_space=pltpu.SMEM)
    return pl.pallas_call(
        partial(filter_kernel, count),
        in_specs=[smem] + [vmem()] * (2 * count + 1),
        out_specs=vmem(),
        out_shape=jax.ShapeDtypeStruct((rows, tiles, 2, deep, LANES), jnp.float32),
        scratch_shapes=[pltpu.VMEM((2 * tiles + 2, rows, deep, LANES), jnp.float32)],
        name="smooth",
        compiler_params=pltpu.CompilerParams(vmem_limit_bytes=GRANT),
    )(info, *own, *partner, weight)


def edge_weights(positions, whole):
    total = jnp.zeros(positions.shape, jnp.float32)
    for k in range(-FILTER_R, FILTER_R + 1):
        at = positions + k
        total = total + jnp.where((at >= 0) & (at < whole), tap(k), 0.0)
    return total


def invert_kernel(normal, out):
    size = normal.shape[0]
    low, high = damping, damping + 4.0 * MAXB
    middle, spread = high + low, high - low
    peak = 2.0 * (middle / spread) ** 2 - 1.0
    row = lax.broadcasted_iota(jnp.int32, (size, size), 0)
    col = lax.broadcasted_iota(jnp.int32, (size, size), 1)
    unit = jnp.where(row == col, 1.0, 0.0).astype(jnp.float32)
    n = normal[...]
    guess = (8.0 * middle / spread**2 / peak) * unit - (8.0 / spread**2 / peak) * n
    whole = n.astype(jnp.bfloat16)

    def times_normal(value):
        total = None
        for _ in range(3):
            part = value.astype(jnp.bfloat16)
            value = value - part.astype(jnp.float32)
            term = jnp.dot(whole, part, preferred_element_type=jnp.float32)
            total = term if total is None else total + term
        return total

    error = 1.0 / peak
    while error > 1e-8:
        scale = 2.0 / (2.0 - error * error)
        residual = unit - times_normal(guess)
        precision = lax.Precision.HIGHEST if error < 0.1 else lax.Precision.DEFAULT
        change = jnp.dot(guess, residual, precision=precision, preferred_element_type=jnp.float32)
        guess = scale * (guess + change)
        error = error * error / (2.0 - error * error)
    out[...] = guess


def invert(normal):
    size = normal.shape[0]
    return pl.pallas_call(
        invert_kernel,
        in_specs=[vmem()],
        out_specs=vmem(),
        out_shape=jax.ShapeDtypeStruct((size, size), jnp.float32),
        name="invert",
        compiler_params=pltpu.CompilerParams(vmem_limit_bytes=GRANT),
        cost_estimate=pl.CostEstimate(
            flops=120 * size**3, transcendentals=0, bytes_accessed=8 * size * size
        ),
    )(normal)


def series_kernel(block, got, inverse, screen, motion, right):
    sources, _, deep = got.shape[:3]
    right[...] = jnp.zeros_like(right)
    for part in range(2):
        lanes = pl.ds(part * LANES, LANES)
        for s in range(sources):
            at = pl.ds(s * block, deep)
            right[at, lanes] = right[at, lanes] + got[s, part]
    result = jnp.dot(
        right[: inverse.shape[0], :].T,
        inverse[...],
        precision=lax.Precision.HIGHEST,
        preferred_element_type=jnp.float32,
    )
    for u in range(8):
        for comp in range(2):
            at = u * 16 + comp * 8
            first, second = result[at : at + 8], result[LANES + at : LANES + at + 8]
            screen[comp, u] = second
            motion[comp, u] = first - second


def invert_pixels(got, inverse, block):
    dates = inverse.shape[0]
    shape = jax.ShapeDtypeStruct((2, 8, 8, dates), jnp.float32)
    return pl.pallas_call(
        partial(series_kernel, block),
        in_specs=[vmem(), vmem()],
        out_specs=[vmem(), vmem()],
        out_shape=[shape, shape],
        scratch_shapes=[pltpu.VMEM((dates + got.shape[2] - block, 2 * LANES), jnp.float32)],
        name="series",
        compiler_params=pltpu.CompilerParams(vmem_limit_bytes=GRANT),
    )(got, inverse)


def local(images, az, rg, pair_list):
    own, _, lines, full = images.shape
    dates = az.shape[0]
    groups, along, _ = (lax.axis_size(name) for name in ("pairs", "z", "x"))
    blocks = groups * along
    block = 2 * own
    deep = -(-(block + MAXB) // 8) * 8
    rows = groups
    if full != 2 * along * LANES or along % STRIPES or lines != rows * 8 * LA:
        raise ValueError("unsupported shape")
    x = lax.axis_index("x")
    place = lax.axis_index(("pairs", "z"))
    info = jnp.stack([x, (2 * place + x) * own, place * block]).astype(jnp.int32)

    date_ids = jnp.arange(dates, dtype=jnp.int32)
    is_reference = date_ids[:, None] == pair_list[None, :, 0]
    is_secondary = date_ids[:, None] == pair_list[None, :, 1]
    design = (is_reference.astype(jnp.float32) - is_secondary.astype(jnp.float32)).astype(
        jnp.bfloat16
    )
    normal = jnp.dot(design, design.T, preferred_element_type=jnp.float32)
    normal = normal + damping * jnp.eye(dates, dtype=jnp.float32)
    gaps = pair_list[:, 1] - pair_list[:, 0]
    is_gap = jnp.arange(1, MAXB + 1, dtype=jnp.int32)[:, None] == gaps[None, :]
    mask = jnp.dot(
        is_gap.astype(jnp.bfloat16),
        is_reference.astype(jnp.bfloat16).T,
        preferred_element_type=jnp.float32,
    )
    mask = mask.astype(jnp.int32)
    inverse = invert(normal)

    swap = [(0, 1), (1, 0)]
    cuts, parts = [0, own], [1]
    if own > MAXB:
        cuts, parts = [0, 1, 2, MAXB, own], [1, 1, min(rows, 2), rows]
    pieces, following = [], []
    left, turn = x == 0, 0

    def send_back(start, keep, received, left):
        hops = []
        for c, other in enumerate(received):
            part = other.shape[2]
            mine = lax.slice_in_dim(keep, c * part, (c + 1) * part, axis=2)
            lower, upper = mine, other
            if own < MAXB:
                lower = jnp.concatenate([mine, other], 0)[:MAXB]
                upper = jnp.concatenate([other, mine], 0)[:MAXB]
            hops.append(jnp.where(left, lower, upper))
            if own > MAXB:
                left, hops[-1] = lax.optimization_barrier((left, hops[-1]))
        if own < MAXB:
            for hop in range(1, -(-MAXB // block) + 1):
                route = [(i + hop, i) for i in range(blocks - hop)]
                count = min(block, MAXB - (hop - 1) * block)
                going = [lax.ppermute(v[:count], ("pairs", "z"), route) for v in hops]
                following.append(((hop - 1) * block, going))
        else:
            route = [(i + 1, i) for i in range(blocks - 1)]
            going = []
            for v in hops:
                going.append(lax.ppermute(v, ("pairs", "z"), route))
            following.append((start, going))
        return left

    for start, end, count in zip(cuts, cuts[1:], parts):
        after = [p[1] for p in pieces[-1:]]
        keep, *sends = resample(images, az, rg, info, start, end - start, count, after)
        received = []
        for v in sends:
            received.append(lax.ppermute(v, "x", swap))
            turn += 1
        pieces.append((start, keep, received))
    for start, keep, received in pieces:
        if start < MAXB:
            left = send_back(start, keep, received, left)

    sums = []
    for c in range(rows):
        earlier = sums[-1] if sums else None
        sums.append(pair_sums(info, mask, pieces, following, earlier, c, rows, own, deep))
    sums = sums[1:]
    partner = [lax.ppermute(s, "x", swap) for s in sums]

    lane = jnp.arange(LANES, dtype=jnp.int32)
    row_at = jnp.arange(rows, dtype=jnp.int32)[:, None] * 8 + (lane // 16)[None, :]
    stripe = 2 * jnp.arange(along, dtype=jnp.int32) + x
    col_at = stripe[:, None] * 8 + (lane & 7)[None, :]
    row_weight = edge_weights(row_at, lines // LA)
    col_weight = edge_weights(col_at, full // LR)
    weight = 1.0 / (row_weight[None, :, :] * col_weight[:, None, :])

    outgoing = filtered(info, sums, partner, weight)
    outgoing = outgoing.reshape((rows * along,) + outgoing.shape[2:])
    got = lax.all_to_all(outgoing, ("pairs", "z"), split_axis=0, concat_axis=0, tiled=True)
    screen, motion = invert_pixels(got, inverse, block)
    return tuple(jnp.transpose(v, (3, 0, 1, 2)) for v in (screen, motion))


def solution(mesh):
    shape = (mesh.shape["pairs"], mesh.shape["stripe"] // 2, 2)
    if isinstance(mesh, Mesh):
        finer = Mesh(mesh.devices.reshape(shape), ("pairs", "z", "x"))
    else:
        finer = jax.sharding.AbstractMesh(shape, ("pairs", "z", "x"))
    placed = P(None, None, "pairs", ("z", "x"))

    return jax.shard_map(
        local,
        mesh=finer,
        in_specs=(P(("pairs", "z", "x"), None, None, None), P(), P(), P()),
        out_specs=(placed, placed),
        check_vma=False,
    )
```

```python
from functools import partial

import jax
import jax.numpy as jnp
from jax import lax
from jax.experimental import pallas as pl
from jax.experimental.pallas import tpu as pltpu
from jax.sharding import Mesh, PartitionSpec as P


MAXB = 5
LA = 4
LR = 16
MAXA = 8
FILTER_R = 3
LANES = 128
STRIPES = 4
GRANT = 16 << 20
WHOLE_GRANT = 60 << 20
damping = 0.5


def vmem():
    return pl.BlockSpec(memory_space=pltpu.VMEM)


def tap(k):
    sigma = FILTER_R / 2.0
    return jnp.exp(-jnp.float32(k * k) / jnp.float32(2.0 * sigma * sigma))


def resample_kernel(first, parts, info, az, rg, img, *rest):
    rest = rest[-4 - parts :]
    keep, sends = rest[0], rest[1 : 1 + parts]
    tiles_of, spread, shifted = rest[1 + parts :]
    lines, full = img.shape[2], img.shape[3]
    tiles = full // LANES
    groups = tiles // (2 * STRIPES)
    blocks = lines // (8 * LA)
    high = lines + 2 * MAXA
    span = STRIPES * LANES
    date = info[1] + first + pl.program_id(0)
    x = info[0]
    shift = rg[date]
    step = az[date]
    behind = shift < 0
    origin = jnp.where(behind, -1, 0)
    amount = shift - origin * LANES
    turn = lax.rem(LANES - amount, LANES)
    lane = lax.broadcasted_iota(jnp.int32, (lines, LANES), 1)
    own = lane + amount < LANES

    @pl.when(pl.program_id(0) == 0)
    def _():
        blank = jnp.zeros((MAXA, LANES), jnp.float32)
        for t in range(shifted.shape[0] // high):
            shifted[pl.ds(t * high, MAXA), :] = blank
            shifted[pl.ds(t * high + MAXA + lines, MAXA), :] = blank
        source = lax.broadcasted_iota(jnp.int32, (span, span), 0)
        target = lax.broadcasted_iota(jnp.int32, (1, span), 1)
        column, few = target & 7, (target >> 3) & 3
        stripe, many = (target >> 5) & 3, target >> 7
        wanted = stripe * LANES + column * LR + many * 4 + few
        spread[...] = jnp.where(source == wanted, 1.0, 0.0).astype(jnp.bfloat16)

    for c in range(2):

        def turned(t):
            place = jnp.clip(t + origin, 0, tiles - 1)
            tile = img[0, c, :, pl.ds(pl.multiple_of(place * LANES, LANES), LANES)]
            out = pltpu.roll(tile.astype(jnp.float32), turn, 1)
            if t == 0:
                out = jnp.where(behind, 0.0, out)
            if t == tiles:
                out = jnp.where(behind, out, 0.0)
            return out

        here = turned(0)
        for t in range(tiles):
            after = turned(t + 1)
            group, stripe, parity = t // 2 // STRIPES, t // 2 % STRIPES, t % 2
            tiles_of[
                group, pl.ds((c * 2 + parity) * lines, lines), pl.ds(stripe * LANES, LANES)
            ] = jnp.where(own, here, after).astype(jnp.bfloat16)
            here = after

    def slab(c, parity, group, many):
        return (((c * 2 + parity) * groups + group) * 4 + many) * high + MAXA

    for group in range(groups):
        for half in range(2):
            result = jnp.dot(
                tiles_of[group],
                spread[:, half * span // 2 : (half + 1) * span // 2],
                preferred_element_type=jnp.float32,
            )
            for c in range(2):
                for parity in range(2):
                    for k in range(2):
                        at = (c * 2 + parity) * lines
                        shifted[pl.ds(slab(c, parity, group, 2 * half + k), lines), :] = result[
                            at : at + lines, k * LANES : (k + 1) * LANES
                        ]

    def put(out, place, block, c, group, parity):
        for look in range(LA):
            for pair in range(2):
                both = [
                    shifted[
                        pl.ds(
                            slab(c, parity, group, 2 * pair + k) + step + 8 * LA * block + look,
                            8,
                            stride=LA,
                        ),
                        :,
                    ]
                    for k in range(2)
                ]
                out[0, c, place, group, pl.ds(32 * look + 16 * pair, 16), :] = jnp.concatenate(
                    both, 0
                ).astype(jnp.bfloat16)

    width = blocks // parts
    for c in range(2):
        for block in range(blocks):
            for group in range(groups):
                put(sends[block // width], block % width, block, c, group, 1 - x)
                put(keep, block, block, c, group, x)


def resample(images, az, rg, info, first, count, parts, earlier):
    lines, full = images.shape[2], images.shape[3]
    tiles = full // LANES
    groups = tiles // (2 * STRIPES)
    blocks = lines // (8 * LA)
    rows = 8 * LA * 4

    def block(width):
        return pl.BlockSpec(
            (1, 2, width, groups, rows, LANES), lambda i, *_: (i, 0, 0, 0, 0, 0)
        )

    def shape(width):
        return jax.ShapeDtypeStruct((count, 2, width, groups, rows, LANES), jnp.bfloat16)

    widths = [blocks] + [blocks // parts] * parts
    return pl.pallas_call(
        partial(resample_kernel, first, parts),
        grid_spec=pltpu.PrefetchScalarGridSpec(
            num_scalar_prefetch=3,
            grid=(count,),
            in_specs=[pl.BlockSpec((1, 2, lines, full), lambda i, *_: (i + first, 0, 0, 0))]
            + [pl.BlockSpec(memory_space=pl.ANY)] * len(earlier),
            out_specs=[block(w) for w in widths],
            scratch_shapes=[
                pltpu.VMEM((groups, 4 * lines, STRIPES * LANES), jnp.bfloat16),
                pltpu.VMEM((STRIPES * LANES, STRIPES * LANES), jnp.bfloat16),
                pltpu.VMEM((16 * groups * (lines + 2 * MAXA), LANES), jnp.float32),
            ],
        ),
        out_shape=[shape(w) for w in widths],
        compiler_params=pltpu.CompilerParams(vmem_limit_bytes=WHOLE_GRANT),
        cost_estimate=pl.CostEstimate(
            flops=count * lines * full * 4,
            transcendentals=0,
            bytes_accessed=count * lines * full * 8,
        ),
    )(info, az, rg, images, *earlier)


def merge(x, y, bit, distance):
    return jnp.where(
        bit, x + pltpu.roll(x, LANES - distance, 1), y + pltpu.roll(y, distance, 1)
    )


def pair_kernel(own, starts, reached, info, mask, *refs):
    count = len(starts)
    parts, following = refs[: 2 * count], refs[2 * count : 2 * count + len(reached)]
    right, images, products, sums = refs[-4:]
    block = 2 * own
    x = info[0]
    mine, other = x * own, (1 - x) * own
    for s, start in enumerate(starts):
        for where, ref in ((mine, parts[2 * s]), (other, parts[2 * s + 1])):
            for i in range(ref.shape[0]):
                images[where + start + i] = ref[i, :, 0, 0].astype(jnp.float32)
    for start, ref in zip(reached, following):
        for i in range(ref.shape[0]):
            images[block + start + i] = ref[i, :, 0, 0].astype(jnp.float32)
    sums[...] = jnp.zeros_like(sums)

    def multiply(d, carry):
        totals = [[None] * 2 for _ in range(MAXB)]
        for k in range(images.shape[2] // 8):
            at = pl.ds(8 * k, 8)
            a, b = images[d, 0, at, :], images[d, 1, at, :]
            for g in range(MAXB):
                c, e = images[d + g + 1, 0, at, :], images[d + g + 1, 1, at, :]
                terms = (a * c + b * e, b * c - a * e)
                for comp, term in enumerate(terms):
                    old = totals[g][comp]
                    totals[g][comp] = term if old is None else old + term
        for g in range(MAXB):
            for comp in range(2):
                at = ((d * MAXB + g) * 2 + comp) * 8
                products[pl.ds(pl.multiple_of(at, 8), 8), :] = totals[g][comp]
        return carry

    lax.fori_loop(0, block, multiply, 0)
    lane = lax.broadcasted_iota(jnp.int32, (8, LANES), 1)
    real = lane & 8 == 0
    place = lane >> 4

    def slot(d, g):
        at = (d * MAXB + g) * 16
        value = merge(
            products[pl.ds(pl.multiple_of(at, 8), 8), :],
            products[pl.ds(pl.multiple_of(at + 8, 8), 8), :],
            real,
            8,
        )
        value = value + pltpu.roll(value, LANES - 16, 1)
        value = (value * (1.0 / (LA * LR))).astype(jnp.bfloat16).astype(jnp.float32)
        return value * mask[g, info[2] + d].astype(jnp.float32)

    step = 4 if block % 4 == 0 else 1

    def gather(i, carry):
        totals = [None] * (step + MAXB)

        def add(at, value):
            totals[at] = value if totals[at] is None else totals[at] + value

        for j in range(step):
            for g in range(MAXB):
                value = slot(i * step + j, g)
                add(j, value)
                add(j + g + 1, -value)
        for j, value in enumerate(totals):
            at = pl.ds(pl.multiple_of(8 * (i * step + j), 8), 8)
            sums[at, :] = sums[at, :] + value
        return carry

    lax.fori_loop(0, block // step, gather, 0)
    for group in range(right.shape[2] // 8):
        rows = [sums[pl.ds(64 * group + u, 8, stride=8), :] for u in range(8)]
        turned = []
        for s in range(8):
            joined = rows[s]
            for z in range(1, STRIPES):
                joined = jnp.where(place == 2 * z, rows[(s + 2 * z) % 8], joined)
            turned.append(pltpu.roll(joined, 16 * s, 1) if s else joined)
        for z in range(STRIPES):
            out = turned[0]
            for s in range(1, 8):
                out = jnp.where(place == (2 * z + s) % 8, turned[s], out)
            right[right.shape[0] - 1, z, pl.ds(8 * group, 8), :] = out
    if right.shape[0] > 1:
        right[0] = refs[-5][0]


def pair_sums(info, mask, pieces, following, earlier, chunk, chunks, own, deep):
    groups, lines = pieces[0][1].shape[3:5]

    def window(array, parts):
        offset = chunk % (chunks // parts)
        return pl.BlockSpec(
            (array.shape[0], 2, 1, 1, lines, LANES), lambda i, *_: (0, 0, offset, i, 0, 0)
        )

    operands, specs = [], []
    for _, keep, received in pieces:
        got = received[chunk * len(received) // chunks]
        operands += [keep, got]
        specs += [window(keep, 1), window(got, len(received))]
    for _, received in following:
        got = received[chunk * len(received) // chunks]
        operands.append(got)
        specs.append(window(got, len(received)))
    joined = chunk == 1
    if earlier is not None:
        operands.append(earlier)
        specs.append(
            pl.BlockSpec((1, STRIPES, deep, LANES), lambda i, *_: (0, i, 0, 0))
            if joined
            else pl.BlockSpec(memory_space=pl.ANY)
        )
    work = 2 * own * MAXB * lines * LANES * groups
    return pl.pallas_call(
        partial(pair_kernel, own, [p[0] for p in pieces], [f[0] for f in following]),
        grid_spec=pltpu.PrefetchScalarGridSpec(
            num_scalar_prefetch=2,
            grid=(groups,),
            in_specs=specs,
            out_specs=pl.BlockSpec((1 + joined, STRIPES, deep, LANES), lambda i, *_: (0, i, 0, 0)),
            scratch_shapes=[
                pltpu.VMEM((2 * own + MAXB, 2, lines, LANES), jnp.float32),
                pltpu.VMEM((2 * own * MAXB * 16, LANES), jnp.float32),
                pltpu.VMEM((8 * deep, LANES), jnp.float32),
            ],
        ),
        out_shape=jax.ShapeDtypeStruct((1 + joined, groups * STRIPES, deep, LANES), jnp.float32),
        compiler_params=pltpu.CompilerParams(vmem_limit_bytes=GRANT),
        cost_estimate=pl.CostEstimate(flops=work * 8, transcendentals=0, bytes_accessed=work),
    )(info, mask, *operands)


def filter_kernel(count, info, *rest):
    weight, out, along = rest[2 * count :]
    own, partner = (
        [ref.at[i] for ref in refs for i in range(ref.shape[0])]
        for refs in (rest[:count], rest[count : 2 * count])
    )
    rows = len(own)
    tiles, deep = own[0].shape[:2]
    x = info[0]
    blank = jnp.zeros((rows, deep, LANES), jnp.float32)
    along[0] = blank
    along[2 * tiles + 1] = blank
    lane = lax.broadcasted_iota(jnp.int32, (deep, LANES), 1)
    place = lane & 7
    taps = [tap(k) for k in range(FILTER_R + 1)]
    most = jnp.zeros((deep, LANES), jnp.float32)
    for ref in own + partner:
        for i in range(tiles):
            most = jnp.maximum(most, jnp.abs(ref[i]))
    most = jnp.full((8, LANES), jnp.maximum(jnp.max(most), 1e-30))
    power = jnp.ceil(jnp.log2(most) + 0.001)
    scale = jnp.exp2(15.0 - power)[:1]
    code = power[:1]
    last_row = lax.broadcasted_iota(jnp.int32, (deep, LANES), 0) == deep - 1

    def coded(value):
        return jnp.where(last_row, code, value * scale)

    def turn(v, k):
        return pltpu.roll(v, k % LANES, 1)

    for refs, side in ((partner, 1 - x), (own, x)):
        for i in range(tiles):
            values = [ref[i] for ref in refs]
            for r in range(rows):
                acc = values[r]
                for k in range(1, FILTER_R + 1):
                    reach = 16 * k
                    last = values[r - 1] if r > 0 else jnp.zeros_like(acc)
                    later = values[r + 1] if r + 1 < rows else jnp.zeros_like(acc)
                    up = turn(jnp.where(lane >= reach, values[r], later), -reach)
                    down = turn(jnp.where(lane < LANES - reach, values[r], last), reach)
                    acc = acc + taps[k] * (up + down)
                along[2 * i + side + 1, r] = acc

    for i in range(tiles):
        at = 2 * i + x + 1
        for r in range(rows):
            v, left, right = along[at, r], along[at - 1, r], along[at + 1, r]
            acc = v
            for k in range(1, FILTER_R + 1):
                near = jnp.where(place < 8 - k, turn(v, -k), turn(right, 8 - k)) + jnp.where(
                    place >= k, turn(v, k), turn(left, k - 8)
                )
                acc = acc + taps[k] * near
            out[r, i, 0] = coded(own[r][i])
            out[r, i, 1] = coded(acc * weight[i, r : r + 1, :])


def filtered(info, own, partner, weight):
    count = len(own)
    rows = sum(v.shape[0] for v in own)
    tiles, deep = own[0].shape[1:3]
    smem = pl.BlockSpec(memory_space=pltpu.SMEM)
    return pl.pallas_call(
        partial(filter_kernel, count),
        in_specs=[smem] + [vmem()] * (2 * count + 1),
        out_specs=vmem(),
        out_shape=jax.ShapeDtypeStruct((rows, tiles, 2, deep, LANES), jnp.float32),
        scratch_shapes=[pltpu.VMEM((2 * tiles + 2, rows, deep, LANES), jnp.float32)],
        name="smooth",
        compiler_params=pltpu.CompilerParams(vmem_limit_bytes=GRANT),
    )(info, *own, *partner, weight)


def edge_weights(positions, whole):
    total = jnp.zeros(positions.shape, jnp.float32)
    for k in range(-FILTER_R, FILTER_R + 1):
        at = positions + k
        total = total + jnp.where((at >= 0) & (at < whole), tap(k), 0.0)
    return total


def invert_kernel(normal, out):
    size = normal.shape[0]
    low, high = damping, damping + 4.0 * MAXB
    middle, spread = high + low, high - low
    peak = 2.0 * (middle / spread) ** 2 - 1.0
    row = lax.broadcasted_iota(jnp.int32, (size, size), 0)
    col = lax.broadcasted_iota(jnp.int32, (size, size), 1)
    unit = jnp.where(row == col, 1.0, 0.0).astype(jnp.float32)
    n = normal[...]
    guess = (8.0 * middle / spread**2 / peak) * unit - (8.0 / spread**2 / peak) * n
    whole = n.astype(jnp.bfloat16)

    def times_normal(value):
        total = None
        for _ in range(3):
            part = value.astype(jnp.bfloat16)
            value = value - part.astype(jnp.float32)
            term = jnp.dot(whole, part, preferred_element_type=jnp.float32)
            total = term if total is None else total + term
        return total

    error = 1.0 / peak
    while error > 1e-8:
        scale = 2.0 / (2.0 - error * error)
        residual = unit - times_normal(guess)
        precision = lax.Precision.HIGHEST if error < 0.1 else lax.Precision.DEFAULT
        change = jnp.dot(guess, residual, precision=precision, preferred_element_type=jnp.float32)
        guess = scale * (guess + change)
        error = error * error / (2.0 - error * error)
    out[...] = guess


def invert(normal):
    size = normal.shape[0]
    return pl.pallas_call(
        invert_kernel,
        in_specs=[vmem()],
        out_specs=vmem(),
        out_shape=jax.ShapeDtypeStruct((size, size), jnp.float32),
        name="invert",
        compiler_params=pltpu.CompilerParams(vmem_limit_bytes=GRANT),
        cost_estimate=pl.CostEstimate(
            flops=120 * size**3, transcendentals=0, bytes_accessed=8 * size * size
        ),
    )(normal)


def series_kernel(block, got, inverse, screen, motion, right):
    sources, _, deep = got.shape[:3]
    right[...] = jnp.zeros_like(right)
    used = lax.broadcasted_iota(jnp.int32, (deep, LANES), 0) < block + MAXB
    for s in range(sources):
        for part in range(2):
            lanes = pl.ds(part * LANES, LANES)
            at = pl.ds(s * block, deep)
            values = got[s, part]
            scale = jnp.exp2(values[deep - 1 :] - 15.0)
            right[at, lanes] = right[at, lanes] + jnp.where(used, values * scale, 0.0)
    result = jnp.dot(
        right[: inverse.shape[0], :].T,
        inverse[...],
        precision=lax.Precision.HIGHEST,
        preferred_element_type=jnp.float32,
    )
    for u in range(8):
        for comp in range(2):
            at = u * 16 + comp * 8
            first, second = result[at : at + 8], result[LANES + at : LANES + at + 8]
            screen[comp, u] = second
            motion[comp, u] = first - second


def invert_pixels(got, inverse, block):
    dates = inverse.shape[0]
    shape = jax.ShapeDtypeStruct((2, 8, 8, dates), jnp.float32)
    return pl.pallas_call(
        partial(series_kernel, block),
        in_specs=[vmem(), vmem()],
        out_specs=[vmem(), vmem()],
        out_shape=[shape, shape],
        scratch_shapes=[pltpu.VMEM((dates + got.shape[2] - block, 2 * LANES), jnp.float32)],
        name="series",
        compiler_params=pltpu.CompilerParams(vmem_limit_bytes=GRANT),
    )(got, inverse)


def local(images, az, rg, pair_list):
    own, _, lines, full = images.shape
    dates = az.shape[0]
    groups, along, _ = (lax.axis_size(name) for name in ("pairs", "z", "x"))
    blocks = groups * along
    block = 2 * own
    deep = -(-(block + MAXB + 1) // 8) * 8
    rows = groups
    if full != 2 * along * LANES or along % STRIPES or lines != rows * 8 * LA:
        raise ValueError("unsupported shape")
    x = lax.axis_index("x")
    place = lax.axis_index(("pairs", "z"))
    info = jnp.stack([x, (2 * place + x) * own, place * block]).astype(jnp.int32)

    date_ids = jnp.arange(dates, dtype=jnp.int32)
    is_reference = date_ids[:, None] == pair_list[None, :, 0]
    is_secondary = date_ids[:, None] == pair_list[None, :, 1]
    design = (is_reference.astype(jnp.float32) - is_secondary.astype(jnp.float32)).astype(
        jnp.bfloat16
    )
    normal = jnp.dot(design, design.T, preferred_element_type=jnp.float32)
    normal = normal + damping * jnp.eye(dates, dtype=jnp.float32)
    gaps = pair_list[:, 1] - pair_list[:, 0]
    is_gap = jnp.arange(1, MAXB + 1, dtype=jnp.int32)[:, None] == gaps[None, :]
    mask = jnp.dot(
        is_gap.astype(jnp.bfloat16),
        is_reference.astype(jnp.bfloat16).T,
        preferred_element_type=jnp.float32,
    )
    mask = mask.astype(jnp.int32)
    inverse = invert(normal)

    swap = [(0, 1), (1, 0)]
    cuts, parts = [0, own], [1]
    if own > MAXB:
        cuts, parts = [0, 1, 2, MAXB, own], [1, 1, min(rows, 2), rows]
    pieces, following = [], []
    left, turn = x == 0, 0

    def send_back(start, keep, received, left):
        hops = []
        for c, other in enumerate(received):
            part = other.shape[2]
            mine = lax.slice_in_dim(keep, c * part, (c + 1) * part, axis=2)
            lower, upper = mine, other
            if own < MAXB:
                lower = jnp.concatenate([mine, other], 0)[:MAXB]
                upper = jnp.concatenate([other, mine], 0)[:MAXB]
            hops.append(jnp.where(left, lower, upper))
            if own > MAXB:
                left, hops[-1] = lax.optimization_barrier((left, hops[-1]))
        if own < MAXB:
            for hop in range(1, -(-MAXB // block) + 1):
                route = [(i + hop, i) for i in range(blocks - hop)]
                count = min(block, MAXB - (hop - 1) * block)
                going = [lax.ppermute(v[:count], ("pairs", "z"), route) for v in hops]
                following.append(((hop - 1) * block, going))
        else:
            route = [(i + 1, i) for i in range(blocks - 1)]
            going = []
            for v in hops:
                going.append(lax.ppermute(v, ("pairs", "z"), route))
            following.append((start, going))
        return left

    for start, end, count in zip(cuts, cuts[1:], parts):
        after = [p[1] for p in pieces[-1:]]
        keep, *sends = resample(images, az, rg, info, start, end - start, count, after)
        received = []
        for v in sends:
            received.append(lax.ppermute(v, "x", swap))
            turn += 1
        pieces.append((start, keep, received))
    for start, keep, received in pieces:
        if start < MAXB:
            left = send_back(start, keep, received, left)

    sums = []
    for c in range(rows):
        earlier = sums[-1] if sums else None
        sums.append(pair_sums(info, mask, pieces, following, earlier, c, rows, own, deep))
    sums = sums[1:]
    partner = [lax.ppermute(s, "x", swap) for s in sums]

    lane = jnp.arange(LANES, dtype=jnp.int32)
    row_at = jnp.arange(rows, dtype=jnp.int32)[:, None] * 8 + (lane // 16)[None, :]
    stripe = 2 * jnp.arange(along, dtype=jnp.int32) + x
    col_at = stripe[:, None] * 8 + (lane & 7)[None, :]
    row_weight = edge_weights(row_at, lines // LA)
    col_weight = edge_weights(col_at, full // LR)
    weight = 1.0 / (row_weight[None, :, :] * col_weight[:, None, :])

    outgoing = filtered(info, sums, partner, weight)
    outgoing = outgoing.reshape((rows * along,) + outgoing.shape[2:]).astype(jnp.float16)
    got = lax.all_to_all(outgoing, ("pairs", "z"), split_axis=0, concat_axis=0, tiled=True)
    got = got.astype(jnp.float32)
    screen, motion = invert_pixels(got, inverse, block)
    return tuple(jnp.transpose(v, (3, 0, 1, 2)) for v in (screen, motion))


def solution(mesh):
    shape = (mesh.shape["pairs"], mesh.shape["stripe"] // 2, 2)
    if isinstance(mesh, Mesh):
        finer = Mesh(mesh.devices.reshape(shape), ("pairs", "z", "x"))
    else:
        finer = jax.sharding.AbstractMesh(shape, ("pairs", "z", "x"))
    placed = P(None, None, "pairs", ("z", "x"))

    return jax.shard_map(
        local,
        mesh=finer,
        in_specs=(P(("pairs", "z", "x"), None, None, None), P(), P(), P()),
        out_specs=(placed, placed),
        check_vma=False,
    )
```

```python
from functools import partial

import jax
import jax.numpy as jnp
from jax import lax
from jax.experimental import pallas as pl
from jax.experimental.pallas import tpu as pltpu
from jax.sharding import Mesh, PartitionSpec as P


MAXB = 5
LA = 4
LR = 16
MAXA = 8
FILTER_R = 3
LANES = 128
STRIPES = 4
GRANT = 16 << 20
WHOLE_GRANT = 60 << 20
damping = 0.5


def vmem():
    return pl.BlockSpec(memory_space=pltpu.VMEM)


def tap(k):
    sigma = FILTER_R / 2.0
    return jnp.exp(-jnp.float32(k * k) / jnp.float32(2.0 * sigma * sigma))


def position(own):
    x = lax.axis_index("x")
    place = lax.axis_index("pairs") * lax.axis_size("z") + lax.axis_index("z")
    return x, (2 * place + x) * own, 2 * place * own


def resample_kernel(own_dates, first, parts, az, rg, img, *rest):
    rest = rest[-4 - parts :]
    keep, sends = rest[0], rest[1 : 1 + parts]
    tiles_of, spread, shifted = rest[1 + parts :]
    lines, full = img.shape[2], img.shape[3]
    tiles = full // LANES
    groups = tiles // (2 * STRIPES)
    blocks = lines // (8 * LA)
    high = lines + 2 * MAXA
    span = STRIPES * LANES
    x, base, _ = position(own_dates)
    date = base + first + pl.program_id(0)
    shift = rg[date]
    step = az[date]
    behind = shift < 0
    origin = jnp.where(behind, -1, 0)
    amount = shift - origin * LANES
    turn = lax.rem(LANES - amount, LANES)
    lane = lax.broadcasted_iota(jnp.int32, (lines, LANES), 1)
    own = lane + amount < LANES

    @pl.when(pl.program_id(0) == 0)
    def _():
        blank = jnp.zeros((MAXA, LANES), jnp.float32)
        for t in range(shifted.shape[0] // high):
            shifted[pl.ds(t * high, MAXA), :] = blank
            shifted[pl.ds(t * high + MAXA + lines, MAXA), :] = blank
        source = lax.broadcasted_iota(jnp.int32, (span, span), 0)
        target = lax.broadcasted_iota(jnp.int32, (1, span), 1)
        column, few = target & 7, (target >> 3) & 3
        stripe, many = (target >> 5) & 3, target >> 7
        wanted = stripe * LANES + column * LR + many * 4 + few
        spread[...] = jnp.where(source == wanted, 1.0, 0.0).astype(jnp.bfloat16)

    for c in range(2):

        def turned(t):
            place = jnp.clip(t + origin, 0, tiles - 1)
            tile = img[0, c, :, pl.ds(pl.multiple_of(place * LANES, LANES), LANES)]
            out = pltpu.roll(tile.astype(jnp.float32), turn, 1)
            if t == 0:
                out = jnp.where(behind, 0.0, out)
            if t == tiles:
                out = jnp.where(behind, out, 0.0)
            return out

        here = turned(0)
        for t in range(tiles):
            after = turned(t + 1)
            group, stripe, parity = t // 2 // STRIPES, t // 2 % STRIPES, t % 2
            tiles_of[
                group, pl.ds((c * 2 + parity) * lines, lines), pl.ds(stripe * LANES, LANES)
            ] = jnp.where(own, here, after).astype(jnp.bfloat16)
            here = after

    def slab(c, parity, group, many):
        return (((c * 2 + parity) * groups + group) * 4 + many) * high + MAXA

    for group in range(groups):
        for half in range(2):
            result = jnp.dot(
                tiles_of[group],
                spread[:, half * span // 2 : (half + 1) * span // 2],
                preferred_element_type=jnp.float32,
            )
            for c in range(2):
                for parity in range(2):
                    for k in range(2):
                        at = (c * 2 + parity) * lines
                        shifted[pl.ds(slab(c, parity, group, 2 * half + k), lines), :] = result[
                            at : at + lines, k * LANES : (k + 1) * LANES
                        ]

    def put(out, place, block, c, group, parity):
        for look in range(LA):
            for pair in range(2):
                both = [
                    shifted[
                        pl.ds(
                            slab(c, parity, group, 2 * pair + k) + step + 8 * LA * block + look,
                            8,
                            stride=LA,
                        ),
                        :,
                    ]
                    for k in range(2)
                ]
                out[0, c, place, group, pl.ds(32 * look + 16 * pair, 16), :] = jnp.concatenate(
                    both, 0
                ).astype(jnp.bfloat16)

    width = blocks // parts
    for c in range(2):
        for block in range(blocks):
            for group in range(groups):
                put(sends[block // width], block % width, block, c, group, 1 - x)
                put(keep, block, block, c, group, x)


def resample(images, az, rg, first, count, parts, earlier):
    lines, full = images.shape[2], images.shape[3]
    tiles = full // LANES
    groups = tiles // (2 * STRIPES)
    blocks = lines // (8 * LA)
    rows = 8 * LA * 4

    def block(width):
        return pl.BlockSpec(
            (1, 2, width, groups, rows, LANES), lambda i, *_: (i, 0, 0, 0, 0, 0)
        )

    def shape(width):
        return jax.ShapeDtypeStruct((count, 2, width, groups, rows, LANES), jnp.bfloat16)

    widths = [blocks] + [blocks // parts] * parts
    return pl.pallas_call(
        partial(resample_kernel, images.shape[0], first, parts),
        grid_spec=pltpu.PrefetchScalarGridSpec(
            num_scalar_prefetch=2,
            grid=(count,),
            in_specs=[pl.BlockSpec((1, 2, lines, full), lambda i, *_: (i + first, 0, 0, 0))]
            + [pl.BlockSpec(memory_space=pl.ANY)] * len(earlier),
            out_specs=[block(w) for w in widths],
            scratch_shapes=[
                pltpu.VMEM((groups, 4 * lines, STRIPES * LANES), jnp.bfloat16),
                pltpu.VMEM((STRIPES * LANES, STRIPES * LANES), jnp.bfloat16),
                pltpu.VMEM((16 * groups * (lines + 2 * MAXA), LANES), jnp.float32),
            ],
        ),
        out_shape=[shape(w) for w in widths],
        compiler_params=pltpu.CompilerParams(vmem_limit_bytes=WHOLE_GRANT),
        cost_estimate=pl.CostEstimate(
            flops=count * lines * full * 4,
            transcendentals=0,
            bytes_accessed=count * lines * full * 8,
        ),
    )(az, rg, images, *earlier)


def merge(x, y, bit, distance):
    return jnp.where(
        bit, x + pltpu.roll(x, LANES - distance, 1), y + pltpu.roll(y, distance, 1)
    )


def pair_kernel(own, starts, reached, mask, *refs):
    count = len(starts)
    parts, following = refs[: 2 * count], refs[2 * count : 2 * count + len(reached)]
    right, images, products, sums = refs[-4:]
    block = 2 * own
    x, _, date0 = position(own)
    mine, other = x * own, (1 - x) * own
    for s, start in enumerate(starts):
        for where, ref in ((mine, parts[2 * s]), (other, parts[2 * s + 1])):
            for i in range(ref.shape[0]):
                images[where + start + i] = ref[i, :, 0, 0].astype(jnp.float32)
    for start, ref in zip(reached, following):
        for i in range(ref.shape[0]):
            images[block + start + i] = ref[i, :, 0, 0].astype(jnp.float32)
    sums[...] = jnp.zeros_like(sums)

    def multiply(d, carry):
        totals = [[None] * 2 for _ in range(MAXB)]
        for k in range(images.shape[2] // 8):
            at = pl.ds(8 * k, 8)
            a, b = images[d, 0, at, :], images[d, 1, at, :]
            for g in range(MAXB):
                c, e = images[d + g + 1, 0, at, :], images[d + g + 1, 1, at, :]
                terms = (a * c + b * e, b * c - a * e)
                for comp, term in enumerate(terms):
                    old = totals[g][comp]
                    totals[g][comp] = term if old is None else old + term
        for g in range(MAXB):
            for comp in range(2):
                at = ((d * MAXB + g) * 2 + comp) * 8
                products[pl.ds(pl.multiple_of(at, 8), 8), :] = totals[g][comp]
        return carry

    lax.fori_loop(0, block, multiply, 0)
    lane = lax.broadcasted_iota(jnp.int32, (8, LANES), 1)
    real = lane & 8 == 0
    place = lane >> 4

    def slot(d, g):
        at = (d * MAXB + g) * 16
        value = merge(
            products[pl.ds(pl.multiple_of(at, 8), 8), :],
            products[pl.ds(pl.multiple_of(at + 8, 8), 8), :],
            real,
            8,
        )
        value = value + pltpu.roll(value, LANES - 16, 1)
        value = (value * (1.0 / (LA * LR))).astype(jnp.bfloat16).astype(jnp.float32)
        return value * mask[g, date0 + d].astype(jnp.float32)

    step = 4 if block % 4 == 0 else 1

    def gather(i, carry):
        totals = [None] * (step + MAXB)

        def add(at, value):
            totals[at] = value if totals[at] is None else totals[at] + value

        for j in range(step):
            for g in range(MAXB):
                value = slot(i * step + j, g)
                add(j, value)
                add(j + g + 1, -value)
        for j, value in enumerate(totals):
            at = pl.ds(pl.multiple_of(8 * (i * step + j), 8), 8)
            sums[at, :] = sums[at, :] + value
        return carry

    lax.fori_loop(0, block // step, gather, 0)
    for group in range(right.shape[2] // 8):
        rows = [sums[pl.ds(64 * group + u, 8, stride=8), :] for u in range(8)]
        turned = []
        for s in range(8):
            joined = rows[s]
            for z in range(1, STRIPES):
                joined = jnp.where(place == 2 * z, rows[(s + 2 * z) % 8], joined)
            turned.append(pltpu.roll(joined, 16 * s, 1) if s else joined)
        for z in range(STRIPES):
            out = turned[0]
            for s in range(1, 8):
                out = jnp.where(place == (2 * z + s) % 8, turned[s], out)
            right[right.shape[0] - 1, z, pl.ds(8 * group, 8), :] = out
    if right.shape[0] > 1:
        right[0] = refs[-5][0]


def pair_sums(mask, pieces, following, earlier, chunk, chunks, own, deep):
    groups, lines = pieces[0][1].shape[3:5]

    def window(array, parts):
        offset = chunk % (chunks // parts)
        return pl.BlockSpec(
            (array.shape[0], 2, 1, 1, lines, LANES), lambda i, *_: (0, 0, offset, i, 0, 0)
        )

    operands, specs = [], []
    for _, keep, received in pieces:
        got = received[chunk * len(received) // chunks]
        operands += [keep, got]
        specs += [window(keep, 1), window(got, len(received))]
    for _, received in following:
        got = received[chunk * len(received) // chunks]
        operands.append(got)
        specs.append(window(got, len(received)))
    joined = chunk == 1
    if earlier is not None:
        operands.append(earlier)
        specs.append(
            pl.BlockSpec((1, STRIPES, deep, LANES), lambda i, *_: (0, i, 0, 0))
            if joined
            else pl.BlockSpec(memory_space=pl.ANY)
        )
    work = 2 * own * MAXB * lines * LANES * groups
    return pl.pallas_call(
        partial(pair_kernel, own, [p[0] for p in pieces], [f[0] for f in following]),
        grid_spec=pltpu.PrefetchScalarGridSpec(
            num_scalar_prefetch=1,
            grid=(groups,),
            in_specs=specs,
            out_specs=pl.BlockSpec((1 + joined, STRIPES, deep, LANES), lambda i, *_: (0, i, 0, 0)),
            scratch_shapes=[
                pltpu.VMEM((2 * own + MAXB, 2, lines, LANES), jnp.float32),
                pltpu.VMEM((2 * own * MAXB * 16, LANES), jnp.float32),
                pltpu.VMEM((8 * deep, LANES), jnp.float32),
            ],
        ),
        out_shape=jax.ShapeDtypeStruct((1 + joined, groups * STRIPES, deep, LANES), jnp.float32),
        compiler_params=pltpu.CompilerParams(vmem_limit_bytes=GRANT),
        cost_estimate=pl.CostEstimate(flops=work * 8, transcendentals=0, bytes_accessed=work),
    )(mask, *operands)


def filter_kernel(count, *rest):
    weight, out, along = rest[2 * count :]
    own, partner = (
        [ref.at[i] for ref in refs for i in range(ref.shape[0])]
        for refs in (rest[:count], rest[count : 2 * count])
    )
    rows = len(own)
    tiles, deep = own[0].shape[:2]
    x = lax.axis_index("x")
    blank = jnp.zeros((rows, deep, LANES), jnp.float32)
    along[0] = blank
    along[2 * tiles + 1] = blank
    lane = lax.broadcasted_iota(jnp.int32, (deep, LANES), 1)
    place = lane & 7
    taps = [tap(k) for k in range(FILTER_R + 1)]
    most = jnp.zeros((deep, LANES), jnp.float32)
    for ref in own + partner:
        for i in range(tiles):
            most = jnp.maximum(most, jnp.abs(ref[i]))
    most = jnp.full((8, LANES), jnp.maximum(jnp.max(most), 1e-30))
    power = jnp.ceil(jnp.log2(most) + 0.001)
    scale = jnp.exp2(15.0 - power)[:1]
    code = power[:1]
    last_row = lax.broadcasted_iota(jnp.int32, (deep, LANES), 0) == deep - 1

    def coded(value):
        return jnp.where(last_row, code, value * scale)

    def turn(v, k):
        return pltpu.roll(v, k % LANES, 1)

    for refs, side in ((partner, 1 - x), (own, x)):
        for i in range(tiles):
            values = [ref[i] for ref in refs]
            for r in range(rows):
                acc = values[r]
                for k in range(1, FILTER_R + 1):
                    reach = 16 * k
                    last = values[r - 1] if r > 0 else jnp.zeros_like(acc)
                    later = values[r + 1] if r + 1 < rows else jnp.zeros_like(acc)
                    up = turn(jnp.where(lane >= reach, values[r], later), -reach)
                    down = turn(jnp.where(lane < LANES - reach, values[r], last), reach)
                    acc = acc + taps[k] * (up + down)
                along[2 * i + side + 1, r] = acc

    for i in range(tiles):
        at = 2 * i + x + 1
        for r in range(rows):
            v, left, right = along[at, r], along[at - 1, r], along[at + 1, r]
            acc = v
            for k in range(1, FILTER_R + 1):
                near = jnp.where(place < 8 - k, turn(v, -k), turn(right, 8 - k)) + jnp.where(
                    place >= k, turn(v, k), turn(left, k - 8)
                )
                acc = acc + taps[k] * near
            out[r, i, 0] = coded(own[r][i])
            out[r, i, 1] = coded(acc * weight[i, r : r + 1, :])


def filtered(own, partner, weight):
    count = len(own)
    rows = sum(v.shape[0] for v in own)
    tiles, deep = own[0].shape[1:3]
    return pl.pallas_call(
        partial(filter_kernel, count),
        in_specs=[vmem()] * (2 * count + 1),
        out_specs=vmem(),
        out_shape=jax.ShapeDtypeStruct((rows, tiles, 2, deep, LANES), jnp.float32),
        scratch_shapes=[pltpu.VMEM((2 * tiles + 2, rows, deep, LANES), jnp.float32)],
        name="smooth",
        compiler_params=pltpu.CompilerParams(vmem_limit_bytes=GRANT),
    )(*own, *partner, weight)


def edge_weights(positions, whole):
    total = jnp.zeros(positions.shape, jnp.float32)
    for k in range(-FILTER_R, FILTER_R + 1):
        at = positions + k
        total = total + jnp.where((at >= 0) & (at < whole), tap(k), 0.0)
    return total


def invert_kernel(normal, out):
    size = normal.shape[0]
    low, high = damping, damping + 4.0 * MAXB
    middle, spread = high + low, high - low
    peak = 2.0 * (middle / spread) ** 2 - 1.0
    row = lax.broadcasted_iota(jnp.int32, (size, size), 0)
    col = lax.broadcasted_iota(jnp.int32, (size, size), 1)
    unit = jnp.where(row == col, 1.0, 0.0).astype(jnp.float32)
    n = normal[...]
    guess = (8.0 * middle / spread**2 / peak) * unit - (8.0 / spread**2 / peak) * n
    whole = n.astype(jnp.bfloat16)

    def times_normal(value):
        total = None
        for _ in range(3):
            part = value.astype(jnp.bfloat16)
            value = value - part.astype(jnp.float32)
            term = jnp.dot(whole, part, preferred_element_type=jnp.float32)
            total = term if total is None else total + term
        return total

    error = 1.0 / peak
    while error > 1e-8:
        scale = 2.0 / (2.0 - error * error)
        residual = unit - times_normal(guess)
        precision = lax.Precision.HIGHEST if error < 0.1 else lax.Precision.DEFAULT
        change = jnp.dot(guess, residual, precision=precision, preferred_element_type=jnp.float32)
        guess = scale * (guess + change)
        error = error * error / (2.0 - error * error)
    out[...] = guess


def invert(normal):
    size = normal.shape[0]
    return pl.pallas_call(
        invert_kernel,
        in_specs=[vmem()],
        out_specs=vmem(),
        out_shape=jax.ShapeDtypeStruct((size, size), jnp.float32),
        name="invert",
        compiler_params=pltpu.CompilerParams(vmem_limit_bytes=GRANT),
        cost_estimate=pl.CostEstimate(
            flops=120 * size**3, transcendentals=0, bytes_accessed=8 * size * size
        ),
    )(normal)


def series_kernel(block, got, inverse, screen, motion, right):
    sources, _, deep = got.shape[:3]
    right[...] = jnp.zeros_like(right)
    used = lax.broadcasted_iota(jnp.int32, (deep, LANES), 0) < block + MAXB
    for s in range(sources):
        for part in range(2):
            lanes = pl.ds(part * LANES, LANES)
            at = pl.ds(s * block, deep)
            values = got[s, part]
            scale = jnp.exp2(values[deep - 1 :] - 15.0)
            right[at, lanes] = right[at, lanes] + jnp.where(used, values * scale, 0.0)
    result = jnp.dot(
        right[: inverse.shape[0], :].T,
        inverse[...],
        precision=lax.Precision.HIGHEST,
        preferred_element_type=jnp.float32,
    )
    for u in range(8):
        for comp in range(2):
            at = u * 16 + comp * 8
            first, second = result[at : at + 8], result[LANES + at : LANES + at + 8]
            screen[comp, u] = second
            motion[comp, u] = first - second


def invert_pixels(got, inverse, block):
    dates = inverse.shape[0]
    shape = jax.ShapeDtypeStruct((2, 8, 8, dates), jnp.float32)
    return pl.pallas_call(
        partial(series_kernel, block),
        in_specs=[vmem(), vmem()],
        out_specs=[vmem(), vmem()],
        out_shape=[shape, shape],
        scratch_shapes=[pltpu.VMEM((dates + got.shape[2] - block, 2 * LANES), jnp.float32)],
        name="series",
        compiler_params=pltpu.CompilerParams(vmem_limit_bytes=GRANT),
    )(got, inverse)


def local(images, az, rg, pair_list):
    own, _, lines, full = images.shape
    dates = az.shape[0]
    groups, along, _ = (lax.axis_size(name) for name in ("pairs", "z", "x"))
    blocks = groups * along
    block = 2 * own
    deep = -(-(block + MAXB + 1) // 8) * 8
    rows = groups
    if full != 2 * along * LANES or along % STRIPES or lines != rows * 8 * LA:
        raise ValueError("unsupported shape")
    x = lax.axis_index("x")

    date_ids = jnp.arange(dates, dtype=jnp.int32)
    is_reference = date_ids[:, None] == pair_list[None, :, 0]
    is_secondary = date_ids[:, None] == pair_list[None, :, 1]
    design = (is_reference.astype(jnp.float32) - is_secondary.astype(jnp.float32)).astype(
        jnp.bfloat16
    )
    normal = jnp.dot(design, design.T, preferred_element_type=jnp.float32)
    normal = normal + damping * jnp.eye(dates, dtype=jnp.float32)
    gaps = pair_list[:, 1] - pair_list[:, 0]
    is_gap = jnp.arange(1, MAXB + 1, dtype=jnp.int32)[:, None] == gaps[None, :]
    mask = jnp.dot(
        is_gap.astype(jnp.bfloat16),
        is_reference.astype(jnp.bfloat16).T,
        preferred_element_type=jnp.float32,
    )
    mask = mask.astype(jnp.int32)
    inverse = invert(normal)

    swap = [(0, 1), (1, 0)]
    cuts, parts = [0, own], [1]
    if own > MAXB:
        cuts, parts = [0, 1, 2, MAXB, own], [1, 1, min(rows, 2), rows]
    pieces, following = [], []
    left, turn = x == 0, 0

    def send_back(start, keep, received, left):
        hops = []
        for c, other in enumerate(received):
            part = other.shape[2]
            mine = lax.slice_in_dim(keep, c * part, (c + 1) * part, axis=2)
            lower, upper = mine, other
            if own < MAXB:
                lower = jnp.concatenate([mine, other], 0)[:MAXB]
                upper = jnp.concatenate([other, mine], 0)[:MAXB]
            hops.append(jnp.where(left, lower, upper))
            if own > MAXB:
                left, hops[-1] = lax.optimization_barrier((left, hops[-1]))
        if own < MAXB:
            for hop in range(1, -(-MAXB // block) + 1):
                route = [(i + hop, i) for i in range(blocks - hop)]
                count = min(block, MAXB - (hop - 1) * block)
                going = [lax.ppermute(v[:count], ("pairs", "z"), route) for v in hops]
                following.append(((hop - 1) * block, going))
        else:
            route = [(i + 1, i) for i in range(blocks - 1)]
            going = []
            for v in hops:
                going.append(lax.ppermute(v, ("pairs", "z"), route))
            following.append((start, going))
        return left

    for start, end, count in zip(cuts, cuts[1:], parts):
        after = [p[1] for p in pieces[-1:]]
        keep, *sends = resample(images, az, rg, start, end - start, count, after)
        received = []
        for v in sends:
            received.append(lax.ppermute(v, "x", swap))
            turn += 1
        pieces.append((start, keep, received))
    for start, keep, received in pieces:
        if start < MAXB:
            left = send_back(start, keep, received, left)

    sums = []
    for c in range(rows):
        earlier = sums[-1] if sums else None
        sums.append(pair_sums(mask, pieces, following, earlier, c, rows, own, deep))
    sums = sums[1:]
    partner = [lax.ppermute(s, "x", swap) for s in sums]

    lane = jnp.arange(LANES, dtype=jnp.int32)
    row_at = jnp.arange(rows, dtype=jnp.int32)[:, None] * 8 + (lane // 16)[None, :]
    stripe = 2 * jnp.arange(along, dtype=jnp.int32) + x
    col_at = stripe[:, None] * 8 + (lane & 7)[None, :]
    row_weight = edge_weights(row_at, lines // LA)
    col_weight = edge_weights(col_at, full // LR)
    weight = 1.0 / (row_weight[None, :, :] * col_weight[:, None, :])

    outgoing = filtered(sums, partner, weight)
    outgoing = outgoing.reshape((rows * along,) + outgoing.shape[2:]).astype(jnp.float16)
    got = lax.all_to_all(outgoing, ("pairs", "z"), split_axis=0, concat_axis=0, tiled=True)
    got = got.astype(jnp.float32)
    screen, motion = invert_pixels(got, inverse, block)
    return tuple(jnp.transpose(v, (3, 0, 1, 2)) for v in (screen, motion))


def solution(mesh):
    shape = (mesh.shape["pairs"], mesh.shape["stripe"] // 2, 2)
    if isinstance(mesh, Mesh):
        finer = Mesh(mesh.devices.reshape(shape), ("pairs", "z", "x"))
    else:
        finer = jax.sharding.AbstractMesh(shape, ("pairs", "z", "x"))
    placed = P(None, None, "pairs", ("z", "x"))

    return jax.shard_map(
        local,
        mesh=finer,
        in_specs=(P(("pairs", "z", "x"), None, None, None), P(), P(), P()),
        out_specs=(placed, placed),
        check_vma=False,
    )
```

```python
from functools import partial

import jax
import jax.numpy as jnp
from jax import lax
from jax.experimental import pallas as pl
from jax.experimental.pallas import tpu as pltpu
from jax.sharding import Mesh, PartitionSpec as P


MAXB = 5
LA = 4
LR = 16
MAXA = 8
FILTER_R = 3
LANES = 128
STRIPES = 4
GRANT = 16 << 20
WHOLE_GRANT = 60 << 20
damping = 0.5


def vmem():
    return pl.BlockSpec(memory_space=pltpu.VMEM)


def tap(k):
    sigma = FILTER_R / 2.0
    return jnp.exp(-jnp.float32(k * k) / jnp.float32(2.0 * sigma * sigma))


def position(own):
    x = lax.axis_index("x")
    place = lax.axis_index("pairs") * lax.axis_size("z") + lax.axis_index("z")
    return x, (2 * place + x) * own, 2 * place * own


def resample_kernel(own_dates, first, parts, az, rg, img, *rest):
    rest = rest[-4 - parts :]
    keep, sends = rest[0], rest[1 : 1 + parts]
    tiles_of, spread, shifted = rest[1 + parts :]
    lines, full = img.shape[2], img.shape[3]
    tiles = full // LANES
    groups = tiles // (2 * STRIPES)
    blocks = lines // (8 * LA)
    high = lines + 2 * MAXA
    span = STRIPES * LANES
    x, base, _ = position(own_dates)
    date = base + first + pl.program_id(0)
    shift = rg[date]
    step = az[date]
    behind = shift < 0
    origin = jnp.where(behind, -1, 0)
    amount = shift - origin * LANES
    turn = lax.rem(LANES - amount, LANES)
    lane = lax.broadcasted_iota(jnp.int32, (lines, LANES), 1)
    own = lane + amount < LANES

    @pl.when(pl.program_id(0) == 0)
    def _():
        blank = jnp.zeros((MAXA, LANES), jnp.float32)
        for t in range(shifted.shape[0] // high):
            shifted[pl.ds(t * high, MAXA), :] = blank
            shifted[pl.ds(t * high + MAXA + lines, MAXA), :] = blank
        source = lax.broadcasted_iota(jnp.int32, (span, span), 0)
        target = lax.broadcasted_iota(jnp.int32, (1, span), 1)
        column, few = target & 7, ((target >> 6) & 1) * 2 + ((target >> 3) & 1)
        stripe, many = (target >> 4) & 3, target >> 7
        wanted = stripe * LANES + column * LR + many * 4 + few
        spread[...] = jnp.where(source == wanted, 1.0, 0.0).astype(jnp.bfloat16)

    for c in range(2):

        def turned(t):
            place = jnp.clip(t + origin, 0, tiles - 1)
            tile = img[0, c, :, pl.ds(pl.multiple_of(place * LANES, LANES), LANES)]
            out = pltpu.roll(tile.astype(jnp.float32), turn, 1)
            if t == 0:
                out = jnp.where(behind, 0.0, out)
            if t == tiles:
                out = jnp.where(behind, out, 0.0)
            return out

        here = turned(0)
        for t in range(tiles):
            after = turned(t + 1)
            group, stripe, parity = t // 2 // STRIPES, t // 2 % STRIPES, t % 2
            tiles_of[
                group, pl.ds((c * 2 + parity) * lines, lines), pl.ds(stripe * LANES, LANES)
            ] = jnp.where(own, here, after).astype(jnp.bfloat16)
            here = after

    def slab(c, parity, group, many):
        return (((c * 2 + parity) * groups + group) * 4 + many) * high + MAXA

    for group in range(groups):
        for half in range(2):
            result = jnp.dot(
                tiles_of[group],
                spread[:, half * span // 2 : (half + 1) * span // 2],
                preferred_element_type=jnp.float32,
            )
            for c in range(2):
                for parity in range(2):
                    for k in range(2):
                        at = (c * 2 + parity) * lines
                        shifted[pl.ds(slab(c, parity, group, 2 * half + k), lines), :] = result[
                            at : at + lines, k * LANES : (k + 1) * LANES
                        ]

    def put(out, place, block, c, group, parity):
        for look in range(LA):
            for pair in range(2):
                both = [
                    shifted[
                        pl.ds(
                            slab(c, parity, group, 2 * pair + k) + step + 8 * LA * block + look,
                            8,
                            stride=LA,
                        ),
                        :,
                    ]
                    for k in range(2)
                ]
                out[0, c, place, group, pl.ds(32 * look + 16 * pair, 16), :] = jnp.concatenate(
                    both, 0
                ).astype(jnp.bfloat16)

    width = blocks // parts
    for c in range(2):
        for block in range(blocks):
            for group in range(groups):
                put(sends[block // width], block % width, block, c, group, 1 - x)
                put(keep, block, block, c, group, x)


def resample(images, az, rg, first, count, parts, earlier):
    lines, full = images.shape[2], images.shape[3]
    tiles = full // LANES
    groups = tiles // (2 * STRIPES)
    blocks = lines // (8 * LA)
    rows = 8 * LA * 4

    def block(width):
        return pl.BlockSpec(
            (1, 2, width, groups, rows, LANES), lambda i, *_: (i, 0, 0, 0, 0, 0)
        )

    def shape(width):
        return jax.ShapeDtypeStruct((count, 2, width, groups, rows, LANES), jnp.bfloat16)

    widths = [blocks] + [blocks // parts] * parts
    return pl.pallas_call(
        partial(resample_kernel, images.shape[0], first, parts),
        grid_spec=pltpu.PrefetchScalarGridSpec(
            num_scalar_prefetch=2,
            grid=(count,),
            in_specs=[pl.BlockSpec((1, 2, lines, full), lambda i, *_: (i + first, 0, 0, 0))]
            + [pl.BlockSpec(memory_space=pl.ANY)] * len(earlier),
            out_specs=[block(w) for w in widths],
            scratch_shapes=[
                pltpu.VMEM((groups, 4 * lines, STRIPES * LANES), jnp.bfloat16),
                pltpu.VMEM((STRIPES * LANES, STRIPES * LANES), jnp.bfloat16),
                pltpu.VMEM((16 * groups * (lines + 2 * MAXA), LANES), jnp.float32),
            ],
        ),
        out_shape=[shape(w) for w in widths],
        compiler_params=pltpu.CompilerParams(vmem_limit_bytes=WHOLE_GRANT),
        cost_estimate=pl.CostEstimate(
            flops=count * lines * full * 4,
            transcendentals=0,
            bytes_accessed=count * lines * full * 8,
        ),
    )(az, rg, images, *earlier)


def pair_kernel(own, starts, reached, mask, *refs):
    count = len(starts)
    parts, following = refs[: 2 * count], refs[2 * count : 2 * count + len(reached)]
    right, images, products, sums = refs[-4:]
    block = 2 * own
    x, _, date0 = position(own)
    mine, other = x * own, (1 - x) * own
    for s, start in enumerate(starts):
        for where, ref in ((mine, parts[2 * s]), (other, parts[2 * s + 1])):
            for i in range(ref.shape[0]):
                images[where + start + i] = ref[i, :, 0, 0].astype(jnp.float32)
    for start, ref in zip(reached, following):
        for i in range(ref.shape[0]):
            images[block + start + i] = ref[i, :, 0, 0].astype(jnp.float32)
    sums[...] = jnp.zeros_like(sums)

    def multiply(d, carry):
        totals = [[None] * 2 for _ in range(MAXB)]
        for k in range(images.shape[2] // 8):
            at = pl.ds(8 * k, 8)
            a, b = images[d, 0, at, :], images[d, 1, at, :]
            for g in range(MAXB):
                c, e = images[d + g + 1, 0, at, :], images[d + g + 1, 1, at, :]
                terms = (a * c + b * e, b * c - a * e)
                for comp, term in enumerate(terms):
                    old = totals[g][comp]
                    totals[g][comp] = term if old is None else old + term
        for g in range(MAXB):
            for comp in range(2):
                at = ((d * MAXB + g) * 2 + comp) * 8
                products[pl.ds(pl.multiple_of(at, 8), 8), :] = totals[g][comp]
        return carry

    lax.fori_loop(0, block, multiply, 0)
    lane = lax.broadcasted_iota(jnp.int32, (8, LANES), 1)
    real = lane < LANES // 2
    place = lane >> 4

    def slot(d, g):
        at = (d * MAXB + g) * 16
        re = products[pl.ds(pl.multiple_of(at, 8), 8), :]
        im = products[pl.ds(pl.multiple_of(at + 8, 8), 8), :]
        value = jnp.where(real, re, im) + pltpu.roll(jnp.where(real, im, re), LANES // 2, 1)
        value = value + pltpu.roll(value, LANES - 8, 1)
        value = (value * (1.0 / (LA * LR))).astype(jnp.bfloat16).astype(jnp.float32)
        return value * mask[g, date0 + d].astype(jnp.float32)

    step = next(k for k in (16, 8, 4, 1) if block % k == 0)

    def gather(i, carry):
        totals = [None] * (step + MAXB)

        def add(at, value):
            totals[at] = value if totals[at] is None else totals[at] + value

        for j in range(step):
            for g in range(MAXB):
                value = slot(i * step + j, g)
                add(j, value)
                add(j + g + 1, -value)
        for j, value in enumerate(totals):
            at = pl.ds(pl.multiple_of(8 * (i * step + j), 8), 8)
            sums[at, :] = sums[at, :] + value
        return carry

    lax.fori_loop(0, block // step, gather, 0)
    for group in range(right.shape[2] // 8):
        rows = [sums[pl.ds(64 * group + u, 8, stride=8), :] for u in range(8)]
        rows = [jnp.where(lane & 8 == 0, v, pltpu.roll(v, LANES // 2 + 8, 1)) for v in rows]
        turned = []
        for s in range(8):
            joined = rows[s]
            for z in range(1, STRIPES):
                joined = jnp.where(place == z, rows[(s + z) % 8], joined)
            turned.append(pltpu.roll(joined, 16 * s, 1) if s else joined)
        for z in range(STRIPES):
            out = turned[0]
            for s in range(1, 8):
                out = jnp.where(place == (z + s) % 8, turned[s], out)
            right[right.shape[0] - 1, z, pl.ds(8 * group, 8), :] = out
    if right.shape[0] > 1:
        right[0] = refs[-5][0]


def pair_sums(mask, pieces, following, earlier, chunk, chunks, own, deep):
    groups, lines = pieces[0][1].shape[3:5]

    def window(array, parts):
        offset = chunk % (chunks // parts)
        return pl.BlockSpec(
            (array.shape[0], 2, 1, 1, lines, LANES), lambda i, *_: (0, 0, offset, i, 0, 0)
        )

    operands, specs = [], []
    for _, keep, received in pieces:
        got = received[chunk * len(received) // chunks]
        operands += [keep, got]
        specs += [window(keep, 1), window(got, len(received))]
    for _, received in following:
        got = received[chunk * len(received) // chunks]
        operands.append(got)
        specs.append(window(got, len(received)))
    joined = chunk == 1
    if earlier is not None:
        operands.append(earlier)
        specs.append(
            pl.BlockSpec((1, STRIPES, deep, LANES), lambda i, *_: (0, i, 0, 0))
            if joined
            else pl.BlockSpec(memory_space=pl.ANY)
        )
    work = 2 * own * MAXB * lines * LANES * groups
    return pl.pallas_call(
        partial(pair_kernel, own, [p[0] for p in pieces], [f[0] for f in following]),
        grid_spec=pltpu.PrefetchScalarGridSpec(
            num_scalar_prefetch=1,
            grid=(groups,),
            in_specs=specs,
            out_specs=pl.BlockSpec((1 + joined, STRIPES, deep, LANES), lambda i, *_: (0, i, 0, 0)),
            scratch_shapes=[
                pltpu.VMEM((2 * own + MAXB, 2, lines, LANES), jnp.float32),
                pltpu.VMEM((2 * own * MAXB * 16, LANES), jnp.float32),
                pltpu.VMEM((8 * deep, LANES), jnp.float32),
            ],
        ),
        out_shape=jax.ShapeDtypeStruct((1 + joined, groups * STRIPES, deep, LANES), jnp.float32),
        compiler_params=pltpu.CompilerParams(vmem_limit_bytes=GRANT),
        cost_estimate=pl.CostEstimate(flops=work * 8, transcendentals=0, bytes_accessed=work),
    )(mask, *operands)


def filter_kernel(count, *rest):
    weight, out, along = rest[2 * count :]
    own, partner = (
        [ref.at[i] for ref in refs for i in range(ref.shape[0])]
        for refs in (rest[:count], rest[count : 2 * count])
    )
    rows = len(own)
    tiles, deep = own[0].shape[:2]
    x = lax.axis_index("x")
    blank = jnp.zeros((rows, deep, LANES), jnp.float32)
    along[0] = blank
    along[2 * tiles + 1] = blank
    lane = lax.broadcasted_iota(jnp.int32, (deep, LANES), 1)
    place = lane & 7
    taps = [tap(k) for k in range(FILTER_R + 1)]
    most = jnp.zeros((deep, LANES), jnp.float32)
    for ref in own + partner:
        for i in range(tiles):
            most = jnp.maximum(most, jnp.abs(ref[i]))
    most = jnp.full((8, LANES), jnp.maximum(jnp.max(most), 1e-30))
    power = jnp.ceil(jnp.log2(most) + 0.001)
    scale = jnp.exp2(15.0 - power)[:1]
    code = power[:1]
    last_row = lax.broadcasted_iota(jnp.int32, (deep, LANES), 0) == deep - 1

    def coded(value):
        return jnp.where(last_row, code, value * scale)

    def turn(v, k):
        return pltpu.roll(v, k % LANES, 1)

    for refs, side in ((partner, 1 - x), (own, x)):
        for i in range(tiles):
            values = [ref[i] for ref in refs]
            for r in range(rows):
                acc = values[r]
                for k in range(1, FILTER_R + 1):
                    reach = 16 * k
                    last = values[r - 1] if r > 0 else jnp.zeros_like(acc)
                    later = values[r + 1] if r + 1 < rows else jnp.zeros_like(acc)
                    up = turn(jnp.where(lane >= reach, values[r], later), -reach)
                    down = turn(jnp.where(lane < LANES - reach, values[r], last), reach)
                    acc = acc + taps[k] * (up + down)
                along[2 * i + side + 1, r] = acc

    for i in range(tiles):
        at = 2 * i + x + 1
        for r in range(rows):
            v, left, right = along[at, r], along[at - 1, r], along[at + 1, r]
            acc = v
            for k in range(1, FILTER_R + 1):
                near = jnp.where(place < 8 - k, turn(v, -k), turn(right, 8 - k)) + jnp.where(
                    place >= k, turn(v, k), turn(left, k - 8)
                )
                acc = acc + taps[k] * near
            out[r, i, 0] = coded(own[r][i])
            out[r, i, 1] = coded(acc * weight[i, r : r + 1, :])


def filtered(own, partner, weight):
    count = len(own)
    rows = sum(v.shape[0] for v in own)
    tiles, deep = own[0].shape[1:3]
    return pl.pallas_call(
        partial(filter_kernel, count),
        in_specs=[vmem()] * (2 * count + 1),
        out_specs=vmem(),
        out_shape=jax.ShapeDtypeStruct((rows, tiles, 2, deep, LANES), jnp.float32),
        scratch_shapes=[pltpu.VMEM((2 * tiles + 2, rows, deep, LANES), jnp.float32)],
        name="smooth",
        compiler_params=pltpu.CompilerParams(vmem_limit_bytes=GRANT),
    )(*own, *partner, weight)


def edge_weights(positions, whole):
    total = jnp.zeros(positions.shape, jnp.float32)
    for k in range(-FILTER_R, FILTER_R + 1):
        at = positions + k
        total = total + jnp.where((at >= 0) & (at < whole), tap(k), 0.0)
    return total


def invert_kernel(normal, out):
    size = normal.shape[0]
    low, high = damping, damping + 4.0 * MAXB
    middle, spread = high + low, high - low
    peak = 2.0 * (middle / spread) ** 2 - 1.0
    row = lax.broadcasted_iota(jnp.int32, (size, size), 0)
    col = lax.broadcasted_iota(jnp.int32, (size, size), 1)
    unit = jnp.where(row == col, 1.0, 0.0).astype(jnp.float32)
    n = normal[...]
    guess = (8.0 * middle / spread**2 / peak) * unit - (8.0 / spread**2 / peak) * n
    whole = n.astype(jnp.bfloat16)

    def times_normal(value):
        total = None
        for _ in range(3):
            part = value.astype(jnp.bfloat16)
            value = value - part.astype(jnp.float32)
            term = jnp.dot(whole, part, preferred_element_type=jnp.float32)
            total = term if total is None else total + term
        return total

    error = 1.0 / peak
    while error > 1e-8:
        scale = 2.0 / (2.0 - error * error)
        residual = unit - times_normal(guess)
        precision = lax.Precision.HIGHEST if error < 0.1 else lax.Precision.DEFAULT
        change = jnp.dot(guess, residual, precision=precision, preferred_element_type=jnp.float32)
        guess = scale * (guess + change)
        error = error * error / (2.0 - error * error)
    out[...] = guess


def invert(normal):
    size = normal.shape[0]
    return pl.pallas_call(
        invert_kernel,
        in_specs=[vmem()],
        out_specs=vmem(),
        out_shape=jax.ShapeDtypeStruct((size, size), jnp.float32),
        name="invert",
        compiler_params=pltpu.CompilerParams(vmem_limit_bytes=GRANT),
        cost_estimate=pl.CostEstimate(
            flops=120 * size**3, transcendentals=0, bytes_accessed=8 * size * size
        ),
    )(normal)


def series_kernel(block, got, inverse, screen, motion, right):
    sources, _, deep = got.shape[:3]
    right[...] = jnp.zeros_like(right)
    used = lax.broadcasted_iota(jnp.int32, (deep, LANES), 0) < block + MAXB
    for s in range(sources):
        for part in range(2):
            lanes = pl.ds(part * LANES, LANES)
            at = pl.ds(s * block, deep)
            values = got[s, part]
            scale = jnp.exp2(values[deep - 1 :] - 15.0)
            right[at, lanes] = right[at, lanes] + jnp.where(used, values * scale, 0.0)
    result = jnp.dot(
        right[: inverse.shape[0], :].T,
        inverse[...],
        precision=lax.Precision.HIGHEST,
        preferred_element_type=jnp.float32,
    )
    for u in range(8):
        for comp in range(2):
            at = u * 16 + comp * 8
            first, second = result[at : at + 8], result[LANES + at : LANES + at + 8]
            screen[comp, u] = second
            motion[comp, u] = first - second


def invert_pixels(got, inverse, block):
    dates = inverse.shape[0]
    shape = jax.ShapeDtypeStruct((2, 8, 8, dates), jnp.float32)
    return pl.pallas_call(
        partial(series_kernel, block),
        in_specs=[vmem(), vmem()],
        out_specs=[vmem(), vmem()],
        out_shape=[shape, shape],
        scratch_shapes=[pltpu.VMEM((dates + got.shape[2] - block, 2 * LANES), jnp.float32)],
        name="series",
        compiler_params=pltpu.CompilerParams(vmem_limit_bytes=GRANT),
    )(got, inverse)


def local(images, az, rg, pair_list):
    own, _, lines, full = images.shape
    dates = az.shape[0]
    groups, along, _ = (lax.axis_size(name) for name in ("pairs", "z", "x"))
    blocks = groups * along
    block = 2 * own
    deep = -(-(block + MAXB + 1) // 8) * 8
    rows = groups
    if full != 2 * along * LANES or along % STRIPES or lines != rows * 8 * LA:
        raise ValueError("unsupported shape")
    x = lax.axis_index("x")

    date_ids = jnp.arange(dates, dtype=jnp.int32)
    is_reference = date_ids[:, None] == pair_list[None, :, 0]
    is_secondary = date_ids[:, None] == pair_list[None, :, 1]
    design = (is_reference.astype(jnp.float32) - is_secondary.astype(jnp.float32)).astype(
        jnp.bfloat16
    )
    normal = jnp.dot(design, design.T, preferred_element_type=jnp.float32)
    normal = normal + damping * jnp.eye(dates, dtype=jnp.float32)
    gaps = pair_list[:, 1] - pair_list[:, 0]
    is_gap = jnp.arange(1, MAXB + 1, dtype=jnp.int32)[:, None] == gaps[None, :]
    mask = jnp.dot(
        is_gap.astype(jnp.bfloat16),
        is_reference.astype(jnp.bfloat16).T,
        preferred_element_type=jnp.float32,
    )
    mask = mask.astype(jnp.int32)
    inverse = invert(normal)

    swap = [(0, 1), (1, 0)]
    cuts, parts = [0, own], [1]
    if own > MAXB:
        cuts, parts = [0, 1, 2, MAXB, own], [1, 1, min(rows, 2), rows]
    pieces, following = [], []
    left, turn = x == 0, 0

    def send_back(start, keep, received, left):
        hops = []
        for c, other in enumerate(received):
            part = other.shape[2]
            mine = lax.slice_in_dim(keep, c * part, (c + 1) * part, axis=2)
            lower, upper = mine, other
            if own < MAXB:
                lower = jnp.concatenate([mine, other], 0)[:MAXB]
                upper = jnp.concatenate([other, mine], 0)[:MAXB]
            hops.append(jnp.where(left, lower, upper))
            if own > MAXB:
                left, hops[-1] = lax.optimization_barrier((left, hops[-1]))
        if own < MAXB:
            for hop in range(1, -(-MAXB // block) + 1):
                route = [(i + hop, i) for i in range(blocks - hop)]
                count = min(block, MAXB - (hop - 1) * block)
                going = [lax.ppermute(v[:count], ("pairs", "z"), route) for v in hops]
                following.append(((hop - 1) * block, going))
        else:
            route = [(i + 1, i) for i in range(blocks - 1)]
            going = []
            for v in hops:
                going.append(lax.ppermute(v, ("pairs", "z"), route))
            following.append((start, going))
        return left

    for start, end, count in zip(cuts, cuts[1:], parts):
        after = [p[1] for p in pieces[-1:]]
        keep, *sends = resample(images, az, rg, start, end - start, count, after)
        received = []
        for v in sends:
            received.append(lax.ppermute(v, "x", swap))
            turn += 1
        pieces.append((start, keep, received))
    for start, keep, received in pieces:
        if start < MAXB:
            left = send_back(start, keep, received, left)

    sums = []
    for c in range(rows):
        earlier = sums[-1] if sums else None
        sums.append(pair_sums(mask, pieces, following, earlier, c, rows, own, deep))
    sums = sums[1:]
    partner = [lax.ppermute(s, "x", swap) for s in sums]

    lane = jnp.arange(LANES, dtype=jnp.int32)
    row_at = jnp.arange(rows, dtype=jnp.int32)[:, None] * 8 + (lane // 16)[None, :]
    stripe = 2 * jnp.arange(along, dtype=jnp.int32) + x
    col_at = stripe[:, None] * 8 + (lane & 7)[None, :]
    row_weight = edge_weights(row_at, lines // LA)
    col_weight = edge_weights(col_at, full // LR)
    weight = 1.0 / (row_weight[None, :, :] * col_weight[:, None, :])

    outgoing = filtered(sums, partner, weight)
    outgoing = outgoing.reshape((rows * along,) + outgoing.shape[2:]).astype(jnp.float16)
    got = lax.all_to_all(outgoing, ("pairs", "z"), split_axis=0, concat_axis=0, tiled=True)
    got = got.astype(jnp.float32)
    screen, motion = invert_pixels(got, inverse, block)
    return tuple(jnp.transpose(v, (3, 0, 1, 2)) for v in (screen, motion))


def solution(mesh):
    shape = (mesh.shape["pairs"], mesh.shape["stripe"] // 2, 2)
    if isinstance(mesh, Mesh):
        finer = Mesh(mesh.devices.reshape(shape), ("pairs", "z", "x"))
    else:
        finer = jax.sharding.AbstractMesh(shape, ("pairs", "z", "x"))
    placed = P(None, None, "pairs", ("z", "x"))

    return jax.shard_map(
        local,
        mesh=finer,
        in_specs=(P(("pairs", "z", "x"), None, None, None), P(), P(), P()),
        out_specs=(placed, placed),
        check_vma=False,
    )
```

```python
from functools import partial

import jax
import jax.numpy as jnp
from jax import lax
from jax.experimental import pallas as pl
from jax.experimental.pallas import tpu as pltpu
from jax.sharding import Mesh, PartitionSpec as P


MAXB = 5
LA = 4
LR = 16
MAXA = 8
FILTER_R = 3
LANES = 128
STRIPES = 4
GRANT = 16 << 20
WHOLE_GRANT = 60 << 20
damping = 0.5


def vmem():
    return pl.BlockSpec(memory_space=pltpu.VMEM)


def tap(k):
    sigma = FILTER_R / 2.0
    return jnp.exp(-jnp.float32(k * k) / jnp.float32(2.0 * sigma * sigma))


def position(own):
    x = lax.axis_index("x")
    place = lax.axis_index("pairs") * lax.axis_size("z") + lax.axis_index("z")
    return x, (2 * place + x) * own, 2 * place * own


def resample_kernel(own_dates, first, parts, az, rg, img, *rest):
    rest = rest[-4 - parts :]
    keep, sends = rest[0], rest[1 : 1 + parts]
    tiles_of, spread, shifted = rest[1 + parts :]
    lines, full = img.shape[2], img.shape[3]
    tiles = full // LANES
    groups = tiles // (2 * STRIPES)
    blocks = lines // (8 * LA)
    high = lines + 2 * MAXA
    span = STRIPES * LANES
    x, base, _ = position(own_dates)
    date = base + first + pl.program_id(0)
    shift = rg[date]
    step = az[date]
    behind = shift < 0
    origin = jnp.where(behind, -1, 0)
    amount = shift - origin * LANES
    turn = lax.rem(LANES - amount, LANES)
    lane = lax.broadcasted_iota(jnp.int32, (lines, LANES), 1)
    own = lane + amount < LANES

    @pl.when(pl.program_id(0) == 0)
    def _():
        blank = jnp.zeros((MAXA, LANES), jnp.float32)
        for t in range(shifted.shape[0] // high):
            shifted[pl.ds(t * high, MAXA), :] = blank
            shifted[pl.ds(t * high + MAXA + lines, MAXA), :] = blank
        source = lax.broadcasted_iota(jnp.int32, (span, span), 0)
        target = lax.broadcasted_iota(jnp.int32, (1, span), 1)
        column, few = target & 7, ((target >> 6) & 1) * 2 + ((target >> 3) & 1)
        stripe, many = (target >> 4) & 3, target >> 7
        wanted = stripe * LANES + column * LR + many * 4 + few
        spread[...] = jnp.where(source == wanted, 1.0, 0.0).astype(jnp.bfloat16)

    for c in range(2):

        def turned(t):
            place = jnp.clip(t + origin, 0, tiles - 1)
            tile = img[0, c, :, pl.ds(pl.multiple_of(place * LANES, LANES), LANES)]
            out = pltpu.roll(tile.astype(jnp.float32), turn, 1)
            if t == 0:
                out = jnp.where(behind, 0.0, out)
            if t == tiles:
                out = jnp.where(behind, out, 0.0)
            return out

        here = turned(0)
        for t in range(tiles):
            after = turned(t + 1)
            group, stripe, parity = t // 2 // STRIPES, t // 2 % STRIPES, t % 2
            tiles_of[
                group, pl.ds((c * 2 + parity) * lines, lines), pl.ds(stripe * LANES, LANES)
            ] = jnp.where(own, here, after).astype(jnp.bfloat16)
            here = after

    def slab(c, parity, group, many):
        return (((c * 2 + parity) * groups + group) * 4 + many) * high + MAXA

    for group in range(groups):
        for half in range(2):
            result = jnp.dot(
                tiles_of[group],
                spread[:, half * span // 2 : (half + 1) * span // 2],
                preferred_element_type=jnp.float32,
            )
            for c in range(2):
                for parity in range(2):
                    for k in range(2):
                        at = (c * 2 + parity) * lines
                        shifted[pl.ds(slab(c, parity, group, 2 * half + k), lines), :] = result[
                            at : at + lines, k * LANES : (k + 1) * LANES
                        ]

    def put(out, place, block, c, group, parity):
        for look in range(LA):
            for pair in range(2):
                both = [
                    shifted[
                        pl.ds(
                            slab(c, parity, group, 2 * pair + k) + step + 8 * LA * block + look,
                            8,
                            stride=LA,
                        ),
                        :,
                    ]
                    for k in range(2)
                ]
                out[0, c, place, group, pl.ds(32 * look + 16 * pair, 16), :] = jnp.concatenate(
                    both, 0
                ).astype(jnp.bfloat16)

    width = blocks // parts
    for c in range(2):
        for block in range(blocks):
            for group in range(groups):
                put(sends[block // width], block % width, block, c, group, 1 - x)
                put(keep, block, block, c, group, x)


def resample(images, az, rg, first, count, parts, earlier):
    lines, full = images.shape[2], images.shape[3]
    tiles = full // LANES
    groups = tiles // (2 * STRIPES)
    blocks = lines // (8 * LA)
    rows = 8 * LA * 4

    def block(width):
        return pl.BlockSpec(
            (1, 2, width, groups, rows, LANES), lambda i, *_: (i, 0, 0, 0, 0, 0)
        )

    def shape(width):
        return jax.ShapeDtypeStruct((count, 2, width, groups, rows, LANES), jnp.bfloat16)

    widths = [blocks] + [blocks // parts] * parts
    return pl.pallas_call(
        partial(resample_kernel, images.shape[0], first, parts),
        grid_spec=pltpu.PrefetchScalarGridSpec(
            num_scalar_prefetch=2,
            grid=(count,),
            in_specs=[pl.BlockSpec((1, 2, lines, full), lambda i, *_: (i + first, 0, 0, 0))]
            + [pl.BlockSpec(memory_space=pl.ANY)] * len(earlier),
            out_specs=[block(w) for w in widths],
            scratch_shapes=[
                pltpu.VMEM((groups, 4 * lines, STRIPES * LANES), jnp.bfloat16),
                pltpu.VMEM((STRIPES * LANES, STRIPES * LANES), jnp.bfloat16),
                pltpu.VMEM((16 * groups * (lines + 2 * MAXA), LANES), jnp.float32),
            ],
        ),
        out_shape=[shape(w) for w in widths],
        compiler_params=pltpu.CompilerParams(vmem_limit_bytes=WHOLE_GRANT),
        cost_estimate=pl.CostEstimate(
            flops=count * lines * full * 4,
            transcendentals=0,
            bytes_accessed=count * lines * full * 8,
        ),
    )(az, rg, images, *earlier)


def pair_kernel(own, starts, reached, mask, *refs):
    count = len(starts)
    parts, following = refs[: 2 * count], refs[2 * count : 2 * count + len(reached)]
    right, images, products, sums = refs[-4:]
    block = 2 * own
    x, _, date0 = position(own)
    mine, other = x * own, (1 - x) * own
    for s, start in enumerate(starts):
        for where, ref in ((mine, parts[2 * s]), (other, parts[2 * s + 1])):
            for i in range(ref.shape[0]):
                images[where + start + i] = ref[i, :, 0, 0].astype(jnp.float32)
    for start, ref in zip(reached, following):
        for i in range(ref.shape[0]):
            images[block + start + i] = ref[i, :, 0, 0].astype(jnp.float32)
    sums[...] = jnp.zeros_like(sums)

    def multiply(d, carry):
        totals = [[None] * 2 for _ in range(MAXB)]
        for k in range(images.shape[2] // 8):
            at = pl.ds(8 * k, 8)
            a, b = images[d, 0, at, :], images[d, 1, at, :]
            for g in range(MAXB):
                c, e = images[d + g + 1, 0, at, :], images[d + g + 1, 1, at, :]
                terms = (a * c + b * e, b * c - a * e)
                for comp, term in enumerate(terms):
                    old = totals[g][comp]
                    totals[g][comp] = term if old is None else old + term
        for g in range(MAXB):
            for comp in range(2):
                at = ((d * MAXB + g) * 2 + comp) * 8
                products[pl.ds(pl.multiple_of(at, 8), 8), :] = totals[g][comp]
        return carry

    lax.fori_loop(0, block, multiply, 0)
    lane = lax.broadcasted_iota(jnp.int32, (8, LANES), 1)
    real = lane < LANES // 2
    place = lane >> 4

    def slot(d, g):
        at = (d * MAXB + g) * 16
        re = products[pl.ds(pl.multiple_of(at, 8), 8), :]
        im = products[pl.ds(pl.multiple_of(at + 8, 8), 8), :]
        value = jnp.where(real, re, im) + pltpu.roll(jnp.where(real, im, re), LANES // 2, 1)
        value = value + pltpu.roll(value, LANES - 8, 1)
        value = (value * (1.0 / (LA * LR))).astype(jnp.bfloat16).astype(jnp.float32)
        return value * mask[g, date0 + d].astype(jnp.float32)

    step = next(k for k in (16, 8, 4, 1) if block % k == 0)

    def gather(i, carry):
        totals = [None] * (step + MAXB)

        def add(at, value):
            totals[at] = value if totals[at] is None else totals[at] + value

        for j in range(step):
            for g in range(MAXB):
                value = slot(i * step + j, g)
                add(j, value)
                add(j + g + 1, -value)
        for j, value in enumerate(totals):
            at = pl.ds(pl.multiple_of(8 * (i * step + j), 8), 8)
            sums[at, :] = sums[at, :] + value
        return carry

    lax.fori_loop(0, block // step, gather, 0)
    for group in range(right.shape[2] // 8):
        rows = [sums[pl.ds(64 * group + u, 8, stride=8), :] for u in range(8)]
        rows = [jnp.where(lane & 8 == 0, v, pltpu.roll(v, LANES // 2 + 8, 1)) for v in rows]
        turned = []
        for s in range(8):
            joined = rows[s]
            for z in range(1, STRIPES):
                joined = jnp.where(place == z, rows[(s + z) % 8], joined)
            turned.append(pltpu.roll(joined, 16 * s, 1) if s else joined)
        for z in range(STRIPES):
            out = turned[0]
            for s in range(1, 8):
                out = jnp.where(place == (z + s) % 8, turned[s], out)
            right[right.shape[0] - 1, z, pl.ds(8 * group, 8), :] = out
    if right.shape[0] > 1:
        right[0] = refs[-5][0]


def pair_sums(mask, pieces, following, earlier, chunk, chunks, own, deep):
    groups, lines = pieces[0][1].shape[3:5]

    def window(array, parts):
        offset = chunk % (chunks // parts)
        return pl.BlockSpec(
            (array.shape[0], 2, 1, 1, lines, LANES), lambda i, *_: (0, 0, offset, i, 0, 0)
        )

    operands, specs = [], []
    for _, keep, received in pieces:
        got = received[chunk * len(received) // chunks]
        operands += [keep, got]
        specs += [window(keep, 1), window(got, len(received))]
    for _, received in following:
        got = received[chunk * len(received) // chunks]
        operands.append(got)
        specs.append(window(got, len(received)))
    joined = chunk % 2 == 1
    if earlier is not None:
        operands.append(earlier)
        specs.append(
            pl.BlockSpec((1, STRIPES, deep, LANES), lambda i, *_: (0, i, 0, 0))
            if joined
            else pl.BlockSpec(memory_space=pl.ANY)
        )
    work = 2 * own * MAXB * lines * LANES * groups
    return pl.pallas_call(
        partial(pair_kernel, own, [p[0] for p in pieces], [f[0] for f in following]),
        grid_spec=pltpu.PrefetchScalarGridSpec(
            num_scalar_prefetch=1,
            grid=(groups,),
            in_specs=specs,
            out_specs=pl.BlockSpec((1 + joined, STRIPES, deep, LANES), lambda i, *_: (0, i, 0, 0)),
            scratch_shapes=[
                pltpu.VMEM((2 * own + MAXB, 2, lines, LANES), jnp.float32),
                pltpu.VMEM((2 * own * MAXB * 16, LANES), jnp.float32),
                pltpu.VMEM((8 * deep, LANES), jnp.float32),
            ],
        ),
        out_shape=jax.ShapeDtypeStruct((1 + joined, groups * STRIPES, deep, LANES), jnp.float32),
        compiler_params=pltpu.CompilerParams(vmem_limit_bytes=GRANT),
        cost_estimate=pl.CostEstimate(flops=work * 8, transcendentals=0, bytes_accessed=work),
    )(mask, *operands)


def filter_kernel(count, *rest):
    weight, out, along = rest[2 * count :]
    own, partner = (
        [ref.at[i] for ref in refs for i in range(ref.shape[0])]
        for refs in (rest[:count], rest[count : 2 * count])
    )
    rows = len(own)
    tiles, deep = own[0].shape[:2]
    x = lax.axis_index("x")
    blank = jnp.zeros((rows, deep, LANES), jnp.float32)
    along[0] = blank
    along[2 * tiles + 1] = blank
    lane = lax.broadcasted_iota(jnp.int32, (deep, LANES), 1)
    place = lane & 7
    taps = [tap(k) for k in range(FILTER_R + 1)]
    most = jnp.zeros((deep, LANES), jnp.float32)
    for ref in own + partner:
        for i in range(tiles):
            most = jnp.maximum(most, jnp.abs(ref[i]))
    most = jnp.full((8, LANES), jnp.maximum(jnp.max(most), 1e-30))
    power = jnp.ceil(jnp.log2(most) + 0.001)
    scale = jnp.exp2(15.0 - power)[:1]
    code = power[:1]
    last_row = lax.broadcasted_iota(jnp.int32, (deep, LANES), 0) == deep - 1

    def coded(value):
        return jnp.where(last_row, code, value * scale)

    def turn(v, k):
        return pltpu.roll(v, k % LANES, 1)

    for refs, side in ((partner, 1 - x), (own, x)):
        for i in range(tiles):
            values = [ref[i] for ref in refs]
            for r in range(rows):
                acc = values[r]
                for k in range(1, FILTER_R + 1):
                    reach = 16 * k
                    last = values[r - 1] if r > 0 else jnp.zeros_like(acc)
                    later = values[r + 1] if r + 1 < rows else jnp.zeros_like(acc)
                    up = turn(jnp.where(lane >= reach, values[r], later), -reach)
                    down = turn(jnp.where(lane < LANES - reach, values[r], last), reach)
                    acc = acc + taps[k] * (up + down)
                along[2 * i + side + 1, r] = acc

    for i in range(tiles):
        at = 2 * i + x + 1
        for r in range(rows):
            v, left, right = along[at, r], along[at - 1, r], along[at + 1, r]
            acc = v
            for k in range(1, FILTER_R + 1):
                near = jnp.where(place < 8 - k, turn(v, -k), turn(right, 8 - k)) + jnp.where(
                    place >= k, turn(v, k), turn(left, k - 8)
                )
                acc = acc + taps[k] * near
            out[r, i, 0] = coded(own[r][i])
            out[r, i, 1] = coded(acc * weight[i, r : r + 1, :])


def filtered(own, partner, weight):
    count = len(own)
    rows = sum(v.shape[0] for v in own)
    tiles, deep = own[0].shape[1:3]
    return pl.pallas_call(
        partial(filter_kernel, count),
        in_specs=[vmem()] * (2 * count + 1),
        out_specs=vmem(),
        out_shape=jax.ShapeDtypeStruct((rows, tiles, 2, deep, LANES), jnp.float32),
        scratch_shapes=[pltpu.VMEM((2 * tiles + 2, rows, deep, LANES), jnp.float32)],
        name="smooth",
        compiler_params=pltpu.CompilerParams(vmem_limit_bytes=GRANT),
    )(*own, *partner, weight)


def edge_weights(positions, whole):
    total = jnp.zeros(positions.shape, jnp.float32)
    for k in range(-FILTER_R, FILTER_R + 1):
        at = positions + k
        total = total + jnp.where((at >= 0) & (at < whole), tap(k), 0.0)
    return total


def invert_kernel(normal, out):
    size = normal.shape[0]
    low, high = damping, damping + 4.0 * MAXB
    middle, spread = high + low, high - low
    peak = 2.0 * (middle / spread) ** 2 - 1.0
    row = lax.broadcasted_iota(jnp.int32, (size, size), 0)
    col = lax.broadcasted_iota(jnp.int32, (size, size), 1)
    unit = jnp.where(row == col, 1.0, 0.0).astype(jnp.float32)
    n = normal[...]
    guess = (8.0 * middle / spread**2 / peak) * unit - (8.0 / spread**2 / peak) * n
    whole = n.astype(jnp.bfloat16)

    def times_normal(value):
        total = None
        for _ in range(3):
            part = value.astype(jnp.bfloat16)
            value = value - part.astype(jnp.float32)
            term = jnp.dot(whole, part, preferred_element_type=jnp.float32)
            total = term if total is None else total + term
        return total

    error = 1.0 / peak
    while error > 1e-8:
        scale = 2.0 / (2.0 - error * error)
        residual = unit - times_normal(guess)
        precision = lax.Precision.HIGHEST if error < 1e-3 else lax.Precision.DEFAULT
        change = jnp.dot(guess, residual, precision=precision, preferred_element_type=jnp.float32)
        guess = scale * (guess + change)
        error = error * error / (2.0 - error * error)
    out[...] = guess


def invert(normal):
    size = normal.shape[0]
    return pl.pallas_call(
        invert_kernel,
        in_specs=[vmem()],
        out_specs=vmem(),
        out_shape=jax.ShapeDtypeStruct((size, size), jnp.float32),
        name="invert",
        compiler_params=pltpu.CompilerParams(vmem_limit_bytes=GRANT),
        cost_estimate=pl.CostEstimate(
            flops=120 * size**3, transcendentals=0, bytes_accessed=8 * size * size
        ),
    )(normal)


def series_kernel(block, got, inverse, screen, motion, right):
    sources, _, deep = got.shape[:3]
    right[...] = jnp.zeros_like(right)
    used = lax.broadcasted_iota(jnp.int32, (deep, LANES), 0) < block + MAXB
    for s in range(sources):
        for part in range(2):
            lanes = pl.ds(part * LANES, LANES)
            at = pl.ds(s * block, deep)
            values = got[s, part]
            scale = jnp.exp2(values[deep - 1 :] - 15.0)
            right[at, lanes] = right[at, lanes] + jnp.where(used, values * scale, 0.0)
    result = jnp.dot(
        right[: inverse.shape[0], :].T,
        inverse[...],
        precision=lax.Precision.HIGHEST,
        preferred_element_type=jnp.float32,
    )
    for u in range(8):
        for comp in range(2):
            at = u * 16 + comp * 8
            first, second = result[at : at + 8], result[LANES + at : LANES + at + 8]
            screen[comp, u] = second
            motion[comp, u] = first - second


def invert_pixels(got, inverse, block):
    dates = inverse.shape[0]
    shape = jax.ShapeDtypeStruct((2, 8, 8, dates), jnp.float32)
    return pl.pallas_call(
        partial(series_kernel, block),
        in_specs=[vmem(), vmem()],
        out_specs=[vmem(), vmem()],
        out_shape=[shape, shape],
        scratch_shapes=[pltpu.VMEM((dates + got.shape[2] - block, 2 * LANES), jnp.float32)],
        name="series",
        compiler_params=pltpu.CompilerParams(vmem_limit_bytes=GRANT),
    )(got, inverse)


def local(images, az, rg, pair_list):
    own, _, lines, full = images.shape
    dates = az.shape[0]
    groups, along, _ = (lax.axis_size(name) for name in ("pairs", "z", "x"))
    blocks = groups * along
    block = 2 * own
    deep = -(-(block + MAXB + 1) // 8) * 8
    rows = groups
    if full != 2 * along * LANES or along % STRIPES or lines != rows * 8 * LA:
        raise ValueError("unsupported shape")
    x = lax.axis_index("x")

    date_ids = jnp.arange(dates, dtype=jnp.int32)
    is_reference = date_ids[:, None] == pair_list[None, :, 0]
    is_secondary = date_ids[:, None] == pair_list[None, :, 1]
    design = (is_reference.astype(jnp.float32) - is_secondary.astype(jnp.float32)).astype(
        jnp.bfloat16
    )
    normal = jnp.dot(design, design.T, preferred_element_type=jnp.float32)
    normal = normal + damping * jnp.eye(dates, dtype=jnp.float32)
    gaps = pair_list[:, 1] - pair_list[:, 0]
    is_gap = jnp.arange(1, MAXB + 1, dtype=jnp.int32)[:, None] == gaps[None, :]
    mask = jnp.dot(
        is_gap.astype(jnp.bfloat16),
        is_reference.astype(jnp.bfloat16).T,
        preferred_element_type=jnp.float32,
    )
    mask = mask.astype(jnp.int32)
    inverse = invert(normal)

    swap = [(0, 1), (1, 0)]
    cuts, parts = [0, own], [1]
    if own > MAXB:
        cuts, parts = [0, 1, 2, MAXB, own], [1, 1, min(rows, 2), rows]
    pieces, following = [], []
    left, turn = x == 0, 0

    def send_back(start, keep, received, left):
        hops = []
        for c, other in enumerate(received):
            part = other.shape[2]
            mine = lax.slice_in_dim(keep, c * part, (c + 1) * part, axis=2)
            lower, upper = mine, other
            if own < MAXB:
                lower = jnp.concatenate([mine, other], 0)[:MAXB]
                upper = jnp.concatenate([other, mine], 0)[:MAXB]
            hops.append(jnp.where(left, lower, upper))
            if own > MAXB:
                left, hops[-1] = lax.optimization_barrier((left, hops[-1]))
        if own < MAXB:
            for hop in range(1, -(-MAXB // block) + 1):
                route = [(i + hop, i) for i in range(blocks - hop)]
                count = min(block, MAXB - (hop - 1) * block)
                going = [lax.ppermute(v[:count], ("pairs", "z"), route) for v in hops]
                following.append(((hop - 1) * block, going))
        else:
            route = [(i + 1, i) for i in range(blocks - 1)]
            going = []
            for v in hops:
                going.append(lax.ppermute(v, ("pairs", "z"), route))
            following.append((start, going))
        return left

    for start, end, count in zip(cuts, cuts[1:], parts):
        after = [p[1] for p in pieces[-1:]]
        keep, *sends = resample(images, az, rg, start, end - start, count, after)
        received = []
        for v in sends:
            received.append(lax.ppermute(v, "x", swap))
            turn += 1
        pieces.append((start, keep, received))
    for start, keep, received in pieces:
        if start < MAXB:
            left = send_back(start, keep, received, left)

    sums = []
    for c in range(rows):
        earlier = sums[-1] if sums else None
        sums.append(pair_sums(mask, pieces, following, earlier, c, rows, own, deep))
    sums = sums[1::2]
    partner = [lax.ppermute(s, "x", swap) for s in sums]

    lane = jnp.arange(LANES, dtype=jnp.int32)
    row_at = jnp.arange(rows, dtype=jnp.int32)[:, None] * 8 + (lane // 16)[None, :]
    stripe = 2 * jnp.arange(along, dtype=jnp.int32) + x
    col_at = stripe[:, None] * 8 + (lane & 7)[None, :]
    row_weight = edge_weights(row_at, lines // LA)
    col_weight = edge_weights(col_at, full // LR)
    weight = 1.0 / (row_weight[None, :, :] * col_weight[:, None, :])

    outgoing = filtered(sums, partner, weight)
    outgoing = outgoing.reshape((rows * along,) + outgoing.shape[2:]).astype(jnp.float16)
    got = lax.all_to_all(outgoing, ("pairs", "z"), split_axis=0, concat_axis=0, tiled=True)
    got = got.astype(jnp.float32)
    screen, motion = invert_pixels(got, inverse, block)
    return tuple(jnp.transpose(v, (3, 0, 1, 2)) for v in (screen, motion))


def solution(mesh):
    shape = (mesh.shape["pairs"], mesh.shape["stripe"] // 2, 2)
    if isinstance(mesh, Mesh):
        finer = Mesh(mesh.devices.reshape(shape), ("pairs", "z", "x"))
    else:
        finer = jax.sharding.AbstractMesh(shape, ("pairs", "z", "x"))
    placed = P(None, None, "pairs", ("z", "x"))

    return jax.shard_map(
        local,
        mesh=finer,
        in_specs=(P(("pairs", "z", "x"), None, None, None), P(), P(), P()),
        out_specs=(placed, placed),
        check_vma=False,
    )
```
